32 devices in a mesh: dp: 16 (over z, y, core), shard: 2 (over x).
Axes of the slice: x: 2, y: 2, z: 4, core: 2. Of those that a mesh axis runs over, the one named last changes fastest.
Arguments:
- tokens: bfloat16 [32768, 512], P(('dp', 'shard')), may hold values from -6 to 6
- cotangent: bfloat16 [32768, 512], P(('dp', 'shard')), may hold values from -6 to 6
- segments: int32 [32, 1024], P(('dp', 'shard')), may hold values from 0 to 3, never falling along the last dimension, each value on 1 to 800 neighbouring positions
- random_blocks: int32 [32, 16, 8, 3], P(('dp', 'shard')), may hold values from 0 to 15
- step_count: int32 [1], replicated, may hold values from 1 to 7
- adam_rates: float32 [2], replicated, may hold values from 0.05 to 0.3
- attn_master: float32 [512, 2048], P('shard'), as said below
- attn_mean: float32 [512, 2048], P('shard'), may hold values from -6 to 6
- attn_square: float32 [512, 2048], P('shard'), may hold values from 0.1 to 10
- ffn_master: float32 [2, 512, 2048], P(None, 'shard'), may hold values from -0.25 to 0.25
- ffn_mean: float32 [2, 512, 2048], P(None, 'shard'), may hold values from -6 to 6
- ffn_square: float32 [2, 512, 2048], P(None, 'shard'), may hold values from 0.1 to 10
- small_master: float32 [12, 512], P(None, 'shard'), as said below
- small_mean: float32 [12, 512], P(None, 'shard'), may hold values from -6 to 6
- small_square: float32 [12, 512], P(None, 'shard'), may hold values from 0.1 to 10
Outputs:
- layer_out: bfloat16 [32768, 512], P(('dp', 'shard'))
- input_grad: bfloat16 [32768, 512], P(('dp', 'shard'))
- attn_updated: float32 [512, 2048], P('shard')
- attn_means: float32 [512, 2048], P('shard')
- attn_squares: float32 [512, 2048], P('shard')
- attn_copy: bfloat16 [512, 2048], P('shard')
- ffn_updated: float32 [2, 512, 2048], P(None, 'shard')
- ffn_means: float32 [2, 512, 2048], P(None, 'shard')
- ffn_squares: float32 [2, 512, 2048], P(None, 'shard')
- ffn_copy: bfloat16 [2, 512, 2048], P(None, 'shard')
- small_updated: float32 [12, 512], P(None, 'shard')
- small_means: float32 [12, 512], P(None, 'shard')
- small_squares: float32 [12, 512], P(None, 'shard')
- small_copy: bfloat16 [12, 512], P(None, 'shard')
The draws below stay inside these ranges and needn't reach their ends.
Inputs may be any that keep to these rules, and one draw needn't show every extreme that they name: `attn_master`: query, key and value projection columns have deviation 512 ** -0.5, the output projection's 8 * 512 ** -0.5. `small_master`: gains near one, biases of deviation 0.3. `segments`: each sequence holds whole documents numbered from 0 in order.
All inputs are finite; a program needn't handle non-finite values.
Results may differ from the reference program's by a relative error of at most 0.017.
The reference program's roundings to bfloat16 on the way count: a program that leaves them out, or rounds other values in their place, can miss the bound.
Values may be sent and summed in bfloat16 or wider, within the bound.
No kernel may reach another device: no remote copies, remote signals or barrier semaphores. Data moves between devices by JAX's collectives and lax.ppermute only.
A program may use at most 128 MiB of HBM per device.

```python
import math
import jax
import jax.numpy as jnp
import numpy as np
from jax import lax

D = 512
HD = 64
HEADS = 8
FF = 2048
BLOCK = 64
RAND = 3
SEQ = 1024
NSEQ = 32
TOKENS = 32768
NB = 16
HA = 512


def draw_attn_master(key, part):
    sample = jnp.clip(jax.random.normal(key, (D, 4 * HEADS * HD), jnp.float32), -4.0, 4.0)
    column = jnp.arange(4 * HEADS * HD)
    factor = jnp.where(column < 3 * HEADS * HD, D ** (-0.5), 8.0 * (HEADS * HD) ** (-0.5))
    return sample * factor


def draw_small_master(key, part):
    sample = jnp.clip(jax.random.normal(key, (12, D), jnp.float32), -4.0, 4.0)
    rownum = jnp.arange(12)[:, None]
    is_gain = (rownum == 0) | (rownum == 2)
    return jnp.where(is_gain, 1.0 + 0.15 * sample, 0.3 * sample)


def plant(array, stream_key, low, largest):
    dims = array.shape
    index_at = [jax.random.randint(jax.random.fold_in(stream_key, axis), (), 0, dims[axis]) for axis in range(len(dims))]
    array = array.at[tuple(index_at)].set(low)
    longest = dims.index(max(dims))
    index_at[longest] = (index_at[longest] + 1) % dims[longest]
    return array.at[tuple(index_at)].set(largest)


def block_levels(key, dims, shards, least, largest):
    level = 1.0
    for position, shards_of in shards:
        draws = jax.random.uniform(jax.random.fold_in(jax.random.fold_in(key, 6), position), (shards_of,), jnp.float32, least / len(shards), largest / len(shards))
        level = level * jnp.repeat(jnp.exp(draws), dims[position] // shards_of).reshape((-1,) + (1,) * (len(dims) - 1 - position))
    return level


def length_profile(amount, total, reach, lean):
    loads = [(1 << 20) // math.isqrt(rank ** lean) + 1 for rank in range(2, amount + 1)]
    surplus, holding = total - reach - (amount - 1), [1] * (amount - 1)
    while surplus > 0:
        candidates = [i for i in range(amount - 1) if holding[i] < reach]
        whole, budget = sum([loads[i] for i in candidates]), surplus
        for i in candidates:
            extra = min(reach - holding[i], max(1, budget * loads[i] // whole), surplus)
            holding[i] = holding[i] + extra
            surplus = surplus - extra
    return np.array([reach] + holding)


def uneven_parts(key, count, total, limit, lean):
    if count == 2:
        one = jax.random.randint(key, (), max(1, total - limit), min(limit, total - 1) + 1)
        return jnp.stack([one, total - one])
    lengths = jnp.asarray(length_profile(count, total, limit, lean), jnp.int32)
    twos = (count - 1) // 2
    source_of, receiver = lengths[1:1 + 2 * twos:2], lengths[2:2 + 2 * twos:2]
    slack = jnp.minimum(source_of - 1, limit - receiver)
    moved = jax.random.randint(jax.random.fold_in(key, 1), (twos,), 0, 1 << 20) % (slack + 1)
    lengths = lengths.at[1:1 + 2 * twos:2].set(source_of - moved).at[2:2 + 2 * twos:2].set(receiver + moved)
    return lengths[jax.random.permutation(jax.random.fold_in(key, 2), count)]


def gaussian(stream_key, extent, deviation, reach, shards=(), kind=jnp.bfloat16):
    values = jax.random.normal(stream_key, extent, jnp.float32) * deviation
    if len(shards) > 0:
        values = block_levels(stream_key, extent, shards, -0.22, 0.18) * values
    return jnp.clip(values, min=-reach, max=reach).astype(kind)


def setup_inputs(seed: int = 0) -> dict:
    splits = jax.random.split(jax.random.key(seed), 16)
    tokens = gaussian(splits[0], (TOKENS, D), 1.0, 6.0, ((0, 32),))
    cotangent = gaussian(splits[1], (TOKENS, D), 1.0, 6.0, ((0, 32),))
    segments = jax.vmap(lambda own: jnp.searchsorted(jnp.cumsum(uneven_parts(own, 4, SEQ, SEQ * 25 // 32, 0)), jnp.arange(SEQ), side="right"))(jax.random.split(splits[2], NSEQ)).reshape((NSEQ, SEQ)).astype(jnp.int32)
    random_blocks = plant(jax.random.randint(splits[3], (NSEQ, NB, HEADS, RAND), 0, NB), jax.random.fold_in(splits[3], 1), 0, NB - 1).astype(jnp.int32)
    step_count = jax.random.randint(splits[4], (1,), 1, 8).astype(jnp.int32)
    adam_rates = jnp.clip(jax.random.uniform(splits[5], (2,), jnp.float32, 0.05, 0.3), 0.05, 0.3)
    attn_master = draw_attn_master(jax.random.fold_in(splits[15], 71), 0)
    attn_mean = gaussian(splits[7], (D, 4 * HA), 1.0, 6.0, ((0, 2),), jnp.float32)
    attn_square = jnp.clip(jnp.exp(math.log(10.0) - 4.6051702 * jax.random.uniform(splits[8], (D, 4 * HA), jnp.float32) ** block_levels(splits[8], (D, 4 * HA), ((0, 2),), -0.2, 0.2)), 0.1, 10.0)
    ffn_master = gaussian(splits[9], (2, D, FF), D ** -0.5, 0.25, ((1, 2),), jnp.float32)
    ffn_mean = gaussian(splits[10], (2, D, FF), 1.0, 6.0, ((1, 2),), jnp.float32)
    ffn_square = jnp.clip(jnp.exp(math.log(10.0) - 4.6051702 * jax.random.uniform(splits[11], (2, D, FF), jnp.float32) ** block_levels(splits[11], (2, D, FF), ((1, 2),), -0.2, 0.2)), 0.1, 10.0)
    small_master = draw_small_master(jax.random.fold_in(splits[15], 71), 0)
    small_mean = gaussian(splits[13], (12, D), 1.0, 6.0, ((1, 2),), jnp.float32)
    small_square = jnp.clip(jnp.exp(math.log(10.0) - 4.6051702 * jax.random.uniform(splits[14], (12, D), jnp.float32) ** block_levels(splits[14], (12, D), ((1, 2),), -0.2, 0.2)), 0.1, 10.0)
    return dict(tokens=tokens, cotangent=cotangent, segments=segments, random_blocks=random_blocks, step_count=step_count, adam_rates=adam_rates, attn_master=attn_master, attn_mean=attn_mean, attn_square=attn_square, ffn_master=ffn_master, ffn_mean=ffn_mean, ffn_square=ffn_square, small_master=small_master, small_mean=small_mean, small_square=small_square)


norm_eps = 1e-12
beta_one = 0.9
beta_two = 0.999
adam_eps = 1e-08

@jax.custom_vjp
def low(v):
    return lax.optimization_barrier(v.astype(jnp.bfloat16)).astype(jnp.float32)

@jax.custom_vjp
def low_back(v):
    return v

def low_keep(v):
    return (low(v), None)

def low_pass(kept, grad):
    return (grad,)

def back_keep(v):
    return (v, None)

def back_low(kept, grad):
    return (low(grad),)
low.defvjp(low_keep, low_pass)
low_back.defvjp(back_keep, back_low)

def matmul(left, right):
    return jnp.dot(left, right, precision=lax.Precision.HIGHEST)

def norm_rows(hidden, gain, shift):
    center = hidden - lax.optimization_barrier(jnp.mean(hidden, axis=-1, keepdims=True))
    spread = lax.optimization_barrier(jnp.mean(center * center, axis=-1, keepdims=True))
    return center * lax.rsqrt(spread + norm_eps) * gain + shift

def key_mask(picks, seg_ids):
    block_ids = jnp.arange(NB)
    query_blocks = block_ids[:, None]
    key_blocks = block_ids[None, :]
    allowed = (jnp.abs(query_blocks - key_blocks) <= 1) | (query_blocks == 0) | (query_blocks == NB - 1)
    allowed = allowed | (key_blocks == 0) | (key_blocks == NB - 1)
    allowed = allowed | jnp.any(picks[:, :, None] == block_ids[None, None, :], axis=1)
    spread_mask = jnp.repeat(jnp.repeat(allowed, BLOCK, axis=0), BLOCK, axis=1)
    return spread_mask & (seg_ids[:, None] == seg_ids[None, :])

def head_attend(items):
    query, keys_in, values_in, picks, seg_ids = items
    scores = low_back(matmul(query, keys_in.T) * HD ** (-0.5))
    scores = jnp.where(key_mask(picks, seg_ids), scores, -1e+30)
    weights = low(jax.nn.softmax(scores, axis=-1))
    return matmul(weights, values_in)

def forward(inputs, attn_w, ffn_w, small_w, seg_rows, pick_rows):
    attn_w = low(attn_w)
    ffn_w = low(ffn_w)
    small_w = low(small_w)
    seq_count = seg_rows.shape[0]
    bias_qkv = jnp.concatenate([small_w[6], jnp.zeros((HA,), inputs.dtype), small_w[7]])
    qkv = low(low_back(matmul(inputs, attn_w[:, :3 * HA]) + bias_qkv))
    parts = qkv.reshape(seq_count, SEQ, 3, HEADS, HD).transpose(2, 0, 3, 1, 4).reshape(3, seq_count * HEADS, SEQ, HD)
    seg_heads = jnp.repeat(seg_rows, HEADS, axis=0)
    pick_heads = pick_rows.transpose(0, 2, 1, 3).reshape(seq_count * HEADS, NB, RAND)
    mixed = lax.map(jax.checkpoint(head_attend), (parts[0], parts[1], parts[2], pick_heads, seg_heads))
    mixed = mixed.reshape(seq_count, HEADS, SEQ, HD).transpose(0, 2, 1, 3).reshape(seq_count * SEQ, HA)
    mixed = low(low_back(mixed))
    attn_out = low_back(matmul(mixed, attn_w[:, 3 * HA:].T) + small_w[4])
    normed = norm_rows(inputs + attn_out, small_w[0], small_w[1])
    up_in = low_back(matmul(low(normed), ffn_w[0]) + small_w[8:12].reshape(-1))
    active = low(jax.nn.gelu(up_in, approximate=False))
    ffn_out = low_back(matmul(active, ffn_w[1].T) + small_w[5])
    return norm_rows(normed + ffn_out, small_w[2], small_w[3])

def adamw(weight, mean_in, square_in, grad, step_value, learn, decay):
    mean_out = beta_one * mean_in + (1.0 - beta_one) * grad
    square_out = beta_two * square_in + (1.0 - beta_two) * grad * grad
    mean_hat = mean_out / (1.0 - beta_one ** step_value)
    square_hat = square_out / (1.0 - beta_two ** step_value)
    weight_out = weight - learn * (mean_hat / (jnp.sqrt(square_hat) + adam_eps) + decay * weight)
    return (weight_out, mean_out, square_out)

def reference(tokens, cotangent, segments, random_blocks, step_count, adam_rates, attn_master, attn_mean, attn_square, ffn_master, ffn_mean, ffn_square, small_master, small_mean, small_square):
    per_group = 4
    batches = NSEQ // per_group
    token_groups = tokens.astype(jnp.float32).reshape(batches, per_group * SEQ, D)
    upstream_groups = cotangent.astype(jnp.float32).reshape(batches, per_group * SEQ, D)
    seg_groups = segments.reshape(batches, per_group, SEQ)
    pick_groups = random_blocks.reshape(batches, per_group, NB, HEADS, RAND)

    def group_grad(totals, items):
        inputs, upstream, seg_rows, pick_rows = items

        def local_forward(inputs_f, attn_w, ffn_w, small_w):
            return forward(inputs_f, attn_w, ffn_w, small_w, seg_rows, pick_rows)
        result, pullback = jax.vjp(local_forward, inputs, attn_master, ffn_master, small_master)
        grad_in, grad_attn, grad_ffn, grad_small = pullback(upstream)
        totals = (totals[0] + grad_attn, totals[1] + grad_ffn, totals[2] + grad_small)
        return (totals, (result.astype(jnp.bfloat16), grad_in.astype(jnp.bfloat16)))
    initial = (jnp.zeros_like(attn_master), jnp.zeros_like(ffn_master), jnp.zeros_like(small_master))
    grads, outputs = lax.scan(group_grad, initial, (token_groups, upstream_groups, seg_groups, pick_groups))
    layer_out = outputs[0].reshape(TOKENS, D)
    input_grad = outputs[1].reshape(TOKENS, D)
    step_value = step_count[0].astype(attn_master.dtype)
    learn = adam_rates[0]
    decay = adam_rates[1]
    attn_new = adamw(attn_master, attn_mean, attn_square, grads[0], step_value, learn, decay)
    ffn_new = adamw(ffn_master, ffn_mean, ffn_square, grads[1], step_value, learn, decay)
    small_new = adamw(small_master, small_mean, small_square, grads[2], step_value, learn, 0.0 * decay)
    return (layer_out, input_grad, attn_new[0], attn_new[1], attn_new[2], attn_new[0].astype(jnp.bfloat16), ffn_new[0], ffn_new[1], ffn_new[2], ffn_new[0].astype(jnp.bfloat16), small_new[0], small_new[1], small_new[2], small_new[0].astype(jnp.bfloat16))
```

```python
import functools

import jax
import jax.numpy as jnp
from jax import lax
from jax.experimental import pallas as pl
from jax.experimental.pallas import tpu as pltpu
from jax.sharding import PartitionSpec as P

HD = 64
LANES = 128
BF = jnp.bfloat16
F32 = jnp.float32
BLOCKED = -(2.0**100)
NN = (((1,), (0,)), ((), ()))
NT = (((1,), (1,)), ((), ()))
TN = (((0,), (0,)), ((), ()))

norm_eps = 1e-12
beta_one = 0.9
beta_two = 0.999
adam_eps = 1e-08


def dotf(a, b, dims=NN):
    return lax.dot_general(a, b, dims, preferred_element_type=F32)


def params():
    return pltpu.CompilerParams(vmem_limit_bytes=56 << 20)


def cost(flops, bytes_accessed, transcendentals=0):
    return pl.CostEstimate(
        flops=int(flops), bytes_accessed=int(bytes_accessed), transcendentals=int(transcendentals)
    )


def shape(dims, dtype):
    return jax.ShapeDtypeStruct(dims, dtype)


VM = pl.BlockSpec(memory_space=pltpu.VMEM)
SM = pl.BlockSpec(memory_space=pltpu.SMEM)


def mask_tables(segments, random_blocks):
    length = segments.shape[1]
    blocks = random_blocks.shape[1]
    lane = jnp.arange(LANES)[None, :]
    block_of = (jnp.arange(length) // (length // blocks))[:, None]
    marks = ((lane == block_of) | (lane == blocks + segments[0][:, None])).astype(BF)
    picks = random_blocks[0].transpose(1, 0, 2)
    row = jnp.arange(LANES)[:, None]
    col = jnp.arange(LANES)[None, :]
    is_block = (row < blocks) & (col < blocks)
    seen = (jnp.abs(row - col) <= 1) | (row == 0) | (row == blocks - 1)
    seen = (seen | (col == 0) | (col == blocks - 1))[None]
    padded = jnp.pad(picks, ((0, 0), (0, LANES - blocks), (0, 0)), constant_values=-1)
    for slot in range(picks.shape[2]):
        seen = seen | (padded[:, None, :, slot] == row[None])
    other_segment = (row >= blocks) & (col >= blocks) & (row != col)
    bad = jnp.where(is_block[None], ~seen, other_segment[None])
    return marks, jnp.where(bad, BLOCKED, 0.0).astype(BF)


def qkv_kernel(
    place, tok_ref, own_ref, near_ref, far_ref, qkv_ref, full_ref, rows_ref, small_scr, *, tile
):
    half = own_ref.shape[0]
    quarter = near_ref.shape[0]
    width = full_ref.shape[1]
    shard = place[0]
    core = place[1]
    other = (1 - shard) * half
    at_own = pl.ds(pl.multiple_of(shard * half, quarter), half)
    at_near = pl.ds(pl.multiple_of(other + core * quarter, quarter), quarter)
    at_far = pl.ds(pl.multiple_of(other + (1 - core) * quarter, quarter), quarter)
    for where, ref in ((at_own, own_ref), (at_near, near_ref), (at_far, far_ref)):
        full_ref[where, :] = ref[:, :width]
        small_scr[where, :] = ref[:, width:].astype(F32)
    rows = jnp.transpose(small_scr[...])[: rows_ref.shape[0], :]
    rows_ref[...] = rows
    feat = width // 3
    bias = jnp.concatenate([rows[6:7], jnp.zeros((1, feat), F32), rows[7:8]], axis=1)
    for at in range(0, tok_ref.shape[0], tile):
        here = pl.ds(at, tile)
        qkv_ref[here, :] = (dotf(tok_ref[here, :], full_ref[...]) + bias).astype(BF)


def qkv_project(place, tokens, own, near, far):
    length, model = tokens.shape
    width = own.shape[1] - LANES
    return pl.pallas_call(
        functools.partial(qkv_kernel, tile=256),
        in_specs=[SM, VM, VM, VM, VM],
        out_specs=[VM, VM, VM],
        out_shape=[
            shape((length, width), BF),
            shape((model, width), BF),
            shape((16, model), F32),
        ],
        scratch_shapes=[pltpu.VMEM((model, LANES), F32)],
        compiler_params=params(),
        cost_estimate=cost(2 * length * model * width, 8 << 20),
        name="qkv_project",
    )(place, tokens, own, near, far)


def attend_kernel(q_ref, k_ref, v_ref, marks_ref, table_ref, o_ref, lse_ref, even, odd, *, tile):
    length = q_ref.shape[0]
    pair = pl.program_id(0)
    lane = lax.broadcasted_iota(jnp.int32, (1, LANES), 1)
    zero = jnp.zeros((), BF)
    keys, values = [], []
    for head in range(2):
        key_marks = dotf(marks_ref[...], table_ref[head]).astype(BF)
        keys.append(jnp.concatenate([k_ref[...], key_marks], axis=1))
        values.append(jnp.where(lane // HD == head, v_ref[...], zero))
    steps = [(at, head) for at in range(0, length, tile) for head in range(2)]
    held = [even, odd]

    def score(index):
        at, head = steps[index]
        here = pl.ds(at, tile)
        query = jnp.where(lane // HD == head, q_ref[here, :] * jnp.asarray(HD**-0.5, BF), zero)
        return dotf(jnp.concatenate([query, marks_ref[here, :]], axis=1), keys[head], NT)

    held[0][...] = score(0)
    first = None
    for index, (at, head) in enumerate(steps):
        here = pl.ds(at, tile)
        if index + 1 < len(steps):
            held[(index + 1) % 2][...] = score(index + 1)
        now = held[index % 2]
        top = jnp.max(now[...], axis=1, keepdims=True)
        raised = jnp.exp(now[...] - top)
        total = jnp.sum(raised, axis=1, keepdims=True)
        mixed = dotf(raised.astype(BF), values[head]) * (1.0 / total)
        log_total = top + jnp.log(total)
        kept = lse_ref[here, :]
        if head == 0:
            first = mixed
            kept = jnp.where(lane < 2 * pair, kept, 0.0)
        else:
            o_ref[here, :] = (first + mixed).astype(BF)
        lse_ref[here, :] = jnp.where(lane == 2 * pair + head, log_total, kept)


def attend(qkv, marks, table):
    length = qkv.shape[0]
    feat = qkv.shape[1] // 3
    pairs = feat // LANES
    tile = 256
    block = lambda pick: pl.BlockSpec((length, LANES), pick)
    return pl.pallas_call(
        functools.partial(attend_kernel, tile=tile),
        grid=(pairs,),
        in_specs=[
            block(lambda i: (0, i)),
            block(lambda i: (0, pairs + i)),
            block(lambda i: (0, 2 * pairs + i)),
            block(lambda i: (0, 0)),
            pl.BlockSpec((2, LANES, LANES), lambda i: (i, 0, 0)),
        ],
        out_specs=[block(lambda i: (0, i)), block(lambda i: (0, 0))],
        out_shape=[shape((length, feat), BF), shape((length, LANES), F32)],
        scratch_shapes=[pltpu.VMEM((tile, length), F32)] * 2,
        compiler_params=params(),
        cost_estimate=cost(16e9, 6 << 20, 8 << 20),
        name="attend",
    )(qkv, qkv, qkv, marks, table)


def attend_back_kernel(
    q_ref,
    k_ref,
    v_ref,
    do_ref,
    o_ref,
    marks_ref,
    table_ref,
    lse_ref,
    dq_ref,
    dk_ref,
    dv_ref,
    lse_rows,
    dv_sum,
    dk_sum,
    *,
    tile,
):
    length = q_ref.shape[0]
    pair = pl.program_id(0)
    lane = lax.broadcasted_iota(jnp.int32, (1, LANES), 1)
    zero = jnp.zeros((), BF)
    scale = jnp.asarray(HD**-0.5, BF)

    @pl.when(pair == 0)
    def _():
        lse_rows[...] = jnp.transpose(lse_ref[...])

    prod = do_ref[...].astype(F32) * o_ref[...].astype(F32)
    high = prod.astype(BF)
    rest = (prod - high.astype(F32)).astype(BF)
    pick = (
        lax.broadcasted_iota(jnp.int32, (8, LANES), 0)
        == lax.broadcasted_iota(jnp.int32, (8, LANES), 1) // HD
    ).astype(BF)
    inner = dotf(pick, high, NT) + dotf(pick, rest, NT)
    for head in range(2):
        mine = lane // HD == head
        key_marks = dotf(marks_ref[...], table_ref[head]).astype(BF)
        keys = jnp.concatenate([k_ref[...], key_marks], axis=1)
        keys_scaled = jnp.where(mine, k_ref[...] * scale, zero)
        log_total = lse_rows[pl.ds(2 * pair + head, 1), :]
        for at in range(0, length, tile):
            here = pl.ds(at, tile)
            query = jnp.where(mine, q_ref[here, :] * scale, zero)
            upstream = jnp.where(mine, do_ref[here, :], zero)
            scores = dotf(keys, jnp.concatenate([query, marks_ref[here, :]], axis=1), NT)
            probs = jnp.exp(scores - log_total[:, at : at + tile])
            grad_probs = dotf(v_ref[...], upstream, NT)
            grad_scores = (probs * (grad_probs - inner[head : head + 1, at : at + tile])).astype(BF)
            grad_v = dotf(probs.astype(BF), upstream)
            grad_k = dotf(grad_scores, query)
            grad_q = dotf(grad_scores, keys_scaled, TN)
            if head == 0 and at == 0:
                dv_sum[...] = grad_v
                dk_sum[...] = grad_k
            else:
                dv_sum[...] += grad_v
                dk_sum[...] += grad_k
            if head == 0:
                dq_ref[here, :] = grad_q.astype(BF)
            else:
                dq_ref[here, :] = jnp.where(mine, grad_q.astype(BF), dq_ref[here, :])
    dk_ref[...] = dk_sum[...].astype(BF)
    dv_ref[...] = dv_sum[...].astype(BF)


def attend_back(qkv, grad_mixed, mixed, marks, table, lse):
    length = qkv.shape[0]
    feat = qkv.shape[1] // 3
    pairs = feat // LANES
    block = lambda pick: pl.BlockSpec((length, LANES), pick)
    return pl.pallas_call(
        functools.partial(attend_back_kernel, tile=512),
        grid=(pairs,),
        in_specs=[
            block(lambda i: (0, i)),
            block(lambda i: (0, pairs + i)),
            block(lambda i: (0, 2 * pairs + i)),
            block(lambda i: (0, i)),
            block(lambda i: (0, i)),
            block(lambda i: (0, 0)),
            pl.BlockSpec((2, LANES, LANES), lambda i: (i, 0, 0)),
            block(lambda i: (0, 0)),
        ],
        out_specs=[block(lambda i: (0, i))] * 3,
        out_shape=[shape((length, feat), BF)] * 3,
        scratch_shapes=[
            pltpu.VMEM((LANES, length), F32),
            pltpu.VMEM((length, LANES), F32),
            pltpu.VMEM((length, LANES), F32),
        ],
        compiler_params=params(),
        cost_estimate=cost(30e9, 10 << 20, 8 << 20),
        name="attend_back",
    )(qkv, qkv, qkv, grad_mixed, mixed, marks, table, lse)


def piece_order(lhs_ref, core):
    quarter = lhs_ref.shape[1] // 4
    cols = []
    for target in (core, 1 - core):
        for half in range(2):
            start = pl.multiple_of(half * 2 * quarter + target * quarter, quarter)
            cols.append(lhs_ref[:, pl.ds(start, quarter)])
    return jnp.transpose(jnp.concatenate(cols, axis=1))


def store_pieces(result, core, outs, cols):
    quarter = result.shape[0] // 4
    piece = quarter // 4
    for which, target in enumerate((core, 1 - core)):
        for r0 in range(2):
            for r2 in range(2):
                for r3 in range(2):
                    at = which * 2 * quarter + r0 * quarter + r2 * 2 * piece + r3 * piece
                    spot = jnp.where(target == 0, r0 * 4 + r2 * 2 + r3, r3 * 4 + r2 * 2 + r0)
                    rows = pl.ds(pl.multiple_of(spot * piece, piece), piece)
                    outs[which][rows, cols] = result[at : at + piece, :]


def weight_grad(lhs_t, rhs_ref, core, outs, first, tile=512):
    for at in range(0, rhs_ref.shape[1], tile):
        result = dotf(lhs_t, rhs_ref[:, at : at + tile]).astype(BF)
        store_pieces(result, core, outs, slice(first + at, first + at + tile))


def normed(hidden):
    center = hidden - jnp.mean(hidden, axis=-1, keepdims=True)
    spread = jnp.mean(center * center, axis=-1, keepdims=True)
    rate = lax.rsqrt(spread + norm_eps)
    return center * rate, rate


def norm_back(grad, unit, rate):
    return rate * (
        grad
        - jnp.mean(grad, axis=-1, keepdims=True)
        - unit * jnp.mean(grad * unit, axis=-1, keepdims=True)
    )


def col_sum(values):
    return jnp.sum(values, axis=0, keepdims=True)


def middle_kernel(
    place,
    tok_ref,
    cot_ref,
    mixed_ref,
    rows_ref,
    own_ref,
    near_ref,
    far_ref,
    out_ref,
    dh_ref,
    do_ref,
    keep_ref,
    send_ref,
    sums_ref,
    w_scr,
    act_scr,
    du_scr,
    z_scr,
    df_scr,
    da_scr,
    sems,
    *,
    tile,
):
    length, model = tok_ref.shape
    half = own_ref.shape[0]
    quarter = near_ref.shape[0]
    shard = place[0]
    core = place[1]
    other = (1 - shard) * half
    copies = []
    for number, (ref, start, count) in enumerate(
        (
            (own_ref, shard * half, half),
            (near_ref, other + core * quarter, quarter),
            (far_ref, other + (1 - core) * quarter, quarter),
        )
    ):
        rows = pl.ds(pl.multiple_of(start, quarter), count)
        copies.append(pltpu.make_async_copy(ref, w_scr.at[rows, :], sems.at[number]))
    for copy in copies:
        copy.start()
    for copy in copies:
        copy.wait()
    hidden_count = act_scr.shape[1]
    w_up = slice(0, hidden_count)
    w_down = slice(hidden_count, 2 * hidden_count)
    w_out = slice(2 * hidden_count, w_scr.shape[1])
    row = lambda number: rows_ref[number : number + 1, :]
    bias_up = jnp.concatenate([row(8), row(9), row(10), row(11)], axis=1)
    sums = [jnp.zeros((1, model), F32)] * 6
    sum_up = jnp.zeros((1, hidden_count), F32)
    for at in range(0, length, tile):
        here = pl.ds(at, tile)
        attn_out = dotf(mixed_ref[here, :], w_scr[:, w_out], NT) + row(4)
        unit_one, rate_one = normed(tok_ref[here, :].astype(F32) + attn_out)
        z_one = unit_one * row(0) + row(1)
        z_low = z_one.astype(BF)
        z_scr[here, :] = z_low
        up = dotf(z_low, w_scr[:, w_up]) + bias_up
        below = 0.5 * (1.0 + lax.erf(up * (0.5**0.5)))
        slope = below + up * (jnp.exp(-0.5 * up * up) * (1.0 / (2.0 * 3.141592653589793) ** 0.5))
        active = (up * below).astype(BF)
        act_scr[here, :] = active
        ffn_out = dotf(active, w_scr[:, w_down], NT) + row(5)
        unit_two, rate_two = normed(z_one + ffn_out)
        out_ref[here, :] = (unit_two * row(2) + row(3)).astype(BF)
        upstream = cot_ref[here, :].astype(F32)
        grad_two = norm_back(upstream * row(2), unit_two, rate_two)
        down_low = grad_two.astype(BF)
        df_scr[here, :] = down_low
        grad_up = (dotf(down_low, w_scr[:, w_down]) * slope).astype(BF)
        du_scr[here, :] = grad_up
        grad_z = grad_two + dotf(grad_up, w_scr[:, w_up], NT)
        grad_one = norm_back(grad_z * row(0), unit_one, rate_one)
        dh_ref[here, :] = grad_one
        attn_low = grad_one.astype(BF)
        da_scr[here, :] = attn_low
        do_ref[here, :] = dotf(attn_low, w_scr[:, w_out]).astype(BF)
        parts = (
            grad_z * unit_one,
            grad_z,
            upstream * unit_two,
            upstream,
            attn_low.astype(F32),
            down_low.astype(F32),
        )
        sums = [a + col_sum(b) for a, b in zip(sums, parts)]
        sum_up = sum_up + col_sum(grad_up.astype(F32))
    for number in range(6):
        sums_ref[number : number + 1, :] = sums[number]
    sums_ref[6:8, :] = jnp.zeros((2, model), F32)
    for number in range(4):
        sums_ref[8 + number : 9 + number, :] = sum_up[:, number * model : (number + 1) * model]
    sums_ref[12:16, :] = jnp.zeros((4, model), F32)
    outs = (keep_ref, send_ref)
    weight_grad(piece_order(z_scr, core), du_scr, core, outs, 0)
    weight_grad(piece_order(df_scr, core), act_scr, core, outs, hidden_count)
    weight_grad(piece_order(da_scr, core), mixed_ref, core, outs, 2 * hidden_count)


def middle(place, tokens, cotangent, mixed, rows, own, near, far):
    length, model = tokens.shape
    width = own.shape[1]
    hidden_count = (width - mixed.shape[1]) // 2
    anywhere = pl.BlockSpec(memory_space=pl.ANY)
    return pl.pallas_call(
        functools.partial(middle_kernel, tile=256),
        in_specs=[SM, VM, VM, VM, VM, anywhere, anywhere, anywhere],
        out_specs=[VM] * 6,
        out_shape=[
            shape((length, model), BF),
            shape((length, model), F32),
            shape((length, mixed.shape[1]), BF),
            shape((model // 2, width), BF),
            shape((model // 2, width), BF),
            shape((16, model), F32),
        ],
        scratch_shapes=[
            pltpu.VMEM((model, width), BF),
            pltpu.VMEM((length, hidden_count), BF),
            pltpu.VMEM((length, hidden_count), BF),
            pltpu.VMEM((length, model), BF),
            pltpu.VMEM((length, model), BF),
            pltpu.VMEM((length, model), BF),
            pltpu.SemaphoreType.DMA((3,)),
        ],
        compiler_params=params(),
        cost_estimate=cost(16e9, 16 << 20, 4 << 20),
        name="middle",
    )(place, tokens, cotangent, mixed, rows, own, near, far)


def project_grad_kernel(place, tok_ref, dq_ref, dk_ref, dv_ref, sums_ref, keep_ref, send_ref):
    core = place[1]
    feat = dq_ref.shape[1]
    model = tok_ref.shape[1]
    outs = (keep_ref, send_ref)
    lhs_t = piece_order(tok_ref, core)
    for number, ref in enumerate((dq_ref, dk_ref, dv_ref)):
        weight_grad(lhs_t, ref, core, outs, number * feat)
    sums = jnp.concatenate(
        [
            sums_ref[0:6, :],
            col_sum(dq_ref[...].astype(F32)),
            col_sum(dv_ref[...].astype(F32)),
            sums_ref[8:16, :],
            jnp.zeros((LANES - 16, model), F32),
        ],
        axis=0,
    )
    quarter = model // 4
    blocks = []
    low = jnp.transpose(sums)
    for r0 in range(2):
        lower = low[r0 * 2 * quarter : r0 * 2 * quarter + quarter]
        upper = low[r0 * 2 * quarter + quarter : (r0 + 1) * 2 * quarter]
        blocks.append((lower, upper))
    kept = [jnp.where(core == 0, a, b) for a, b in blocks]
    sent = [jnp.where(core == 0, b, a) for a, b in blocks]
    result = jnp.concatenate(kept + sent, axis=0).astype(BF)
    store_pieces(result, core, outs, slice(3 * feat, 3 * feat + LANES))


def project_grad(place, tokens, dq, dk, dv, sums):
    length, model = tokens.shape
    width = 3 * dq.shape[1] + LANES
    return pl.pallas_call(
        project_grad_kernel,
        in_specs=[SM] + [VM] * 5,
        out_specs=[VM] * 2,
        out_shape=[shape((model // 2, width), BF)] * 2,
        compiler_params=params(),
        cost_estimate=cost(2 * length * model * width, 8 << 20),
        name="project_grad",
    )(place, tokens, dq, dk, dv, sums)


def input_grad_kernel(dh_ref, dq_ref, dk_ref, dv_ref, w_ref, out_ref, *, tile):
    feat = dq_ref.shape[1]
    for at in range(0, dh_ref.shape[0], tile):
        here = pl.ds(at, tile)
        total = dh_ref[here, :]
        for number, ref in enumerate((dq_ref, dk_ref, dv_ref)):
            total = total + dotf(ref[here, :], w_ref[:, number * feat : (number + 1) * feat], NT)
        out_ref[here, :] = total.astype(BF)


def input_gradient(dh, dq, dk, dv, weights):
    length, model = dh.shape
    return pl.pallas_call(
        functools.partial(input_grad_kernel, tile=256),
        in_specs=[VM] * 5,
        out_specs=VM,
        out_shape=shape((length, model), BF),
        compiler_params=params(),
        cost_estimate=cost(2 * length * model * 3 * dq.shape[1], 8 << 20),
        name="input_gradient",
    )(dh, dq, dk, dv, weights)


def add_low(a, b):
    return (a.astype(F32) + b.astype(F32)).astype(BF)


def flip(count, bit):
    return [(i, i ^ (1 << bit)) for i in range(count)]


def mixed_flip(count, even, odd):
    return [(i, i ^ (1 << (odd if (i >> 1) & 1 else even))) for i in range(2 * count)]


def reduce_rows(keep, send, count):
    replica = lax.axis_index("dp")
    shard = lax.axis_index("shard")
    core = replica & 1
    low, high = (replica >> 1) & 1, (replica >> 2) & 1
    both = ("dp", "shard")
    total = add_low(keep, lax.ppermute(send, "dp", flip(count, 0)))
    for even, odd, mine in (
        (0, 2, jnp.where(core == 0, shard, low)),
        (2, 3, jnp.where(core == 0, low, high)),
        (3, 0, jnp.where(core == 0, high, shard)),
    ):
        halves = total.reshape(2, total.shape[0] // 2, total.shape[1])
        given = lax.dynamic_index_in_dim(halves, 1 - mine, 0, keepdims=False)
        kept = lax.dynamic_index_in_dim(halves, mine, 0, keepdims=False)
        total = add_low(kept, lax.ppermute(given, both, mixed_flip(count, even, odd)))
    bit = 3
    while (1 << bit) < count:
        total = add_low(total, lax.ppermute(total, "dp", flip(count, bit)))
        bit += 1
    for even, odd, mine in (
        (3, 2, jnp.where(core == 0, high, low)),
        (2, 3, jnp.where(core == 0, low, high)),
    ):
        got = lax.ppermute(total, both, mixed_flip(count, even, odd))
        total = jnp.where(
            mine == 0, jnp.concatenate([total, got]), jnp.concatenate([got, total])
        )
    got = lax.ppermute(total, "dp", flip(count, 0))
    return total, got


def adamw(weight, mean_in, square_in, grad, step_value, learn, decay):
    mean_out = beta_one * mean_in + (1.0 - beta_one) * grad
    square_out = beta_two * square_in + (1.0 - beta_two) * grad * grad
    mean_hat = mean_out / (1.0 - beta_one**step_value)
    square_hat = square_out / (1.0 - beta_two**step_value)
    weight_out = weight - learn * (mean_hat / (jnp.sqrt(square_hat) + adam_eps) + decay * weight)
    return (weight_out, mean_out, square_out)


def gathered(rows, count):
    quarter = rows.shape[0] // 2
    core = lax.axis_index("dp") & 1
    mine = lax.dynamic_slice_in_dim(rows, core * quarter, quarter, 0)
    near = lax.ppermute(mine, "shard", [(0, 1), (1, 0)])
    far = lax.ppermute(near, "dp", flip(count, 0))
    return near, far


def local(
    count,
    tokens,
    cotangent,
    segments,
    random_blocks,
    step_count,
    adam_rates,
    attn_master,
    attn_mean,
    attn_square,
    ffn_master,
    ffn_mean,
    ffn_square,
    small_master,
    small_mean,
    small_square,
):
    core = lax.axis_index("dp") & 1
    place = jnp.stack([lax.axis_index("shard"), core]).astype(jnp.int32)
    feat = attn_master.shape[1] // 4
    rows_here = attn_master.shape[0]
    hidden_count = ffn_master.shape[2]
    small_cols = jnp.pad(
        small_master.T.astype(BF), ((0, 0), (0, LANES - small_master.shape[0]))
    )
    own_a = jnp.concatenate([attn_master[:, : 3 * feat].astype(BF), small_cols], axis=1)
    own_b = jnp.concatenate(
        [
            ffn_master[0].astype(BF),
            ffn_master[1].astype(BF),
            attn_master[:, 3 * feat :].astype(BF),
        ],
        axis=1,
    )
    near_a, far_a = gathered(own_a, count)
    near_b, far_b = gathered(own_b, count)
    marks, table = mask_tables(segments, random_blocks)
    qkv, w_in, rows = qkv_project(place, tokens, own_a, near_a, far_a)
    mixed, lse = attend(qkv, marks, table)
    layer_out, dh, grad_mixed, keep_b, send_b, sums = middle(
        place, tokens, cotangent, mixed, rows, own_b, near_b, far_b
    )
    mine_b, other_b = reduce_rows(keep_b, send_b, count)
    dq, dk, dv = attend_back(qkv, grad_mixed, mixed, marks, table, lse)
    keep_a, send_a = project_grad(place, tokens, dq, dk, dv, sums)
    mine_a, other_a = reduce_rows(keep_a, send_a, count)
    input_grad = input_gradient(dh, dq, dk, dv, w_in)

    def in_order(mine, other):
        return jnp.where(
            core == 0, jnp.concatenate([mine, other]), jnp.concatenate([other, mine])
        ).astype(F32)

    grad_b = in_order(mine_b, other_b)
    grad_a = in_order(mine_a, other_a)
    step_value = step_count[0].astype(F32)
    learn = adam_rates[0]
    decay = adam_rates[1]
    grad_ffn = jnp.stack([grad_b[:, :hidden_count], grad_b[:, hidden_count : 2 * hidden_count]])
    grad_attn = jnp.concatenate([grad_a[:, : 3 * feat], grad_b[:, 2 * hidden_count :]], axis=1)
    grad_small = grad_a[:, 3 * feat : 3 * feat + small_master.shape[0]].T
    attn_new = adamw(attn_master, attn_mean, attn_square, grad_attn, step_value, learn, decay)
    ffn_new = adamw(ffn_master, ffn_mean, ffn_square, grad_ffn, step_value, learn, decay)
    small_new = adamw(
        small_master, small_mean, small_square, grad_small, step_value, learn, 0.0 * decay
    )
    return (
        layer_out,
        input_grad,
        attn_new[0],
        attn_new[1],
        attn_new[2],
        attn_new[0].astype(BF),
        ffn_new[0],
        ffn_new[1],
        ffn_new[2],
        ffn_new[0].astype(BF),
        small_new[0],
        small_new[1],
        small_new[2],
        small_new[0].astype(BF),
    )


def solution(mesh):
    tokens_in = P(("dp", "shard"), None)
    rows_in = P("shard", None)
    stack_in = P(None, "shard", None)
    cols_in = P(None, "shard")
    placed = (
        (tokens_in,) * 3
        + (P(("dp", "shard"), None, None, None), P(), P())
        + (rows_in,) * 3
        + (stack_in,) * 3
        + (cols_in,) * 3
    )
    return jax.shard_map(
        functools.partial(local, mesh.shape["dp"]),
        mesh=mesh,
        in_specs=placed,
        out_specs=(tokens_in,) * 2 + (rows_in,) * 4 + (stack_in,) * 4 + (cols_in,) * 4,
        check_vma=False,
    )
```

```python
import functools

import jax
import jax.numpy as jnp
from jax import lax
from jax.experimental import pallas as pl
from jax.experimental.pallas import tpu as pltpu
from jax.sharding import PartitionSpec as P

HD = 64
LANES = 128
BF = jnp.bfloat16
F32 = jnp.float32
BLOCKED = -(2.0**100)
NN = (((1,), (0,)), ((), ()))
NT = (((1,), (1,)), ((), ()))
TN = (((0,), (0,)), ((), ()))

norm_eps = 1e-12
beta_one = 0.9
beta_two = 0.999
adam_eps = 1e-08


def dotf(a, b, dims=NN):
    return lax.dot_general(a, b, dims, preferred_element_type=F32)


def params():
    return pltpu.CompilerParams(vmem_limit_bytes=56 << 20)


def cost(flops, bytes_accessed, transcendentals=0):
    return pl.CostEstimate(
        flops=int(flops), bytes_accessed=int(bytes_accessed), transcendentals=int(transcendentals)
    )


def shape(dims, dtype):
    return jax.ShapeDtypeStruct(dims, dtype)


VM = pl.BlockSpec(memory_space=pltpu.VMEM)
SM = pl.BlockSpec(memory_space=pltpu.SMEM)


def mask_tables(segments, random_blocks):
    length = segments.shape[1]
    blocks = random_blocks.shape[1]
    lane = jnp.arange(LANES)[None, :]
    block_of = (jnp.arange(length) // (length // blocks))[:, None]
    marks = ((lane == block_of) | (lane == blocks + segments[0][:, None])).astype(BF)
    picks = random_blocks[0].transpose(1, 0, 2)
    row = jnp.arange(LANES)[:, None]
    col = jnp.arange(LANES)[None, :]
    is_block = (row < blocks) & (col < blocks)
    seen = (jnp.abs(row - col) <= 1) | (row == 0) | (row == blocks - 1)
    seen = (seen | (col == 0) | (col == blocks - 1))[None]
    padded = jnp.pad(picks, ((0, 0), (0, LANES - blocks), (0, 0)), constant_values=-1)
    for slot in range(picks.shape[2]):
        seen = seen | (padded[:, None, :, slot] == row[None])
    other_segment = (row >= blocks) & (col >= blocks) & (row != col)
    bad = jnp.where(is_block[None], ~seen, other_segment[None])
    return marks, jnp.where(bad, BLOCKED, 0.0).astype(BF)


def gathered_rows(place, own_ref, near_ref, far_ref, into, sems):
    half = own_ref.shape[0]
    quarter = near_ref.shape[0]
    shard = place[0]
    core = place[1]
    other = (1 - shard) * half
    copies = []
    for number, (ref, start, count) in enumerate(
        (
            (own_ref, shard * half, half),
            (near_ref, other + core * quarter, quarter),
            (far_ref, other + (1 - core) * quarter, quarter),
        )
    ):
        rows = pl.ds(pl.multiple_of(start, quarter), count)
        copies.append(pltpu.make_async_copy(ref, into.at[rows, :], sems.at[number]))
    return copies


def attend_kernel(
    place,
    tok_ref,
    own_ref,
    near_ref,
    far_ref,
    marks_ref,
    table_ref,
    q_ref,
    k_ref,
    v_ref,
    o_ref,
    lse_ref,
    rows_ref,
    tok_t_ref,
    w_scr,
    lse_scr,
    even,
    odd,
    sems,
    *,
    tile,
):
    length = q_ref.shape[0]
    model = tok_ref.shape[1]
    pair = pl.program_id(0)
    lane = lax.broadcasted_iota(jnp.int32, (1, LANES), 1)
    zero = jnp.zeros((), BF)

    @pl.when(pair == 0)
    def _():
        copies = gathered_rows(place, own_ref, near_ref, far_ref, w_scr, sems)
        for copy in copies:
            copy.start()
        tok_t_ref[...] = piece_order(tok_ref, place[1])
        lse_scr[...] = jnp.zeros_like(lse_scr)
        for copy in copies:
            copy.wait()
        small = w_scr[:, w_scr.shape[1] - LANES :].astype(F32)
        rows_ref[...] = jnp.transpose(small)[: rows_ref.shape[0], :]

    cols = pl.ds(pl.multiple_of(pair * 3 * LANES, LANES), 3 * LANES)
    here = pl.ds(pl.multiple_of(pair * LANES, LANES), LANES)
    bias = jnp.concatenate(
        [rows_ref[6:7, here], jnp.zeros((1, LANES), F32), rows_ref[7:8, here]], axis=1
    )
    qkv = (dotf(tok_ref[...], w_scr[:, cols]) + bias).astype(BF)
    q_ref[...] = qkv[:, :LANES]
    k_ref[...] = qkv[:, LANES : 2 * LANES]
    v_ref[...] = qkv[:, 2 * LANES :]
    keys, values = [], []
    for head in range(2):
        key_marks = dotf(marks_ref[...], table_ref[head]).astype(BF)
        keys.append(jnp.concatenate([k_ref[...], key_marks], axis=1))
        values.append(jnp.where(lane // HD == head, v_ref[...], zero))
    steps = [(at, head) for at in range(0, length, tile) for head in range(2)]
    held = [even, odd]

    def score(index):
        at, head = steps[index]
        rows = pl.ds(at, tile)
        query = jnp.where(lane // HD == head, q_ref[rows, :] * jnp.asarray(HD**-0.5, BF), zero)
        return dotf(jnp.concatenate([query, marks_ref[rows, :]], axis=1), keys[head], NT)

    held[0][...] = score(0)
    first = None
    for index, (at, head) in enumerate(steps):
        rows = pl.ds(at, tile)
        if index + 1 < len(steps):
            held[(index + 1) % 2][...] = score(index + 1)
        now = held[index % 2]
        top = jnp.max(now[...], axis=1, keepdims=True)
        raised = jnp.exp(now[...] - top)
        total = jnp.sum(raised, axis=1, keepdims=True)
        mixed = dotf(raised.astype(BF), values[head]) * (1.0 / total)
        if head == 0:
            first = mixed
        else:
            o_ref[rows, :] = (first + mixed).astype(BF)
        lse_scr[rows, :] = jnp.where(
            lane == 2 * pair + head, top + jnp.log(total), lse_scr[rows, :]
        )

    @pl.when(pair == pl.num_programs(0) - 1)
    def _():
        lse_ref[...] = jnp.transpose(lse_scr[...])[: lse_ref.shape[0], :]


def attend(place, tokens, own, near, far, marks, table):
    length, model = tokens.shape
    width = own.shape[1]
    pairs = (width - LANES) // (3 * LANES)
    tile = 256
    whole = lambda dims: pl.BlockSpec(dims, lambda i: (0,) * len(dims))
    anywhere = pl.BlockSpec(memory_space=pl.ANY)
    block = pl.BlockSpec((length, LANES), lambda i: (0, i))
    out_rows = 16
    return pl.pallas_call(
        functools.partial(attend_kernel, tile=tile),
        grid=(pairs,),
        in_specs=[
            SM,
            whole((length, model)),
            anywhere,
            anywhere,
            anywhere,
            whole((length, LANES)),
            pl.BlockSpec((2, LANES, LANES), lambda i: (i, 0, 0)),
        ],
        out_specs=[
            block,
            block,
            block,
            block,
            whole((out_rows, length)),
            whole((out_rows, model)),
            whole((model, length)),
        ],
        out_shape=[shape((length, pairs * LANES), BF)] * 4
        + [shape((out_rows, length), F32), shape((out_rows, model), F32), shape((model, length), BF)],
        scratch_shapes=[
            pltpu.VMEM((model, width), BF),
            pltpu.VMEM((length, LANES), F32),
            pltpu.VMEM((tile, length), F32),
            pltpu.VMEM((tile, length), F32),
            pltpu.SemaphoreType.DMA((3,)),
        ],
        compiler_params=params(),
        cost_estimate=cost(18e9, 12 << 20, 8 << 20),
        name="attend",
    )(place, tokens, own, near, far, marks, table)


def attend_back_kernel(
    place, q_ref, k_ref, v_ref, do_ref, o_ref, marks_ref, table_ref, lse_ref, tok_t_ref, *rest, pair, pairs, tile
):
    last = pair == pairs - 1
    rest = list(rest)
    if pair > 0:
        rest = rest[2:]
    if last:
        bias_refs, mid_ref = rest[: pairs - 1], rest[pairs - 1]
        rest = rest[pairs:]
    keep_hbm, send_hbm, d_ref, bias_ref, dv_sum, dk_sum, keep_scr, send_scr, sems = rest
    length = q_ref.shape[0]
    core = place[1]
    lane = lax.broadcasted_iota(jnp.int32, (1, LANES), 1)
    zero = jnp.zeros((), BF)
    scale = jnp.asarray(HD**-0.5, BF)
    prod = do_ref[...].astype(F32) * o_ref[...].astype(F32)
    high = prod.astype(BF)
    low = (prod - high.astype(F32)).astype(BF)
    pick = (
        lax.broadcasted_iota(jnp.int32, (8, LANES), 0)
        == lax.broadcasted_iota(jnp.int32, (8, LANES), 1) // HD
    ).astype(BF)
    inner = dotf(pick, high, NT) + dotf(pick, low, NT)
    for head in range(2):
        mine = lane // HD == head
        key_marks = dotf(marks_ref[...], table_ref[head]).astype(BF)
        keys = jnp.concatenate([k_ref[...], key_marks], axis=1)
        keys_scaled = jnp.where(mine, k_ref[...] * scale, zero)
        log_total = lse_ref[2 * pair + head : 2 * pair + head + 1, :]
        for at in range(0, length, tile):
            here = pl.ds(at, tile)
            query = jnp.where(mine, q_ref[here, :] * scale, zero)
            upstream = jnp.where(mine, do_ref[here, :], zero)
            scores = dotf(keys, jnp.concatenate([query, marks_ref[here, :]], axis=1), NT)
            probs = jnp.exp(scores - log_total[:, at : at + tile])
            grad_probs = dotf(v_ref[...], upstream, NT)
            grad_scores = (probs * (grad_probs - inner[head : head + 1, at : at + tile])).astype(BF)
            grad_v = dotf(probs.astype(BF), upstream)
            grad_k = dotf(grad_scores, query)
            grad_q = dotf(grad_scores, keys_scaled, TN)
            if head == 0 and at == 0:
                dv_sum[...] = grad_v
                dk_sum[...] = grad_k
            else:
                dv_sum[...] += grad_v
                dk_sum[...] += grad_k
            if head == 0:
                d_ref[here, :LANES] = grad_q.astype(BF)
            else:
                d_ref[here, :LANES] = jnp.where(mine, grad_q.astype(BF), d_ref[here, :LANES])
    d_ref[:, LANES : 2 * LANES] = dk_sum[...].astype(BF)
    d_ref[:, 2 * LANES :] = dv_sum[...].astype(BF)
    outs = (keep_scr, send_scr)
    result = dotf(tok_t_ref[...], d_ref[...]).astype(BF)
    store_pieces(result, core, outs, slice(0, 3 * LANES))
    sum_q = col_sum(d_ref[:, :LANES].astype(F32))
    sum_v = col_sum(d_ref[:, 2 * LANES :].astype(F32))
    bias_ref[...] = jnp.concatenate([sum_q, sum_v, jnp.zeros((6, LANES), F32)], axis=0)
    width = 3 * LANES
    if last:
        model = mid_ref.shape[1]
        sums = jnp.concatenate(
            [
                mid_ref[0:6, :],
                jnp.concatenate([ref[0:1, :] for ref in bias_refs] + [sum_q], axis=1),
                jnp.concatenate([ref[1:2, :] for ref in bias_refs] + [sum_v], axis=1),
                mid_ref[8:16, :],
                jnp.zeros((LANES - 16, model), F32),
            ],
            axis=0,
        )
        quarter = model // 4
        turned = jnp.transpose(sums)
        kept, sent = [], []
        for r0 in range(2):
            lower = turned[r0 * 2 * quarter : r0 * 2 * quarter + quarter]
            upper = turned[r0 * 2 * quarter + quarter : (r0 + 1) * 2 * quarter]
            kept.append(jnp.where(core == 0, lower, upper))
            sent.append(jnp.where(core == 0, upper, lower))
        store_pieces(
            jnp.concatenate(kept + sent, axis=0).astype(BF), core, outs, slice(width, width + LANES)
        )
        width += LANES
    copies = [
        pltpu.make_async_copy(scr, hbm.at[:, pair * 3 * LANES : pair * 3 * LANES + width], sems.at[n])
        for n, (scr, hbm) in enumerate(((keep_scr, keep_hbm), (send_scr, send_hbm)))
    ]
    for copy in copies:
        copy.start()
    for copy in copies:
        copy.wait()


def attend_back(place, pair, q, k, v, grad_mixed, mixed, marks, table, lse, tok_t, before, biases, sums):
    length = q.shape[0]
    model = tok_t.shape[0]
    pairs = q.shape[1] // LANES
    last = pair == pairs - 1
    whole = lambda dims: pl.BlockSpec(dims, lambda i: (0,) * len(dims))
    anywhere = pl.BlockSpec(memory_space=pl.ANY)
    block = pl.BlockSpec((length, LANES), lambda i: (0, pair))
    operands = [place, q, k, v, grad_mixed, mixed, marks, table, lse, tok_t]
    specs = [SM] + [block] * 5 + [whole((length, LANES))]
    specs += [pl.BlockSpec((2, LANES, LANES), lambda i: (pair, 0, 0))]
    specs += [whole(lse.shape), whole(tok_t.shape)]
    aliases = {}
    if pair > 0:
        aliases = {len(operands): 0, len(operands) + 1: 1}
        operands += list(before)
        specs += [anywhere] * 2
    width = 3 * LANES
    if last:
        operands += list(biases) + [sums]
        specs += [whole((8, LANES))] * len(biases) + [whole(sums.shape)]
        width += LANES
    total = pairs * 3 * LANES + LANES
    return pl.pallas_call(
        functools.partial(attend_back_kernel, pair=pair, pairs=pairs, tile=512),
        grid=(1,),
        in_specs=specs,
        out_specs=[anywhere, anywhere, whole((length, 3 * LANES)), whole((8, LANES))],
        out_shape=[
            shape((model // 2, total), BF),
            shape((model // 2, total), BF),
            shape((length, 3 * LANES), BF),
            shape((8, LANES), F32),
        ],
        scratch_shapes=[
            pltpu.VMEM((length, LANES), F32),
            pltpu.VMEM((length, LANES), F32),
            pltpu.VMEM((model // 2, width), BF),
            pltpu.VMEM((model // 2, width), BF),
            pltpu.SemaphoreType.DMA((2,)),
        ],
        input_output_aliases=aliases,
        compiler_params=params(),
        cost_estimate=cost(8e9, 4 << 20, 2 << 20),
        name=f"attend_back_{pair}",
    )(*operands)


def piece_order(lhs_ref, core):
    quarter = lhs_ref.shape[1] // 4
    cols = []
    for target in (core, 1 - core):
        for half in range(2):
            start = pl.multiple_of(half * 2 * quarter + target * quarter, quarter)
            cols.append(lhs_ref[:, pl.ds(start, quarter)])
    return jnp.transpose(jnp.concatenate(cols, axis=1))


def store_pieces(result, core, outs, cols):
    quarter = result.shape[0] // 4
    piece = quarter // 4
    for which, target in enumerate((core, 1 - core)):
        for r0 in range(2):
            for r2 in range(2):
                for r3 in range(2):
                    at = which * 2 * quarter + r0 * quarter + r2 * 2 * piece + r3 * piece
                    spot = jnp.where(target == 0, r0 * 4 + r2 * 2 + r3, r3 * 4 + r2 * 2 + r0)
                    rows = pl.ds(pl.multiple_of(spot * piece, piece), piece)
                    outs[which][rows, cols] = result[at : at + piece, :]


def weight_grad(lhs_t, rhs_ref, core, outs, first, tile=512):
    for at in range(0, rhs_ref.shape[1], tile):
        result = dotf(lhs_t, rhs_ref[:, at : at + tile]).astype(BF)
        store_pieces(result, core, outs, slice(first + at, first + at + tile))


def normed(hidden):
    center = hidden - jnp.mean(hidden, axis=-1, keepdims=True)
    spread = jnp.mean(center * center, axis=-1, keepdims=True)
    rate = lax.rsqrt(spread + norm_eps)
    return center * rate, rate


def norm_back(grad, unit, rate):
    return rate * (
        grad
        - jnp.mean(grad, axis=-1, keepdims=True)
        - unit * jnp.mean(grad * unit, axis=-1, keepdims=True)
    )


def col_sum(values):
    return jnp.sum(values, axis=0, keepdims=True)


def middle_kernel(
    place,
    tok_ref,
    cot_ref,
    mixed_ref,
    rows_ref,
    own_ref,
    near_ref,
    far_ref,
    out_ref,
    dh_ref,
    do_ref,
    keep_ref,
    send_ref,
    sums_ref,
    w_scr,
    act_scr,
    du_scr,
    z_scr,
    df_scr,
    da_scr,
    sems,
    *,
    tile,
):
    length, model = tok_ref.shape
    core = place[1]
    copies = gathered_rows(place, own_ref, near_ref, far_ref, w_scr, sems)
    for copy in copies:
        copy.start()
    for copy in copies:
        copy.wait()
    hidden_count = act_scr.shape[1]
    w_up = slice(0, hidden_count)
    w_down = slice(hidden_count, 2 * hidden_count)
    w_out = slice(2 * hidden_count, w_scr.shape[1])
    row = lambda number: rows_ref[number : number + 1, :]
    bias_up = jnp.concatenate([row(8), row(9), row(10), row(11)], axis=1)
    sums = [jnp.zeros((1, model), F32)] * 6
    sum_up = jnp.zeros((1, hidden_count), F32)
    for at in range(0, length, tile):
        here = pl.ds(at, tile)
        attn_out = dotf(mixed_ref[here, :], w_scr[:, w_out], NT) + row(4)
        unit_one, rate_one = normed(tok_ref[here, :].astype(F32) + attn_out)
        z_one = unit_one * row(0) + row(1)
        z_low = z_one.astype(BF)
        z_scr[here, :] = z_low
        up = dotf(z_low, w_scr[:, w_up]) + bias_up
        below = 0.5 * (1.0 + lax.erf(up * (0.5**0.5)))
        slope = below + up * (jnp.exp(-0.5 * up * up) * (1.0 / (2.0 * 3.141592653589793) ** 0.5))
        active = (up * below).astype(BF)
        act_scr[here, :] = active
        ffn_out = dotf(active, w_scr[:, w_down], NT) + row(5)
        unit_two, rate_two = normed(z_one + ffn_out)
        out_ref[here, :] = (unit_two * row(2) + row(3)).astype(BF)
        upstream = cot_ref[here, :].astype(F32)
        grad_two = norm_back(upstream * row(2), unit_two, rate_two)
        down_low = grad_two.astype(BF)
        df_scr[here, :] = down_low
        grad_up = (dotf(down_low, w_scr[:, w_down]) * slope).astype(BF)
        du_scr[here, :] = grad_up
        grad_z = grad_two + dotf(grad_up, w_scr[:, w_up], NT)
        grad_one = norm_back(grad_z * row(0), unit_one, rate_one)
        dh_ref[here, :] = grad_one
        attn_low = grad_one.astype(BF)
        da_scr[here, :] = attn_low
        do_ref[here, :] = dotf(attn_low, w_scr[:, w_out]).astype(BF)
        parts = (
            grad_z * unit_one,
            grad_z,
            upstream * unit_two,
            upstream,
            attn_low.astype(F32),
            down_low.astype(F32),
        )
        sums = [a + col_sum(b) for a, b in zip(sums, parts)]
        sum_up = sum_up + col_sum(grad_up.astype(F32))
    for number in range(6):
        sums_ref[number : number + 1, :] = sums[number]
    sums_ref[6:8, :] = jnp.zeros((2, model), F32)
    for number in range(4):
        sums_ref[8 + number : 9 + number, :] = sum_up[:, number * model : (number + 1) * model]
    sums_ref[12:16, :] = jnp.zeros((4, model), F32)
    outs = (keep_ref, send_ref)
    weight_grad(piece_order(z_scr, core), du_scr, core, outs, 0)
    weight_grad(piece_order(df_scr, core), act_scr, core, outs, hidden_count)
    weight_grad(piece_order(da_scr, core), mixed_ref, core, outs, 2 * hidden_count)


def middle(place, tokens, cotangent, mixed, rows, own, near, far):
    length, model = tokens.shape
    width = own.shape[1]
    hidden_count = (width - mixed.shape[1]) // 2
    anywhere = pl.BlockSpec(memory_space=pl.ANY)
    return pl.pallas_call(
        functools.partial(middle_kernel, tile=256),
        in_specs=[SM, VM, VM, VM, VM, anywhere, anywhere, anywhere],
        out_specs=[VM] * 6,
        out_shape=[
            shape((length, model), BF),
            shape((length, model), F32),
            shape((length, mixed.shape[1]), BF),
            shape((model // 2, width), BF),
            shape((model // 2, width), BF),
            shape((16, model), F32),
        ],
        scratch_shapes=[
            pltpu.VMEM((model, width), BF),
            pltpu.VMEM((length, hidden_count), BF),
            pltpu.VMEM((length, hidden_count), BF),
            pltpu.VMEM((length, model), BF),
            pltpu.VMEM((length, model), BF),
            pltpu.VMEM((length, model), BF),
            pltpu.SemaphoreType.DMA((3,)),
        ],
        compiler_params=params(),
        cost_estimate=cost(16e9, 16 << 20, 4 << 20),
        name="middle",
    )(place, tokens, cotangent, mixed, rows, own, near, far)


def input_grad_kernel(place, dh_ref, *rest, parts):
    grads = rest[:parts]
    own_ref, near_ref, far_ref, out_ref, w_scr, sems = rest[parts:]
    width = grads[0].shape[1]

    @pl.when(pl.program_id(0) == 0)
    def _():
        copies = gathered_rows(place, own_ref, near_ref, far_ref, w_scr, sems)
        for copy in copies:
            copy.start()
        for copy in copies:
            copy.wait()

    total = dh_ref[...]
    for number, ref in enumerate(grads):
        total = total + dotf(ref[...], w_scr[:, number * width : (number + 1) * width], NT)
    out_ref[...] = total.astype(BF)


def input_gradient(place, dh, grads, own, near, far):
    length, model = dh.shape
    tile = 256
    anywhere = pl.BlockSpec(memory_space=pl.ANY)
    rows = lambda width: pl.BlockSpec((tile, width), lambda i: (i, 0))
    return pl.pallas_call(
        functools.partial(input_grad_kernel, parts=len(grads)),
        grid=(length // tile,),
        in_specs=[SM, rows(model)] + [rows(g.shape[1]) for g in grads] + [anywhere] * 3,
        out_specs=rows(model),
        out_shape=shape((length, model), BF),
        scratch_shapes=[pltpu.VMEM((model, own.shape[1]), BF), pltpu.SemaphoreType.DMA((3,))],
        compiler_params=params(),
        cost_estimate=cost(2 * length * model * 3 * grads[0].shape[1] * len(grads), 8 << 20),
        name="input_gradient",
    )(place, dh, *grads, own, near, far)


def add_low(a, b):
    return (a.astype(F32) + b.astype(F32)).astype(BF)


def halve_kernel(place, keep_ref, got_ref, send_ref, kept_ref, *, which):
    half = send_ref.shape[0]
    mine = place[which]
    for out, side in ((send_ref, 1 - mine), (kept_ref, mine)):
        rows = pl.ds(pl.multiple_of(side * half, half), half)
        out[...] = add_low(keep_ref[rows, :], got_ref[rows, :])


def halve(place, keep, got, which):
    rows, width = keep.shape
    return pl.pallas_call(
        functools.partial(halve_kernel, which=which),
        in_specs=[SM, VM, VM],
        out_specs=[VM, VM],
        out_shape=[shape((rows // 2, width), BF)] * 2,
        compiler_params=params(),
        cost_estimate=cost(rows * width, 8 * rows * width),
        name="halve",
    )(place, keep, got)


def flip(count, bit):
    return [(i, i ^ (1 << bit)) for i in range(count)]


def mixed_flip(count, even, odd):
    return [(i, i ^ (1 << (odd if (i >> 1) & 1 else even))) for i in range(2 * count)]


STEPS = ((0, 2), (2, 3), (3, 0))


def swap_core(value, count):
    return lax.ppermute(value, "dp", flip(count, 0))


def swap_mixed(value, count, step):
    return lax.ppermute(value, ("dp", "shard"), mixed_flip(count, *step))


def spread_rest(total, count):
    bit = 3
    while (1 << bit) < count:
        total = add_low(total, lax.ppermute(total, "dp", flip(count, bit)))
        bit += 1
    return total


def gather_pieces(total, count):
    for step in ((3, 2), (2, 3)):
        total = jnp.concatenate([total, swap_mixed(total, count, step)])
    return total, swap_core(total, count)


def after(value, *others):
    return lax.optimization_barrier((value,) + others)[0]


def adam_values(scalars, weight_ref, mean_ref, square_ref, grad, decay, outs):
    weight = weight_ref[...]
    mean_out = beta_one * mean_ref[...] + (1.0 - beta_one) * grad
    square_out = beta_two * square_ref[...] + (1.0 - beta_two) * grad * grad
    mean_hat = mean_out * scalars[2]
    square_hat = square_out * scalars[3]
    weight_out = weight - scalars[0] * (
        mean_hat / (jnp.sqrt(square_hat) + adam_eps) + decay * weight
    )
    outs[0][...] = weight_out
    outs[1][...] = mean_out
    outs[2][...] = square_out
    outs[3][...] = weight_out.astype(BF)


def ordered_rows(place, mine_ref, other_ref, half):
    piece = mine_ref.shape[0] // 2
    own = half == place[1]
    bit = jnp.where(own, place[5], place[4])
    spots = [pl.ds(pl.multiple_of((r3 ^ bit) * piece, piece), piece) for r3 in range(2)]
    pick = lambda rows: jnp.where(own, mine_ref[rows, :].astype(F32), other_ref[rows, :].astype(F32))
    return jnp.concatenate([pick(rows) for rows in spots], axis=0)


def adam_ffn_kernel(place, scalars, mine_ref, other_ref, w_ref, m_ref, s_ref, *outs):
    grad = ordered_rows(place, mine_ref, other_ref, pl.program_id(1))[None]
    adam_values(scalars, w_ref, m_ref, s_ref, grad, scalars[1], outs)


def adam_attn_kernel(
    place, scalars, mine_ref, other_ref, mine_o, other_o, w_ref, m_ref, s_ref, sw, sm, ss, *rest
):
    outs, small_outs, small_scr = rest[:4], rest[4:8], rest[8]
    half, r2 = pl.program_id(0), pl.program_id(1)
    grad = ordered_rows(place, mine_ref, other_ref, half)
    out_grad = ordered_rows(place, mine_o, other_o, half)
    pairs = grad.shape[1] // (3 * LANES)
    parts = [
        grad[:, p * 3 * LANES + kind * LANES : p * 3 * LANES + (kind + 1) * LANES]
        for kind in range(3)
        for p in range(pairs)
    ]
    adam_values(
        scalars, w_ref, m_ref, s_ref, jnp.concatenate(parts + [out_grad], axis=1), scalars[1], outs
    )
    count = grad.shape[0]
    small_scr[pl.ds(pl.multiple_of((half * 2 + r2) * count, count), count), :] = grad[
        :, pairs * 3 * LANES :
    ]

    @pl.when((half == 1) & (r2 == 1))
    def _():
        turned = jnp.transpose(small_scr[...])[: sw.shape[0], :]
        adam_values(scalars, sw, sm, ss, turned, 0.0 * scalars[1], small_outs)


def piece_maps(cols):
    def mine(half, r2, place):
        return (jnp.where(half == place[1], r2 ^ place[4], 0), cols)

    def other(half, r2, place):
        return (jnp.where(half == place[1], 0, r2 ^ place[5]), cols)

    return mine, other


def adam_ffn(place, scalars, mine, other, weight, mean, square):
    stack, rows, width = weight.shape
    count = rows // 4

    def at(pick):
        return pl.BlockSpec((count, width), lambda w, h, r, place, sc: (pick(h, r, place)[0], w))

    maps = piece_maps(0)
    state = pl.BlockSpec((1, count, width), lambda w, h, r, place, sc: (w, 2 * h + r, 0))
    return pl.pallas_call(
        adam_ffn_kernel,
        grid_spec=pltpu.PrefetchScalarGridSpec(
            num_scalar_prefetch=2,
            grid=(stack, 2, 2),
            in_specs=[at(maps[0]), at(maps[1]), state, state, state],
            out_specs=[state] * 4,
        ),
        out_shape=[shape(weight.shape, F32)] * 3 + [shape(weight.shape, BF)],
        compiler_params=params(),
        cost_estimate=cost(20 * stack * rows * width, 28 * stack * rows * width),
        name="adam_ffn",
    )(place, scalars, mine, other, weight, mean, square)


def adam_attn(place, scalars, mine, other, mine_b, other_b, weight, mean, square, small):
    rows, width = weight.shape
    count = rows // 4
    out_width = width // 4

    def at(pick, cols, block):
        return pl.BlockSpec((count, block), lambda h, r, place, sc: (pick(h, r, place)[0], cols))

    maps = piece_maps(0)
    state = pl.BlockSpec((count, width), lambda h, r, place, sc: (2 * h + r, 0))
    little = pl.BlockSpec(small[0].shape, lambda h, r, place, sc: (0, 0))
    last = (mine_b.shape[1] - out_width) // out_width
    return pl.pallas_call(
        adam_attn_kernel,
        grid_spec=pltpu.PrefetchScalarGridSpec(
            num_scalar_prefetch=2,
            grid=(2, 2),
            in_specs=[at(p, 0, mine.shape[1]) for p in maps]
            + [at(p, last, out_width) for p in maps]
            + [state] * 3
            + [little] * 3,
            out_specs=[state] * 4 + [little] * 4,
            scratch_shapes=[pltpu.VMEM((rows, LANES), F32)],
        ),
        out_shape=[shape(weight.shape, F32)] * 3
        + [shape(weight.shape, BF)]
        + [shape(small[0].shape, F32)] * 3
        + [shape(small[0].shape, BF)],
        compiler_params=params(),
        cost_estimate=cost(20 * rows * width, 28 * rows * width),
        name="adam_attn",
    )(place, scalars, mine, other, mine_b, other_b, weight, mean, square, *small)


def fetched(rows, count):
    quarter = rows.shape[0] // 2
    core = lax.axis_index("dp") & 1
    mine = lax.dynamic_slice_in_dim(rows, core * quarter, quarter, 0)
    return lax.ppermute(mine, "shard", [(0, 1), (1, 0)])


def local(
    count,
    tokens,
    cotangent,
    segments,
    random_blocks,
    step_count,
    adam_rates,
    attn_master,
    attn_mean,
    attn_square,
    ffn_master,
    ffn_mean,
    ffn_square,
    small_master,
    small_mean,
    small_square,
):
    replica = lax.axis_index("dp")
    shard = lax.axis_index("shard")
    core, low, high = replica & 1, (replica >> 1) & 1, (replica >> 2) & 1
    even = core == 0
    place = jnp.stack(
        [
            shard,
            core,
            jnp.zeros_like(core),
            jnp.where(even, shard, low),
            jnp.where(even, low, high),
            jnp.where(even, high, low),
            jnp.where(even, high, shard),
        ]
    ).astype(jnp.int32)
    feat = attn_master.shape[1] // 4
    pairs = feat // LANES
    groups = [
        attn_master[:, kind * feat + p * LANES : kind * feat + (p + 1) * LANES]
        for p in range(pairs)
        for kind in range(3)
    ]
    small_cols = jnp.pad(small_master.T, ((0, 0), (0, LANES - small_master.shape[0])))
    own_a = jnp.concatenate(groups + [small_cols], axis=1).astype(BF)
    own_b = jnp.concatenate(
        [ffn_master[0], ffn_master[1], attn_master[:, 3 * feat :]], axis=1
    ).astype(BF)
    near_a = fetched(own_a, count)
    far_a = swap_core(near_a, count)
    near_b = fetched(own_b, count)
    marks, table = mask_tables(segments, random_blocks)
    q, k, v, mixed, lse, rows, tok_t = attend(place, tokens, own_a, near_a, far_a, marks, table)
    near_b = after(near_b, lse)
    far_b = swap_core(near_b, count)
    layer_out, dh, grad_mixed, keep_b, send_b, sums = middle(
        place, tokens, cotangent, mixed, rows, own_b, near_b, far_b
    )
    send_b, keep_b = halve(place, keep_b, swap_core(send_b, count), 3)
    got_b = swap_mixed(send_b, count, STEPS[0])
    back = functools.partial(attend_back, place)
    before, biases, grads = None, [], []
    for pair in range(pairs):
        grad_mixed = after(grad_mixed, send_b)
        *before, grad, bias = back(
            pair, q, k, v, grad_mixed, mixed, marks, table, lse, tok_t, before, biases, sums
        )
        biases.append(bias)
        grads.append(grad)
        if pair == pairs - 3:
            send_b, keep_b = halve(place, keep_b, after(got_b, bias), 4)
            got_b = swap_mixed(send_b, count, STEPS[1])
        elif pair == pairs - 2:
            send_b, keep_b = halve(place, keep_b, after(got_b, bias), 6)
            got_b = swap_mixed(send_b, count, STEPS[2])
    keep_a, send_a = before
    total_b = spread_rest(add_low(keep_b, after(got_b, bias)), count)
    mine_b, other_b = gather_pieces(total_b, count)
    send_a, keep_a = halve(place, keep_a, swap_core(send_a, count), 3)
    for which, step in ((4, STEPS[0]), (6, STEPS[1])):
        send_a, keep_a = halve(place, keep_a, swap_mixed(send_a, count, step), which)
    total_a = spread_rest(add_low(keep_a, swap_mixed(send_a, count, STEPS[2])), count)
    mine_a, other_a = gather_pieces(total_a, count)
    input_grad = input_gradient(place, dh, grads, own_a, near_a, far_a)
    step_value = step_count[0].astype(F32)
    scalars = jnp.stack(
        [
            adam_rates[0],
            adam_rates[1],
            1.0 / (1.0 - beta_one**step_value),
            1.0 / (1.0 - beta_two**step_value),
        ]
    )
    ffn_new = adam_ffn(place, scalars, mine_b, other_b, ffn_master, ffn_mean, ffn_square)
    attn_new = adam_attn(
        place,
        scalars,
        mine_a,
        other_a,
        mine_b,
        other_b,
        attn_master,
        attn_mean,
        attn_square,
        (small_master, small_mean, small_square),
    )
    return (layer_out, input_grad) + tuple(attn_new[:4]) + tuple(ffn_new) + tuple(attn_new[4:])


def solution(mesh):
    tokens_in = P(("dp", "shard"), None)
    rows_in = P("shard", None)
    stack_in = P(None, "shard", None)
    cols_in = P(None, "shard")
    placed = (
        (tokens_in,) * 3
        + (P(("dp", "shard"), None, None, None), P(), P())
        + (rows_in,) * 3
        + (stack_in,) * 3
        + (cols_in,) * 3
    )
    return jax.shard_map(
        functools.partial(local, mesh.shape["dp"]),
        mesh=mesh,
        in_specs=placed,
        out_specs=(tokens_in,) * 2 + (rows_in,) * 4 + (stack_in,) * 4 + (cols_in,) * 4,
        check_vma=False,
    )
```

```python
import functools

import jax
import jax.numpy as jnp
from jax import lax
from jax.experimental import pallas as pl
from jax.experimental.pallas import tpu as pltpu
from jax.sharding import PartitionSpec as P

HD = 64
LANES = 128
BF = jnp.bfloat16
F32 = jnp.float32
BLOCKED = -(2.0**100)
NN = (((1,), (0,)), ((), ()))
NT = (((1,), (1,)), ((), ()))
TN = (((0,), (0,)), ((), ()))

norm_eps = 1e-12
beta_one = 0.9
beta_two = 0.999
adam_eps = 1e-08


def dotf(a, b, dims=NN):
    return lax.dot_general(a, b, dims, preferred_element_type=F32)


def params(mebibytes):
    return pltpu.CompilerParams(vmem_limit_bytes=mebibytes << 20)


def cost(flops, bytes_accessed, transcendentals=0, share=0.05):
    return pl.CostEstimate(
        flops=int(flops * share),
        bytes_accessed=int(bytes_accessed * share),
        transcendentals=int(transcendentals * share),
    )


def shape(dims, dtype):
    return jax.ShapeDtypeStruct(dims, dtype)


VM = pl.BlockSpec(memory_space=pltpu.VMEM)
SM = pl.BlockSpec(memory_space=pltpu.SMEM)


def token_marks(segments, blocks):
    length = segments.shape[1]
    row = lax.broadcasted_iota(jnp.int32, (LANES, length), 0)
    block_of = lax.broadcasted_iota(jnp.int32, (LANES, length), 1) // (length // blocks)
    marks = jnp.where((row == block_of) | (row == blocks + segments), 1.0, 0.0)
    return jnp.transpose(marks).astype(BF)


def head_table(picks, slots, blocks):
    row = lax.broadcasted_iota(jnp.int32, (LANES, LANES), 0)
    col = lax.broadcasted_iota(jnp.int32, (LANES, LANES), 1)
    seen = (jnp.abs(row - col) <= 1) | (row == 0) | (row == blocks - 1)
    seen = seen | (col == 0) | (col == blocks - 1)
    for slot in range(slots):
        seen = seen | (row == picks[slot : slot + 1, :])
    bad_block = (row < blocks) & (col < blocks) & ~seen
    bad_segment = (row >= blocks) & (col >= blocks) & (row != col)
    return jnp.where(bad_block | bad_segment, BLOCKED, 0.0).astype(BF)


def grouped_a(attn):
    feat = attn.shape[1] // 4
    return [
        attn[:, kind * feat + at : kind * feat + at + LANES]
        for at in range(0, feat, LANES)
        for kind in range(3)
    ]


def turned_small(small):
    fill = jnp.zeros((LANES - small.shape[0], small.shape[1]), F32)
    return jnp.transpose(jnp.concatenate([small, fill], axis=0))


def packed_b(attn_ref, ffn_ref, first):
    return jnp.concatenate([ffn_ref[0], ffn_ref[1], attn_ref[:, first:]], axis=1).astype(BF)


def pack_a_kernel(place, attn_ref, small_ref, out_ref, small_scr):
    eighth = out_ref.shape[0]
    small_scr[...] = turned_small(small_ref[...])
    small = small_scr[pl.ds(pl.multiple_of(place[2] * eighth, eighth), eighth), :]
    out_ref[...] = jnp.concatenate(grouped_a(attn_ref[...]) + [small], axis=1).astype(BF)


def pack_b_kernel(place, attn_ref, ffn_ref, out_ref):
    out_ref[...] = packed_b(attn_ref, ffn_ref, 0)


def pack_own_kernel(attn_ref, ffn_ref, small_ref, a_ref, b_ref):
    parts = grouped_a(attn_ref[...]) + [turned_small(small_ref[...])]
    a_ref[...] = jnp.concatenate(parts, axis=1).astype(BF)
    b_ref[...] = packed_b(attn_ref, ffn_ref, attn_ref.shape[1] // 4 * 3)


def pack_eighth_a(place, attn, small):
    eighth = attn.shape[0] // 4
    width = attn.shape[1] // 4 * 3 + LANES
    return pl.pallas_call(
        pack_a_kernel,
        grid_spec=pltpu.PrefetchScalarGridSpec(
            num_scalar_prefetch=1,
            grid=(1,),
            in_specs=[
                pl.BlockSpec((eighth, attn.shape[1]), lambda i, place: (2 * place[1] + place[2], 0)),
                pl.BlockSpec((small.shape[0], 2 * eighth), lambda i, place: (0, place[1])),
            ],
            out_specs=pl.BlockSpec((eighth, width), lambda i, place: (0, 0)),
            scratch_shapes=[pltpu.VMEM((2 * eighth, LANES), F32)],
        ),
        out_shape=shape((eighth, width), BF),
        compiler_params=params(8),
        cost_estimate=cost(1e6, 2 << 20),
        name="pack_eighth_a",
    )(place, attn, small)


def pack_quarter_b(place, attn, ffn):
    quarter = attn.shape[0] // 2
    feat = attn.shape[1] // 4
    hidden_count = ffn.shape[2]
    width = 2 * hidden_count + feat
    return pl.pallas_call(
        pack_b_kernel,
        grid_spec=pltpu.PrefetchScalarGridSpec(
            num_scalar_prefetch=1,
            grid=(1,),
            in_specs=[
                pl.BlockSpec((quarter, feat), lambda i, place: (place[1], 3)),
                pl.BlockSpec((2, quarter, hidden_count), lambda i, place: (0, place[1], 0)),
            ],
            out_specs=pl.BlockSpec((quarter, width), lambda i, place: (0, 0)),
        ),
        out_shape=shape((quarter, width), BF),
        compiler_params=params(12),
        cost_estimate=cost(1e6, 4 << 20),
        name="pack_quarter_b",
    )(place, attn, ffn)


def pack_own(attn, ffn, small):
    rows = attn.shape[0]
    step = rows // 2
    width_a = attn.shape[1] // 4 * 3 + LANES
    width_b = 2 * ffn.shape[2] + attn.shape[1] // 4
    return pl.pallas_call(
        pack_own_kernel,
        grid=(2,),
        in_specs=[
            pl.BlockSpec((step, attn.shape[1]), lambda i: (i, 0)),
            pl.BlockSpec((2, step, ffn.shape[2]), lambda i: (0, i, 0)),
            pl.BlockSpec((small.shape[0], step), lambda i: (0, i)),
        ],
        out_specs=[
            pl.BlockSpec((step, width_a), lambda i: (i, 0)),
            pl.BlockSpec((step, width_b), lambda i: (i, 0)),
        ],
        out_shape=[shape((rows, width_a), BF), shape((rows, width_b), BF)],
        compiler_params=params(16),
        cost_estimate=cost(1e6, 10 << 20),
        name="pack_own",
    )(attn, ffn, small)


def gathered_eighths(place, own_ref, near_ref, side_ref, far_ref, into, sems):
    half = own_ref.shape[0]
    eighth = near_ref.shape[0]
    shard, core, low = place[0], place[1], place[2]
    other = (1 - shard) * half
    copies = []
    for number, (ref, start, count) in enumerate(
        (
            (own_ref, shard * half, half),
            (near_ref, other + (2 * core + low) * eighth, eighth),
            (side_ref, other + (2 * core + 1 - low) * eighth, eighth),
            (far_ref.at[:eighth], other + (2 * (1 - core) + low) * eighth, eighth),
            (far_ref.at[eighth:], other + (2 * (1 - core) + 1 - low) * eighth, eighth),
        )
    ):
        rows = pl.ds(pl.multiple_of(start, eighth), count)
        copies.append(pltpu.make_async_copy(ref, into.at[rows, :], sems.at[number]))
    return copies


def gathered_rows(place, own_ref, near_ref, far_ref, into, sems, cols=slice(None), first=0):
    half = own_ref.shape[0]
    quarter = near_ref.shape[0]
    shard = place[0]
    core = place[1]
    other = (1 - shard) * half
    copies = []
    for number, (ref, start, count) in enumerate(
        (
            (own_ref, shard * half, half),
            (near_ref, other + core * quarter, quarter),
            (far_ref, other + (1 - core) * quarter, quarter),
        )
    ):
        rows = pl.ds(pl.multiple_of(start, quarter), count)
        copies.append(
            pltpu.make_async_copy(ref.at[:, cols], into.at[rows, cols], sems.at[first + number])
        )
    return copies


def attend_kernel(
    place,
    tok_ref,
    own_ref,
    near_ref,
    side_ref,
    far_ref,
    seg_ref,
    picks_ref,
    q_ref,
    k_ref,
    v_ref,
    o_ref,
    lse_ref,
    rows_ref,
    tok_t_ref,
    marks_ref,
    table_ref,
    w_scr,
    lse_scr,
    even,
    odd,
    sems,
    *,
    tile,
    slots,
    blocks,
):
    length = q_ref.shape[0]
    pair = pl.program_id(0)
    lane = lax.broadcasted_iota(jnp.int32, (1, LANES), 1)
    zero = jnp.zeros((), BF)

    @pl.when(pair == 0)
    def _():
        copies = gathered_eighths(place, own_ref, near_ref, side_ref, far_ref, w_scr, sems)
        for copy in copies:
            copy.start()
        tok_t_ref[...] = piece_order(tok_ref, place[1])
        lse_scr[...] = jnp.zeros_like(lse_scr)
        marks_ref[...] = token_marks(seg_ref[...], blocks)
        for copy in copies:
            copy.wait()
        small = w_scr[:, w_scr.shape[1] - LANES :].astype(F32)
        rows_ref[...] = jnp.transpose(small)[: rows_ref.shape[0], :]

    cols = pl.ds(pl.multiple_of(pair * 3 * LANES, LANES), 3 * LANES)
    here = pl.ds(pl.multiple_of(pair * LANES, LANES), LANES)
    bias = jnp.concatenate(
        [rows_ref[6:7, here], jnp.zeros((1, LANES), F32), rows_ref[7:8, here]], axis=1
    )
    qkv = (dotf(tok_ref[...], w_scr[:, cols]) + bias).astype(BF)
    q_ref[...] = qkv[:, :LANES]
    k_ref[...] = qkv[:, LANES : 2 * LANES]
    v_ref[...] = qkv[:, 2 * LANES :]
    keys, values = [], []
    for head in range(2):
        table_ref[head] = head_table(picks_ref[head], slots, blocks)
        key_marks = dotf(marks_ref[...], table_ref[head]).astype(BF)
        keys.append(jnp.concatenate([k_ref[...], key_marks], axis=1))
        values.append(jnp.where(lane // HD == head, v_ref[...], zero))
    steps = [(at, head) for at in range(0, length, tile) for head in range(2)]
    held = [even, odd]

    def score(index):
        at, head = steps[index]
        rows = pl.ds(at, tile)
        query = jnp.where(lane // HD == head, q_ref[rows, :] * jnp.asarray(HD**-0.5, BF), zero)
        return dotf(jnp.concatenate([query, marks_ref[rows, :]], axis=1), keys[head], NT)

    held[0][...] = score(0)
    first = None
    for index, (at, head) in enumerate(steps):
        rows = pl.ds(at, tile)
        if index + 1 < len(steps):
            held[(index + 1) % 2][...] = score(index + 1)
        now = held[index % 2]
        top = jnp.max(now[...], axis=1, keepdims=True)
        raised = jnp.exp(now[...] - top)
        total = jnp.sum(raised, axis=1, keepdims=True)
        mixed = dotf(raised.astype(BF), values[head]) * (1.0 / total)
        if head == 0:
            first = mixed
        else:
            o_ref[rows, :] = (first + mixed).astype(BF)
        lse_scr[rows, :] = jnp.where(
            lane == 2 * pair + head, top + jnp.log(total), lse_scr[rows, :]
        )

    @pl.when(pair == pl.num_programs(0) - 1)
    def _():
        lse_ref[...] = jnp.transpose(lse_scr[...])[: lse_ref.shape[0], :]


def attend(place, tokens, own, near, side, far, segments, random_blocks):
    length, model = tokens.shape
    blocks, heads, slots = random_blocks.shape[1:]
    picks = jnp.pad(
        random_blocks[0].transpose(1, 2, 0),
        ((0, 0), (0, 8 - slots), (0, LANES - blocks)),
        constant_values=-1,
    )
    width = own.shape[1]
    pairs = (width - LANES) // (3 * LANES)
    tile = 256
    whole = lambda dims: pl.BlockSpec(dims, lambda i: (0,) * len(dims))
    anywhere = pl.BlockSpec(memory_space=pl.ANY)
    block = pl.BlockSpec((length, LANES), lambda i: (0, i))
    out_rows = 16
    return pl.pallas_call(
        functools.partial(attend_kernel, tile=tile, slots=slots, blocks=blocks),
        grid=(pairs,),
        in_specs=[
            SM,
            whole((length, model)),
            anywhere,
            anywhere,
            anywhere,
            anywhere,
            whole((1, length)),
            pl.BlockSpec((2, 8, LANES), lambda i: (i, 0, 0)),
        ],
        out_specs=[
            block,
            block,
            block,
            block,
            whole((out_rows, length)),
            whole((out_rows, model)),
            whole((model, length)),
            whole((length, LANES)),
            pl.BlockSpec((2, LANES, LANES), lambda i: (i, 0, 0)),
        ],
        out_shape=[shape((length, pairs * LANES), BF)] * 4
        + [
            shape((out_rows, length), F32),
            shape((out_rows, model), F32),
            shape((model, length), BF),
            shape((length, LANES), BF),
            shape((heads, LANES, LANES), BF),
        ],
        scratch_shapes=[
            pltpu.VMEM((model, width), BF),
            pltpu.VMEM((length, LANES), F32),
            pltpu.VMEM((tile, length), F32),
            pltpu.VMEM((tile, length), F32),
            pltpu.SemaphoreType.DMA((5,)),
        ],
        compiler_params=params(56),
        cost_estimate=cost(18e9, 12 << 20, 8 << 20),
        name="attend",
    )(place, tokens, own, near, side, far, segments, picks)


def attend_back_kernel(
    place,
    q_ref,
    k_ref,
    v_ref,
    do_ref,
    o_ref,
    marks_ref,
    table_ref,
    lse_ref,
    tok_t_ref,
    mid_ref,
    keep_ref,
    send_ref,
    d_ref,
    dv_sum,
    dk_sum,
    bias_scr,
    *,
    tile,
):
    length = q_ref.shape[0]
    pair = pl.program_id(0)
    core = place[1]
    lane = lax.broadcasted_iota(jnp.int32, (1, LANES), 1)
    zero = jnp.zeros((), BF)
    scale = jnp.asarray(HD**-0.5, BF)
    prod = do_ref[...].astype(F32) * o_ref[...].astype(F32)
    high = prod.astype(BF)
    low = (prod - high.astype(F32)).astype(BF)
    pick = (
        lax.broadcasted_iota(jnp.int32, (8, LANES), 0)
        == lax.broadcasted_iota(jnp.int32, (8, LANES), 1) // HD
    ).astype(BF)
    inner = dotf(pick, high, NT) + dotf(pick, low, NT)
    for head in range(2):
        mine = lane // HD == head
        key_marks = dotf(marks_ref[...], table_ref[head]).astype(BF)
        keys = jnp.concatenate([k_ref[...], key_marks], axis=1)
        keys_scaled = jnp.where(mine, k_ref[...] * scale, zero)
        log_total = lse_ref[pl.ds(2 * pair + head, 1), :]
        for at in range(0, length, tile):
            here = pl.ds(at, tile)
            query = jnp.where(mine, q_ref[here, :] * scale, zero)
            upstream = jnp.where(mine, do_ref[here, :], zero)
            scores = dotf(keys, jnp.concatenate([query, marks_ref[here, :]], axis=1), NT)
            probs = jnp.exp(scores - log_total[:, at : at + tile])
            grad_probs = dotf(v_ref[...], upstream, NT)
            grad_scores = (probs * (grad_probs - inner[head : head + 1, at : at + tile])).astype(BF)
            grad_v = dotf(probs.astype(BF), upstream)
            grad_k = dotf(grad_scores, query)
            grad_q = dotf(grad_scores, keys_scaled, TN)
            if head == 0 and at == 0:
                dv_sum[...] = grad_v
                dk_sum[...] = grad_k
            else:
                dv_sum[...] += grad_v
                dk_sum[...] += grad_k
            if head == 0:
                d_ref[here, :LANES] = grad_q.astype(BF)
            else:
                d_ref[here, :LANES] = jnp.where(mine, grad_q.astype(BF), d_ref[here, :LANES])
    d_ref[:, LANES : 2 * LANES] = dk_sum[...].astype(BF)
    d_ref[:, 2 * LANES :] = dv_sum[...].astype(BF)
    outs = (keep_ref, send_ref)
    width = 3 * LANES
    result = dotf(tok_t_ref[...], d_ref[...]).astype(BF)
    store_pieces(result, core, outs, pl.ds(pl.multiple_of(pair * width, LANES), width))
    here = pl.ds(pl.multiple_of(pair * LANES, LANES), LANES)
    bias_scr[0:1, here] = col_sum(d_ref[:, :LANES].astype(F32))
    bias_scr[1:2, here] = col_sum(d_ref[:, 2 * LANES :].astype(F32))

    @pl.when(pair == pl.num_programs(0) - 1)
    def _():
        model = mid_ref.shape[1]
        sums = jnp.concatenate(
            [
                mid_ref[0:6, :],
                bias_scr[0:2, :],
                mid_ref[8:16, :],
                jnp.zeros((LANES - 16, model), F32),
            ],
            axis=0,
        )
        quarter = model // 4
        turned = jnp.transpose(sums)
        kept, sent = [], []
        for r0 in range(2):
            lower = turned[r0 * 2 * quarter : r0 * 2 * quarter + quarter]
            upper = turned[r0 * 2 * quarter + quarter : (r0 + 1) * 2 * quarter]
            kept.append(jnp.where(core == 0, lower, upper))
            sent.append(jnp.where(core == 0, upper, lower))
        total = keep_ref.shape[1]
        store_pieces(
            jnp.concatenate(kept + sent, axis=0).astype(BF), core, outs, slice(total - LANES, total)
        )


def attend_back(place, q, k, v, grad_mixed, mixed, marks, table, lse, tok_t, sums):
    length = q.shape[0]
    model = tok_t.shape[0]
    pairs = q.shape[1] // LANES
    width = 3 * LANES
    total = pairs * width + LANES
    whole = lambda dims: pl.BlockSpec(dims, lambda i: (0,) * len(dims))
    block = pl.BlockSpec((length, LANES), lambda i: (0, i))
    return pl.pallas_call(
        functools.partial(attend_back_kernel, tile=512),
        grid=(pairs,),
        in_specs=[SM]
        + [block] * 5
        + [whole(marks.shape), pl.BlockSpec((2, LANES, LANES), lambda i: (i, 0, 0))]
        + [whole(lse.shape), whole(tok_t.shape), whole(sums.shape)],
        out_specs=[
            whole((model // 2, total)),
            whole((model // 2, total)),
            pl.BlockSpec((length, width), lambda i: (0, i)),
        ],
        out_shape=[
            shape((model // 2, total), BF),
            shape((model // 2, total), BF),
            shape((length, pairs * width), BF),
        ],
        scratch_shapes=[
            pltpu.VMEM((length, LANES), F32),
            pltpu.VMEM((length, LANES), F32),
            pltpu.VMEM((8, model), F32),
        ],
        compiler_params=params(56),
        cost_estimate=cost(30e9, 10 << 20, 8 << 20, 1.0),
        name="attend_back",
    )(place, q, k, v, grad_mixed, mixed, marks, table, lse, tok_t, sums)


def piece_order(lhs_ref, core):
    quarter = lhs_ref.shape[1] // 4
    cols = []
    for target in (core, 1 - core):
        for half in range(2):
            start = pl.multiple_of(half * 2 * quarter + target * quarter, quarter)
            cols.append(lhs_ref[:, pl.ds(start, quarter)])
    return jnp.transpose(jnp.concatenate(cols, axis=1))


def store_pieces(result, core, outs, cols):
    quarter = result.shape[0] // 4
    piece = quarter // 4
    for which, target in enumerate((core, 1 - core)):
        for r0 in range(2):
            for r2 in range(2):
                for r3 in range(2):
                    at = which * 2 * quarter + r0 * quarter + r2 * 2 * piece + r3 * piece
                    spot = jnp.where(target == 0, r0 * 4 + r2 * 2 + r3, r3 * 4 + r2 * 2 + r0)
                    rows = pl.ds(pl.multiple_of(spot * piece, piece), piece)
                    outs[which][rows, cols] = result[at : at + piece, :]


def weight_grad(lhs_t, rhs_ref, core, outs, first, tile=512):
    for at in range(0, rhs_ref.shape[1], tile):
        result = dotf(lhs_t, rhs_ref[:, at : at + tile]).astype(BF)
        store_pieces(result, core, outs, slice(first + at, first + at + tile))


def normed(hidden):
    center = hidden - jnp.mean(hidden, axis=-1, keepdims=True)
    spread = jnp.mean(center * center, axis=-1, keepdims=True)
    rate = lax.rsqrt(spread + norm_eps)
    return center * rate, rate


def norm_back(grad, unit, rate):
    return rate * (
        grad
        - jnp.mean(grad, axis=-1, keepdims=True)
        - unit * jnp.mean(grad * unit, axis=-1, keepdims=True)
    )


def col_sum(values):
    return jnp.sum(values, axis=0, keepdims=True)


def middle_kernel(
    place,
    rows_ref,
    tok_hbm,
    cot_hbm,
    mixed_hbm,
    own_hbm,
    near_hbm,
    far_hbm,
    out_hbm,
    dh_hbm,
    do_hbm,
    keep_hbm,
    send_hbm,
    sums_ref,
    tok_ref,
    cot_ref,
    mixed_ref,
    out_ref,
    dh_ref,
    do_ref,
    keep_ref,
    send_ref,
    w_scr,
    act_scr,
    du_scr,
    z_scr,
    df_scr,
    da_scr,
    sems,
    out_sems,
    *,
    tile,
):
    length, model = tok_ref.shape
    core = place[1]
    hidden_count = act_scr.shape[1]
    w_up = slice(0, hidden_count)
    w_down = slice(hidden_count, 2 * hidden_count)
    w_out = slice(2 * hidden_count, w_scr.shape[1])
    waits = {}
    number = 0
    for name, sources in (
        ("out", w_out),
        ("mixed", ((mixed_hbm, mixed_ref), (tok_hbm, tok_ref))),
        ("up", w_up),
        ("down", w_down),
        ("cot", ((cot_hbm, cot_ref),)),
    ):
        if isinstance(sources, slice):
            copies = gathered_rows(
                place, own_hbm, near_hbm, far_hbm, w_scr, sems, sources, number
            )
        else:
            copies = [
                pltpu.make_async_copy(source, into, sems.at[number + n])
                for n, (source, into) in enumerate(sources)
            ]
        number += len(copies)
        for copy in copies:
            copy.start()
        waits[name] = copies

    def ready(name):
        for copy in waits.pop(name, ()):
            copy.wait()

    pending = []

    def write_out(source, into):
        copy = pltpu.make_async_copy(source, into, out_sems.at[len(pending)])
        copy.start()
        pending.append(copy)

    row = lambda number: rows_ref[number : number + 1, :]
    bias_up = jnp.concatenate([row(8), row(9), row(10), row(11)], axis=1)
    sums = [jnp.zeros((1, model), F32)] * 6
    sum_up = jnp.zeros((1, hidden_count), F32)
    for at in range(0, length, tile):
        here = pl.ds(at, tile)
        ready("out")
        ready("mixed")
        attn_out = dotf(mixed_ref[here, :], w_scr[:, w_out], NT) + row(4)
        unit_one, rate_one = normed(tok_ref[here, :].astype(F32) + attn_out)
        z_one = unit_one * row(0) + row(1)
        z_low = z_one.astype(BF)
        z_scr[here, :] = z_low
        ready("up")
        up = dotf(z_low, w_scr[:, w_up]) + bias_up
        below = 0.5 * (1.0 + lax.erf(up * (0.5**0.5)))
        slope = below + up * (jnp.exp(-0.5 * up * up) * (1.0 / (2.0 * 3.141592653589793) ** 0.5))
        active = (up * below).astype(BF)
        act_scr[here, :] = active
        ready("down")
        ffn_out = dotf(active, w_scr[:, w_down], NT) + row(5)
        unit_two, rate_two = normed(z_one + ffn_out)
        out_ref[here, :] = (unit_two * row(2) + row(3)).astype(BF)
        ready("cot")
        upstream = cot_ref[here, :].astype(F32)
        grad_two = norm_back(upstream * row(2), unit_two, rate_two)
        down_low = grad_two.astype(BF)
        df_scr[here, :] = down_low
        grad_up = (dotf(down_low, w_scr[:, w_down]) * slope).astype(BF)
        du_scr[here, :] = grad_up
        grad_z = grad_two + dotf(grad_up, w_scr[:, w_up], NT)
        grad_one = norm_back(grad_z * row(0), unit_one, rate_one)
        dh_ref[here, :] = grad_one
        attn_low = grad_one.astype(BF)
        da_scr[here, :] = attn_low
        do_ref[here, :] = dotf(attn_low, w_scr[:, w_out]).astype(BF)
        for source, into in ((out_ref, out_hbm), (dh_ref, dh_hbm), (do_ref, do_hbm)):
            write_out(source.at[here, :], into.at[here, :])
        parts = (
            grad_z * unit_one,
            grad_z,
            upstream * unit_two,
            upstream,
            attn_low.astype(F32),
            down_low.astype(F32),
        )
        sums = [a + col_sum(b) for a, b in zip(sums, parts)]
        sum_up = sum_up + col_sum(grad_up.astype(F32))
    for number in range(6):
        sums_ref[number : number + 1, :] = sums[number]
    sums_ref[6:8, :] = jnp.zeros((2, model), F32)
    for number in range(4):
        sums_ref[8 + number : 9 + number, :] = sum_up[:, number * model : (number + 1) * model]
    sums_ref[12:16, :] = jnp.zeros((4, model), F32)
    outs = (keep_ref, send_ref)
    for lhs, rhs, cols in (
        (z_scr, du_scr, w_up),
        (df_scr, act_scr, w_down),
        (da_scr, mixed_ref, w_out),
    ):
        weight_grad(piece_order(lhs, core), rhs, core, outs, cols.start)
        for source, into in ((send_ref, send_hbm), (keep_ref, keep_hbm)):
            write_out(source.at[:, cols], into.at[:, cols])
    for copy in pending:
        copy.wait()


def middle(place, tokens, cotangent, mixed, rows, own, near, far):
    length, model = tokens.shape
    width = own.shape[1]
    hidden_count = (width - mixed.shape[1]) // 2
    tile = 256
    anywhere = pl.BlockSpec(memory_space=pl.ANY)
    outs = [
        shape((length, model), BF),
        shape((length, model), F32),
        shape((length, mixed.shape[1]), BF),
        shape((model // 2, width), BF),
        shape((model // 2, width), BF),
    ]
    vmem = lambda x: pltpu.VMEM(x.shape, x.dtype)
    return pl.pallas_call(
        functools.partial(middle_kernel, tile=tile),
        in_specs=[SM, VM] + [anywhere] * 6,
        out_specs=[anywhere] * 5 + [VM],
        out_shape=outs + [shape((16, model), F32)],
        scratch_shapes=[vmem(x) for x in (tokens, cotangent, mixed, *outs)]
        + [
            pltpu.VMEM((model, width), BF),
            pltpu.VMEM((length, hidden_count), BF),
            pltpu.VMEM((length, hidden_count), BF),
            pltpu.VMEM((length, model), BF),
            pltpu.VMEM((length, model), BF),
            pltpu.VMEM((length, model), BF),
            pltpu.SemaphoreType.DMA((12,)),
            pltpu.SemaphoreType.DMA((3 * (length // tile) + 6,)),
        ],
        compiler_params=params(44),
        cost_estimate=cost(16e9, 16 << 20, 4 << 20, 1.0),
        name="middle",
    )(place, rows, tokens, cotangent, mixed, own, near, far)


def input_grad_kernel(
    place, dh_ref, d_ref, own_ref, near_ref, side_ref, far_ref, out_ref, w_scr, sems
):
    width = d_ref.shape[1]

    @pl.when(pl.program_id(0) == 0)
    def _():
        copies = gathered_eighths(place, own_ref, near_ref, side_ref, far_ref, w_scr, sems)
        for copy in copies:
            copy.start()
        for copy in copies:
            copy.wait()

    out_ref[...] = (dh_ref[...] + dotf(d_ref[...], w_scr[:, :width], NT)).astype(BF)


def input_gradient(place, dh, d, own, near, side, far):
    length, model = dh.shape
    tile = 256
    anywhere = pl.BlockSpec(memory_space=pl.ANY)
    rows = lambda width: pl.BlockSpec((tile, width), lambda i: (i, 0))
    return pl.pallas_call(
        input_grad_kernel,
        grid=(length // tile,),
        in_specs=[SM, rows(model), rows(d.shape[1])] + [anywhere] * 4,
        out_specs=rows(model),
        out_shape=shape((length, model), BF),
        scratch_shapes=[pltpu.VMEM((model, own.shape[1]), BF), pltpu.SemaphoreType.DMA((5,))],
        compiler_params=params(16),
        cost_estimate=cost(2 * length * model * d.shape[1], 8 << 20),
        name="input_gradient",
    )(place, dh, d, own, near, side, far)


def add_low(a, b):
    return (a.astype(F32) + b.astype(F32)).astype(BF)


def add_parts_kernel(place, *refs):
    total = refs[0][...].astype(F32)
    for ref in refs[1:-1]:
        total = total + ref[...].astype(F32)
    refs[-1][...] = total.astype(BF)


def add_parts(place, parts, give):
    rows = min(part.shape[0] for part in parts)
    rows = rows // 2 if give else rows
    width = parts[0].shape[1]

    def pick(part):
        if part.shape[0] == rows:
            return pl.BlockSpec((rows, width), lambda i, place: (0, 0))
        return pl.BlockSpec((rows, width), lambda i, place: (1 - place[6] if give else place[6], 0))

    return pl.pallas_call(
        add_parts_kernel,
        grid_spec=pltpu.PrefetchScalarGridSpec(
            num_scalar_prefetch=1,
            grid=(1,),
            in_specs=[pick(part) for part in parts],
            out_specs=pl.BlockSpec((rows, width), lambda i, place: (0, 0)),
        ),
        out_shape=shape((rows, width), BF),
        compiler_params=params(8),
        cost_estimate=cost(len(parts) * rows * width, 2 * len(parts) * rows * width),
        name="add_parts",
    )(place, *parts)


def flip(count, bit):
    return [(i, i ^ (1 << bit)) for i in range(count)]


def mixed_flip(count, even, odd):
    return [(i, i ^ (1 << (odd if (i >> 1) & 1 else even))) for i in range(2 * count)]


STEPS = ((0, 2), (2, 3), (3, 0))


def mixed_mask(count, mask):
    pairs = []
    for i in range(2 * count):
        partner = i
        for bit, step in zip((2, 1), STEPS):
            if mask & bit:
                partner ^= 1 << step[(i >> 1) & 1]
        pairs.append((i, partner))
    return pairs


def split_kernel(place, keep_ref, got_ref, *outs):
    piece = outs[0].shape[0]
    mine = place[3] * 2 + place[4]
    for mask, out in enumerate(outs):
        rows = pl.ds(pl.multiple_of((mine ^ mask) * piece, piece), piece)
        out[...] = add_low(keep_ref[rows, :], got_ref[rows, :])


def swap_two(value, count, mask):
    return lax.ppermute(value, ("dp", "shard"), mixed_mask(count, mask))


def split(place, keep, got):
    rows, width = keep.shape
    steps = 4 if width % (4 * LANES) == 0 else 1
    step = width // steps
    whole = pl.BlockSpec((rows, step), lambda i: (0, i))
    part = pl.BlockSpec((rows // 4, step), lambda i: (0, i))
    return pl.pallas_call(
        split_kernel,
        grid=(steps,),
        in_specs=[SM, whole, whole],
        out_specs=[part] * 4,
        out_shape=[shape((rows // 4, width), BF)] * 4,
        compiler_params=params(16),
        cost_estimate=cost(rows * width, 6 * rows * width),
        name="split",
    )(place, keep, got)


def swap_core(value, count):
    return lax.ppermute(value, "dp", flip(count, 0))


def swap_mixed(value, count, step):
    return lax.ppermute(value, ("dp", "shard"), mixed_flip(count, *step))


def swap_pieces(value, count):
    both = [(i, i ^ 12) for i in range(2 * count)]
    return [
        swap_mixed(value, count, (3, 2)),
        swap_mixed(value, count, (2, 3)),
        lax.ppermute(value, ("dp", "shard"), both),
    ]


def swap_bit(value, count, bit):
    return lax.ppermute(value, "dp", flip(count, bit))


def after(value, *others):
    return lax.optimization_barrier((value,) + others)[0]


def adam_values(scalars, weight_ref, mean_ref, square_ref, grad, decay, outs):
    weight = weight_ref[...]
    mean_out = beta_one * mean_ref[...] + (1.0 - beta_one) * grad
    square_out = beta_two * square_ref[...] + (1.0 - beta_two) * grad * grad
    mean_hat = mean_out * scalars[2]
    square_hat = square_out * scalars[3]
    weight_out = weight - scalars[0] * (
        mean_hat / (jnp.sqrt(square_hat) + adam_eps) + decay * weight
    )
    outs[0][...] = weight_out
    outs[1][...] = mean_out
    outs[2][...] = square_out
    outs[3][...] = weight_out.astype(BF)


def ordered_rows(place, refs, own):
    bit2, bit3 = (place[4], place[5]) if own else (place[5], place[4])
    upper = (pl.program_id(0) ^ bit2) == 1
    near, far = [
        jnp.where(upper, refs[2 + n][...].astype(F32), refs[n][...].astype(F32)) for n in range(2)
    ]
    swapped = bit3 == 1
    return jnp.concatenate([jnp.where(swapped, far, near), jnp.where(swapped, near, far)], axis=0)


def adam_ffn_kernel(place, scalars, *rest, own):
    grad = ordered_rows(place, rest[:4], own)[None]
    w_ref, m_ref, s_ref = rest[4:7]
    adam_values(scalars, w_ref, m_ref, s_ref, grad, scalars[1], rest[-4:])


def adam_attn_kernel(place, scalars, *rest, own):
    grad = ordered_rows(place, rest[:4], own)
    out_grad = ordered_rows(place, rest[4:8], own)
    w_ref, m_ref, s_ref = rest[8:11]
    rest = rest[11:]
    pairs = grad.shape[1] // (3 * LANES)
    parts = [
        grad[:, p * 3 * LANES + kind * LANES : p * 3 * LANES + (kind + 1) * LANES]
        for kind in range(3)
        for p in range(pairs)
    ]
    whole = jnp.concatenate(parts + [out_grad], axis=1)
    small_grad = grad[:, pairs * 3 * LANES :]
    if own:
        outs, small_out = rest[:4], rest[4]
        small_out[...] = small_grad
    else:
        mine_ref, sw, sm, ss = rest[:4]
        outs, small_outs, scr = rest[8:12], rest[12:16], rest[16]
        count = small_grad.shape[0]
        r2 = pl.program_id(0)
        here = pl.ds(pl.multiple_of(((1 - place[1]) * 2 + r2) * count, count), count)
        scr[here, :] = small_grad

        @pl.when(r2 == 0)
        def _():
            rows = mine_ref.shape[0]
            scr[pl.ds(pl.multiple_of(place[1] * rows, rows), rows), :] = mine_ref[...]

        @pl.when(r2 == 1)
        def _():
            turned = jnp.transpose(scr[...])[: sw.shape[0], :]
            adam_values(scalars, sw, sm, ss, turned, 0.0 * scalars[1], small_outs)

    adam_values(scalars, w_ref, m_ref, s_ref, whole, scalars[1], outs)


def half_number(place, own):
    return place[1] if own else 1 - place[1]


def grad_blocks(rows, width, column):
    return [pl.BlockSpec((rows, width), lambda r, place, sc: (0, column))] * 4


def adam_ffn(place, scalars, grad, own, which, state, before):
    stack, rows, width = state[0].shape
    count = rows // 4
    block = pl.BlockSpec(
        (1, count, width), lambda r, place, sc: (which, 2 * half_number(place, own) + r, 0)
    )
    anywhere = pl.BlockSpec(memory_space=pl.ANY)
    before = list(before or ())
    return pl.pallas_call(
        functools.partial(adam_ffn_kernel, own=own),
        grid_spec=pltpu.PrefetchScalarGridSpec(
            num_scalar_prefetch=2,
            grid=(2,),
            in_specs=grad_blocks(count // 2, width, which) + [block] * 3 + [anywhere] * len(before),
            out_specs=[block] * 4,
        ),
        out_shape=[shape(state[0].shape, F32)] * 3 + [shape(state[0].shape, BF)],
        input_output_aliases={9 + n: n for n in range(len(before))},
        compiler_params=params(24),
        cost_estimate=cost(10 * rows * width, 14 * rows * width),
        name=f"adam_ffn_{which}_{int(own)}",
    )(place, scalars, *grad, *state, *before)


def adam_attn(place, scalars, grad, grad_b, own, state, mine_small, small, before):
    rows, width = state[0].shape
    count = rows // 4
    out_width = width // 4
    block = pl.BlockSpec((count, width), lambda r, place, sc: (2 * half_number(place, own) + r, 0))
    anywhere = pl.BlockSpec(memory_space=pl.ANY)
    last = (grad_b[0].shape[1] - out_width) // out_width
    in_specs = grad_blocks(count // 2, grad[0].shape[1], 0)
    in_specs += grad_blocks(count // 2, out_width, last) + [block] * 3
    out_specs = [block] * 4
    out_shape = [shape(state[0].shape, F32)] * 3 + [shape(state[0].shape, BF)]
    operands = [place, scalars, *grad, *grad_b, *state]
    aliases, scratch = {}, []
    if own:
        out_specs += [pl.BlockSpec((count, LANES), lambda r, place, sc: (r, 0))]
        out_shape += [shape((2 * count, LANES), F32)]
    else:
        whole = lambda dims: pl.BlockSpec(dims, lambda r, place, sc: (0, 0))
        operands += [mine_small, *small]
        in_specs += [whole(mine_small.shape)] + [whole(small[0].shape)] * 3
        aliases = {len(operands) + n: n for n in range(4)}
        operands += list(before)
        in_specs += [anywhere] * 4
        out_specs += [whole(small[0].shape)] * 4
        out_shape += [shape(small[0].shape, F32)] * 3 + [shape(small[0].shape, BF)]
        scratch = [pltpu.VMEM((rows, LANES), F32)]
    return pl.pallas_call(
        functools.partial(adam_attn_kernel, own=own),
        grid_spec=pltpu.PrefetchScalarGridSpec(
            num_scalar_prefetch=2,
            grid=(2,),
            in_specs=in_specs,
            out_specs=out_specs,
            scratch_shapes=scratch,
        ),
        out_shape=out_shape,
        input_output_aliases=aliases,
        compiler_params=params(24),
        cost_estimate=cost(10 * rows * width, 14 * rows * width),
        name=f"adam_attn_{int(own)}",
    )(*operands)


def from_neighbour(value):
    return lax.ppermute(value, "shard", [(0, 1), (1, 0)])


def local(
    count,
    tokens,
    cotangent,
    segments,
    random_blocks,
    step_count,
    adam_rates,
    attn_master,
    attn_mean,
    attn_square,
    ffn_master,
    ffn_mean,
    ffn_square,
    small_master,
    small_mean,
    small_square,
):
    replica = lax.axis_index("dp")
    shard = lax.axis_index("shard")
    core, low, high = replica & 1, (replica >> 1) & 1, (replica >> 2) & 1
    even = core == 0
    place = jnp.stack(
        [
            shard,
            core,
            low,
            jnp.where(even, shard, low),
            jnp.where(even, low, high),
            jnp.where(even, high, low),
            jnp.where(even, high, shard),
        ]
    ).astype(jnp.int32)
    pairs = attn_master.shape[1] // 4 // LANES
    near_a = from_neighbour(pack_eighth_a(place, attn_master, small_master))
    quarter_b = pack_quarter_b(place, attn_master, ffn_master)
    near_a = after(near_a, quarter_b)
    near_b = from_neighbour(after(quarter_b, near_a))
    side_a = swap_bit(near_a, count, 1)
    own_a, own_b = pack_own(attn_master, ffn_master, small_master)
    far_a = swap_core(jnp.concatenate([near_a, after(side_a, own_a)]), count)
    q, k, v, mixed, lse, rows, tok_t, marks, table = attend(
        place, tokens, own_a, near_a, side_a, far_a, segments, random_blocks
    )
    far_b = swap_core(after(near_b, lse), count)
    layer_out, dh, grad_mixed, keep_b, send_b, sums = middle(
        place, tokens, cotangent, mixed, rows, own_b, near_b, far_b
    )
    parts_b = list(split(place, keep_b, swap_core(send_b, count)))
    parts_b = parts_b[:1] + [swap_two(parts_b[mask], count, mask) for mask in (1, 2, 3)]
    keep_a, send_a, d = attend_back(
        place, q, k, v, after(grad_mixed, parts_b[0]), mixed, marks, table, lse, tok_t, sums
    )
    got_a = swap_core(send_a, count)
    parts_b = parts_b[:1] + [after(part, d) for part in parts_b[1:]]
    got_b = swap_mixed(add_parts(place, parts_b, True), count, STEPS[2])

    step_value = step_count[0].astype(F32)
    scalars = jnp.stack(
        [
            adam_rates[0],
            adam_rates[1],
            1.0 / (1.0 - beta_one**step_value),
            1.0 / (1.0 - beta_two**step_value),
        ]
    )
    ffn_state = (ffn_master, ffn_mean, ffn_square)
    attn_state = (attn_master, attn_mean, attn_square)
    small_state = (small_master, small_mean, small_square)
    bits = [bit for bit in range(3, count.bit_length() - 1)]

    parts_a = list(split(place, keep_a, got_a))
    parts_a = parts_a[:1] + [swap_two(parts_a[mask], count, mask) for mask in (1, 2, 3)]
    total_b = add_parts(place, parts_b + [after(got_b, parts_a[0])], False)
    got_b = swap_bit(total_b, count, bits[0])
    input_grad = input_gradient(place, after(dh, total_b), d, own_a, near_a, side_a, far_a)
    parts_a = parts_a[:1] + [after(part, input_grad) for part in parts_a[1:]]
    got_a = swap_mixed(add_parts(place, parts_a, True), count, STEPS[2])
    total_a = add_parts(place, parts_a + [got_a], False)
    got_a = swap_bit(total_a, count, bits[0])
    total_b = add_low(total_b, after(got_b, total_a))
    for bit in bits[1:]:
        total_b = add_low(total_b, swap_bit(total_b, count, bit))
    mine_b = swap_pieces(total_b, count)
    total_a = add_low(total_a, after(got_a, total_b))
    for bit in bits[1:]:
        total_a = add_low(total_a, swap_bit(total_a, count, bit))
    mine_a = swap_pieces(total_a, count)
    mine_b = [total_b] + [after(piece, total_a) for piece in mine_b]
    other_b = [swap_core(piece, count) for piece in mine_b]
    ffn_new = adam_ffn(place, scalars, mine_b, True, 0, ffn_state, None)
    mine_a = [total_a] + [after(piece, ffn_new[0]) for piece in mine_a]
    other_a = [swap_core(piece, count) for piece in mine_a]
    ffn_new = adam_ffn(place, scalars, mine_b, True, 1, ffn_state, ffn_new)
    ffn_new = adam_ffn(place, scalars, other_b, False, 0, ffn_state, ffn_new)
    ffn_new = adam_ffn(place, scalars, other_b, False, 1, ffn_state, ffn_new)
    *attn_new, small_grad = adam_attn(
        place, scalars, mine_a, mine_b, True, attn_state, None, None, None
    )
    attn_new = adam_attn(
        place, scalars, other_a, other_b, False, attn_state, small_grad, small_state, attn_new
    )
    return (layer_out, input_grad) + tuple(attn_new[:4]) + tuple(ffn_new) + tuple(attn_new[4:])


def solution(mesh):
    tokens_in = P(("dp", "shard"), None)
    rows_in = P("shard", None)
    stack_in = P(None, "shard", None)
    cols_in = P(None, "shard")
    placed = (
        (tokens_in,) * 3
        + (P(("dp", "shard"), None, None, None), P(), P())
        + (rows_in,) * 3
        + (stack_in,) * 3
        + (cols_in,) * 3
    )
    return jax.shard_map(
        functools.partial(local, mesh.shape["dp"]),
        mesh=mesh,
        in_specs=placed,
        out_specs=(tokens_in,) * 2 + (rows_in,) * 4 + (stack_in,) * 4 + (cols_in,) * 4,
        check_vma=False,
    )
```

```python
import functools

import jax
import jax.numpy as jnp
from jax import lax
from jax.experimental import pallas as pl
from jax.experimental.pallas import tpu as pltpu
from jax.sharding import PartitionSpec as P

HD = 64
LANES = 128
BF = jnp.bfloat16
F32 = jnp.float32
BLOCKED = -(2.0**100)
NN = (((1,), (0,)), ((), ()))
NT = (((1,), (1,)), ((), ()))
TN = (((0,), (0,)), ((), ()))

norm_eps = 1e-12
beta_one = 0.9
beta_two = 0.999
adam_eps = 1e-08


def dotf(a, b, dims=NN):
    return lax.dot_general(a, b, dims, preferred_element_type=F32)


def params(mebibytes):
    return pltpu.CompilerParams(vmem_limit_bytes=mebibytes << 20)


def cost(flops, bytes_accessed, transcendentals=0, share=0.05):
    return pl.CostEstimate(
        flops=int(flops * share),
        bytes_accessed=int(bytes_accessed * share),
        transcendentals=int(transcendentals * share),
    )


def shape(dims, dtype):
    return jax.ShapeDtypeStruct(dims, dtype)


VM = pl.BlockSpec(memory_space=pltpu.VMEM)
SM = pl.BlockSpec(memory_space=pltpu.SMEM)


def token_marks(segments, blocks):
    length = segments.shape[1]
    row = lax.broadcasted_iota(jnp.int32, (LANES, length), 0)
    block_of = lax.broadcasted_iota(jnp.int32, (LANES, length), 1) // (length // blocks)
    marks = jnp.where((row == block_of) | (row == blocks + segments), 1.0, 0.0)
    return jnp.transpose(marks).astype(BF)


def head_table(picks, slots, blocks):
    row = lax.broadcasted_iota(jnp.int32, (LANES, LANES), 0)
    col = lax.broadcasted_iota(jnp.int32, (LANES, LANES), 1)
    seen = (jnp.abs(row - col) <= 1) | (row == 0) | (row == blocks - 1)
    seen = seen | (col == 0) | (col == blocks - 1)
    for slot in range(slots):
        seen = seen | (row == picks[slot : slot + 1, :])
    bad_block = (row < blocks) & (col < blocks) & ~seen
    bad_segment = (row >= blocks) & (col >= blocks) & (row != col)
    return jnp.where(bad_block | bad_segment, BLOCKED, 0.0).astype(BF)


def grouped_a(kinds):
    return [
        kind[:, at : at + LANES] for at in range(0, kinds[0].shape[1], LANES) for kind in kinds
    ]


def turned_small(small):
    fill = jnp.zeros((LANES - small.shape[0], small.shape[1]), F32)
    return jnp.transpose(jnp.concatenate([small, fill], axis=0))


def packed_b(attn_ref, ffn_ref, first):
    return jnp.concatenate([ffn_ref[0], ffn_ref[1], attn_ref[:, first:]], axis=1).astype(BF)


def pack_a_kernel(place, *refs):
    attn_refs, small_ref, out_ref, small_scr = refs[:3], *refs[3:]
    eighth = out_ref.shape[0]
    small_scr[...] = turned_small(small_ref[...])
    small = small_scr[pl.ds(pl.multiple_of(place[2] * eighth, eighth), eighth), :]
    out_ref[...] = jnp.concatenate(
        grouped_a([ref[...] for ref in attn_refs]) + [small], axis=1
    ).astype(BF)


def pack_b_kernel(place, attn_ref, ffn_ref, out_ref):
    out_ref[...] = packed_b(attn_ref, ffn_ref, 0)


def pack_own_kernel(attn_ref, ffn_ref, small_ref, a_ref, b_ref):
    feat = attn_ref.shape[1] // 4
    kinds = [attn_ref[:, kind * feat : (kind + 1) * feat] for kind in range(3)]
    parts = grouped_a(kinds) + [turned_small(small_ref[...])]
    a_ref[...] = jnp.concatenate(parts, axis=1).astype(BF)
    b_ref[...] = packed_b(attn_ref, ffn_ref, attn_ref.shape[1] // 4 * 3)


def pack_eighth_a(place, attn, small):
    eighth = attn.shape[0] // 4
    width = attn.shape[1] // 4 * 3 + LANES
    return pl.pallas_call(
        pack_a_kernel,
        grid_spec=pltpu.PrefetchScalarGridSpec(
            num_scalar_prefetch=1,
            grid=(1,),
            in_specs=[
                pl.BlockSpec(
                    (eighth, attn.shape[1] // 4),
                    lambda i, place, kind=kind: (2 * place[1] + place[2], kind),
                )
                for kind in range(3)
            ]
            + [
                pl.BlockSpec((small.shape[0], 2 * eighth), lambda i, place: (0, place[1])),
            ],
            out_specs=pl.BlockSpec((eighth, width), lambda i, place: (0, 0)),
            scratch_shapes=[pltpu.VMEM((2 * eighth, LANES), F32)],
        ),
        out_shape=shape((eighth, width), BF),
        compiler_params=params(58),
        cost_estimate=cost(1e6, 2 << 20),
        name="pack_eighth_a",
    )(place, attn, attn, attn, small)


def pack_quarter_b(place, attn, ffn):
    quarter = attn.shape[0] // 2
    feat = attn.shape[1] // 4
    hidden_count = ffn.shape[2]
    width = 2 * hidden_count + feat
    return pl.pallas_call(
        pack_b_kernel,
        grid_spec=pltpu.PrefetchScalarGridSpec(
            num_scalar_prefetch=1,
            grid=(1,),
            in_specs=[
                pl.BlockSpec((quarter, feat), lambda i, place: (place[1], 3)),
                pl.BlockSpec((2, quarter, hidden_count), lambda i, place: (0, place[1], 0)),
            ],
            out_specs=pl.BlockSpec((quarter, width), lambda i, place: (0, 0)),
        ),
        out_shape=shape((quarter, width), BF),
        compiler_params=params(12),
        cost_estimate=cost(1e6, 4 << 20),
        name="pack_quarter_b",
    )(place, attn, ffn)


def pack_own(attn, ffn, small):
    rows = attn.shape[0]
    step = rows // 2
    width_a = attn.shape[1] // 4 * 3 + LANES
    width_b = 2 * ffn.shape[2] + attn.shape[1] // 4
    return pl.pallas_call(
        pack_own_kernel,
        grid=(2,),
        in_specs=[
            pl.BlockSpec((step, attn.shape[1]), lambda i: (i, 0)),
            pl.BlockSpec((2, step, ffn.shape[2]), lambda i: (0, i, 0)),
            pl.BlockSpec((small.shape[0], step), lambda i: (0, i)),
        ],
        out_specs=[
            pl.BlockSpec((step, width_a), lambda i: (i, 0)),
            pl.BlockSpec((step, width_b), lambda i: (i, 0)),
        ],
        out_shape=[shape((rows, width_a), BF), shape((rows, width_b), BF)],
        compiler_params=params(16),
        cost_estimate=cost(1e6, 10 << 20),
        name="pack_own",
    )(attn, ffn, small)


def gathered_eighths(place, own_ref, near_ref, side_ref, far_ref, into, sems):
    half = own_ref.shape[0]
    eighth = near_ref.shape[0]
    shard, core, low = place[0], place[1], place[2]
    other = (1 - shard) * half
    copies = []
    for number, (ref, start, count) in enumerate(
        (
            (own_ref, shard * half, half),
            (near_ref, other + (2 * core + low) * eighth, eighth),
            (side_ref, other + (2 * core + 1 - low) * eighth, eighth),
            (far_ref.at[:eighth], other + (2 * (1 - core) + low) * eighth, eighth),
            (far_ref.at[eighth:], other + (2 * (1 - core) + 1 - low) * eighth, eighth),
        )
    ):
        rows = pl.ds(pl.multiple_of(start, eighth), count)
        copies.append(pltpu.make_async_copy(ref, into.at[rows, :], sems.at[number]))
    return copies


def gathered_rows(place, own_ref, near_ref, far_ref, into, sems, cols=slice(None), first=0):
    half = own_ref.shape[0]
    quarter = near_ref.shape[0]
    shard = place[0]
    core = place[1]
    other = (1 - shard) * half
    copies = []
    for number, (ref, start, count) in enumerate(
        (
            (own_ref, shard * half, half),
            (near_ref, other + core * quarter, quarter),
            (far_ref, other + (1 - core) * quarter, quarter),
        )
    ):
        rows = pl.ds(pl.multiple_of(start, quarter), count)
        copies.append(
            pltpu.make_async_copy(ref.at[:, cols], into.at[rows, cols], sems.at[first + number])
        )
    return copies


def attend_kernel(
    place,
    tok_hbm,
    own_ref,
    near_ref,
    side_ref,
    far_ref,
    seg_ref,
    picks_ref,
    q_ref,
    k_ref,
    v_ref,
    o_ref,
    lse_ref,
    rows_ref,
    tok_t_hbm,
    marks_ref,
    table_ref,
    tok_ref,
    tok_t_ref,
    w_scr,
    lse_scr,
    even,
    odd,
    sems,
    tok_sems,
    *,
    tile,
    slots,
    blocks,
):
    length = q_ref.shape[0]
    pair = pl.program_id(0)
    lane = lax.broadcasted_iota(jnp.int32, (1, LANES), 1)
    zero = jnp.zeros((), BF)

    @pl.when(pair == 0)
    def _():
        copies = gathered_eighths(place, own_ref, near_ref, side_ref, far_ref, w_scr, sems)
        step = length // 4
        loads = [
            pltpu.make_async_copy(
                tok_hbm.at[n * step : (n + 1) * step, :],
                tok_ref.at[n * step : (n + 1) * step, :],
                tok_sems.at[n],
            )
            for n in range(4)
        ]
        for copy in copies + loads:
            copy.start()
        lse_scr[...] = jnp.zeros_like(lse_scr)
        marks_ref[...] = token_marks(seg_ref[...], blocks)
        for load in loads:
            load.wait()
        tok_t_ref[...] = piece_order(tok_ref, place[1])
        pltpu.make_async_copy(tok_t_ref, tok_t_hbm, tok_sems.at[4]).start()
        for copy in copies:
            copy.wait()
        small = w_scr[:, w_scr.shape[1] - LANES :].astype(F32)
        rows_ref[...] = jnp.transpose(small)[: rows_ref.shape[0], :]

    cols = pl.ds(pl.multiple_of(pair * 3 * LANES, LANES), 3 * LANES)
    here = pl.ds(pl.multiple_of(pair * LANES, LANES), LANES)
    bias = jnp.concatenate(
        [rows_ref[6:7, here], jnp.zeros((1, LANES), F32), rows_ref[7:8, here]], axis=1
    )
    qkv = (dotf(tok_ref[...], w_scr[:, cols]) + bias).astype(BF)
    q_ref[...] = qkv[:, :LANES]
    k_ref[...] = qkv[:, LANES : 2 * LANES]
    v_ref[...] = qkv[:, 2 * LANES :]
    keys, values = [], []
    for head in range(2):
        table_ref[head] = head_table(picks_ref[head], slots, blocks)
        key_marks = dotf(marks_ref[...], table_ref[head]).astype(BF)
        keys.append(jnp.concatenate([k_ref[...], key_marks], axis=1))
        values.append(jnp.where(lane // HD == head, v_ref[...], zero))
    steps = [(at, head) for at in range(0, length, tile) for head in range(2)]
    held = [even, odd]

    def score(index):
        at, head = steps[index]
        rows = pl.ds(at, tile)
        query = jnp.where(lane // HD == head, q_ref[rows, :] * jnp.asarray(HD**-0.5, BF), zero)
        return dotf(jnp.concatenate([query, marks_ref[rows, :]], axis=1), keys[head], NT)

    held[0][...] = score(0)
    first = None
    for index, (at, head) in enumerate(steps):
        rows = pl.ds(at, tile)
        if index + 1 < len(steps):
            held[(index + 1) % 2][...] = score(index + 1)
        now = held[index % 2]
        top = jnp.max(now[...], axis=1, keepdims=True)
        raised = jnp.exp(now[...] - top)
        total = jnp.sum(raised, axis=1, keepdims=True)
        mixed = dotf(raised.astype(BF), values[head]) * (1.0 / total)
        if head == 0:
            first = mixed
        else:
            o_ref[rows, :] = (first + mixed).astype(BF)
        lse_scr[rows, :] = jnp.where(
            lane == 2 * pair + head, top + jnp.log(total), lse_scr[rows, :]
        )

    @pl.when(pair == pl.num_programs(0) - 1)
    def _():
        lse_ref[...] = jnp.transpose(lse_scr[...])[: lse_ref.shape[0], :]
        pltpu.make_async_copy(tok_t_ref, tok_t_hbm, tok_sems.at[4]).wait()


def attend(place, tokens, own, near, side, far, segments, random_blocks):
    length, model = tokens.shape
    blocks, heads, slots = random_blocks.shape[1:]
    picks = jnp.pad(
        random_blocks[0].transpose(1, 2, 0),
        ((0, 0), (0, 8 - slots), (0, LANES - blocks)),
        constant_values=-1,
    )
    width = own.shape[1]
    pairs = (width - LANES) // (3 * LANES)
    tile = 256
    whole = lambda dims: pl.BlockSpec(dims, lambda i: (0,) * len(dims))
    anywhere = pl.BlockSpec(memory_space=pl.ANY)
    block = pl.BlockSpec((length, LANES), lambda i: (0, i))
    out_rows = 16
    return pl.pallas_call(
        functools.partial(attend_kernel, tile=tile, slots=slots, blocks=blocks),
        grid=(pairs,),
        in_specs=[
            SM,
            anywhere,
            anywhere,
            anywhere,
            anywhere,
            anywhere,
            whole((1, length)),
            pl.BlockSpec((2, 8, LANES), lambda i: (i, 0, 0)),
        ],
        out_specs=[
            block,
            block,
            block,
            block,
            whole((out_rows, length)),
            whole((out_rows, model)),
            anywhere,
            whole((length, LANES)),
            pl.BlockSpec((2, LANES, LANES), lambda i: (i, 0, 0)),
        ],
        out_shape=[shape((length, pairs * LANES), BF)] * 4
        + [
            shape((out_rows, length), F32),
            shape((out_rows, model), F32),
            shape((model, length), BF),
            shape((length, LANES), BF),
            shape((heads, LANES, LANES), BF),
        ],
        scratch_shapes=[
            pltpu.VMEM((length, model), BF),
            pltpu.VMEM((model, length), BF),
            pltpu.VMEM((model, width), BF),
            pltpu.VMEM((length, LANES), F32),
            pltpu.VMEM((tile, length), F32),
            pltpu.VMEM((tile, length), F32),
            pltpu.SemaphoreType.DMA((5,)),
            pltpu.SemaphoreType.DMA((5,)),
        ],
        compiler_params=params(58),
        cost_estimate=cost(18e9, 12 << 20, 8 << 20),
        name="attend",
    )(place, tokens, own, near, side, far, segments, picks)


def attend_back_kernel(
    place,
    q_ref,
    k_ref,
    v_ref,
    do_ref,
    o_ref,
    marks_ref,
    table_ref,
    lse_ref,
    tok_t_hbm,
    mid_ref,
    keep_hbm,
    send_hbm,
    d_ref,
    keep_ref,
    send_ref,
    tok_t_ref,
    dq_sum,
    dv_sum,
    dk_sum,
    bias_scr,
    load_sem,
    out_sems,
    *,
    tile,
):
    length = q_ref.shape[0]
    pair = pl.program_id(0)
    load = pltpu.make_async_copy(tok_t_hbm, tok_t_ref, load_sem)

    @pl.when(pair == 0)
    def _():
        load.start()

    core = place[1]
    lane = lax.broadcasted_iota(jnp.int32, (1, LANES), 1)
    zero = jnp.zeros((), BF)
    scale = jnp.asarray(HD**-0.5, BF)
    prod = do_ref[...].astype(F32) * o_ref[...].astype(F32)
    high = prod.astype(BF)
    low = (prod - high.astype(F32)).astype(BF)
    pick = (
        lax.broadcasted_iota(jnp.int32, (8, LANES), 0)
        == lax.broadcasted_iota(jnp.int32, (8, LANES), 1) // HD
    ).astype(BF)
    inner = dotf(pick, high, NT) + dotf(pick, low, NT)
    keys_t = jnp.transpose(k_ref[...] * scale)
    for head in range(2):
        mine = lane // HD == head
        key_marks = dotf(marks_ref[...], table_ref[head]).astype(BF)
        keys = jnp.concatenate([k_ref[...], key_marks], axis=1)
        log_total = lse_ref[pl.ds(2 * pair + head, 1), :]
        for at in range(0, length, tile):
            here = pl.ds(at, tile)
            query = jnp.where(mine, q_ref[here, :] * scale, zero)
            upstream = jnp.where(mine, do_ref[here, :], zero)
            scores = dotf(keys, jnp.concatenate([query, marks_ref[here, :]], axis=1), NT)
            probs = jnp.exp(scores - log_total[:, at : at + tile])
            grad_probs = dotf(v_ref[...], upstream, NT)
            grad_scores = (probs * (grad_probs - inner[head : head + 1, at : at + tile])).astype(BF)
            grad_v = dotf(probs.astype(BF), upstream)
            grad_k = dotf(grad_scores, query)
            dq_sum[head * HD : (head + 1) * HD, here] = dotf(
                keys_t[head * HD : (head + 1) * HD], grad_scores
            )
            if head == 0 and at == 0:
                dv_sum[...] = grad_v
                dk_sum[...] = grad_k
            else:
                dv_sum[...] += grad_v
                dk_sum[...] += grad_k
    d_ref[:, :LANES] = jnp.transpose(dq_sum[...]).astype(BF)
    d_ref[:, LANES : 2 * LANES] = dk_sum[...].astype(BF)
    d_ref[:, 2 * LANES :] = dv_sum[...].astype(BF)
    outs = (keep_ref, send_ref)
    width = 3 * LANES

    @pl.when(pair == 0)
    def _():
        load.wait()

    def write_out(group, count):
        cols = pl.ds(pl.multiple_of(group * width, LANES), count)
        return [
            pltpu.make_async_copy(source.at[:, cols], into.at[:, cols], out_sems.at[number, group])
            for number, (source, into) in enumerate(((send_ref, send_hbm), (keep_ref, keep_hbm)))
        ]

    result = dotf(tok_t_ref[...], d_ref[...]).astype(BF)
    store_pieces(result, core, outs, pl.ds(pl.multiple_of(pair * width, LANES), width))
    for copy in write_out(pair, width):
        copy.start()
    here = pl.ds(pl.multiple_of(pair * LANES, LANES), LANES)
    bias_scr[0:1, here] = col_sum(d_ref[:, :LANES].astype(F32))
    bias_scr[1:2, here] = col_sum(d_ref[:, 2 * LANES :].astype(F32))

    @pl.when(pair == pl.num_programs(0) - 1)
    def _():
        model = mid_ref.shape[1]
        sums = jnp.concatenate(
            [
                mid_ref[0:6, :],
                bias_scr[0:2, :],
                mid_ref[8:16, :],
                jnp.zeros((LANES - 16, model), F32),
            ],
            axis=0,
        )
        quarter = model // 4
        turned = jnp.transpose(sums)
        kept, sent = [], []
        for r0 in range(2):
            lower = turned[r0 * 2 * quarter : r0 * 2 * quarter + quarter]
            upper = turned[r0 * 2 * quarter + quarter : (r0 + 1) * 2 * quarter]
            kept.append(jnp.where(core == 0, lower, upper))
            sent.append(jnp.where(core == 0, upper, lower))
        total = keep_ref.shape[1]
        store_pieces(
            jnp.concatenate(kept + sent, axis=0).astype(BF), core, outs, slice(total - LANES, total)
        )
        groups = (total - LANES) // width
        last = write_out(groups, LANES)
        for copy in last:
            copy.start()
        for group in range(groups):
            for copy in write_out(group, width):
                copy.wait()
        for copy in last:
            copy.wait()


def attend_back(place, q, k, v, grad_mixed, mixed, marks, table, lse, tok_t, sums):
    length = q.shape[0]
    model = tok_t.shape[0]
    pairs = q.shape[1] // LANES
    width = 3 * LANES
    total = pairs * width + LANES
    whole = lambda dims: pl.BlockSpec(dims, lambda i: (0,) * len(dims))
    block = pl.BlockSpec((length, LANES), lambda i: (0, i))
    return pl.pallas_call(
        functools.partial(attend_back_kernel, tile=512),
        grid=(pairs,),
        in_specs=[SM]
        + [block] * 5
        + [whole(marks.shape), pl.BlockSpec((2, LANES, LANES), lambda i: (i, 0, 0))]
        + [whole(lse.shape), pl.BlockSpec(memory_space=pl.ANY), whole(sums.shape)],
        out_specs=[
            pl.BlockSpec(memory_space=pl.ANY),
            pl.BlockSpec(memory_space=pl.ANY),
            pl.BlockSpec((length, width), lambda i: (0, i)),
        ],
        out_shape=[
            shape((model // 2, total), BF),
            shape((model // 2, total), BF),
            shape((length, pairs * width), BF),
        ],
        scratch_shapes=[
            pltpu.VMEM((model // 2, total), BF),
            pltpu.VMEM((model // 2, total), BF),
            pltpu.VMEM((model, length), BF),
            pltpu.VMEM((LANES, length), F32),
            pltpu.VMEM((length, LANES), F32),
            pltpu.VMEM((length, LANES), F32),
            pltpu.VMEM((8, model), F32),
            pltpu.SemaphoreType.DMA,
            pltpu.SemaphoreType.DMA((2, pairs + 1)),
        ],
        compiler_params=params(58),
        cost_estimate=cost(30e9, 10 << 20, 8 << 20, 1.0),
        name="attend_back",
    )(place, q, k, v, grad_mixed, mixed, marks, table, lse, tok_t, sums)


def piece_order(lhs_ref, core):
    quarter = lhs_ref.shape[1] // 4
    cols = []
    for target in (core, 1 - core):
        for half in range(2):
            start = pl.multiple_of(half * 2 * quarter + target * quarter, quarter)
            cols.append(lhs_ref[:, pl.ds(start, quarter)])
    return jnp.transpose(jnp.concatenate(cols, axis=1))


def store_pieces(result, core, outs, cols):
    quarter = result.shape[0] // 4
    piece = quarter // 4
    for which, target in enumerate((core, 1 - core)):
        for r0 in range(2):
            for r2 in range(2):
                for r3 in range(2):
                    at = which * 2 * quarter + r0 * quarter + r2 * 2 * piece + r3 * piece
                    spot = jnp.where(target == 0, r0 * 4 + r2 * 2 + r3, r3 * 4 + r2 * 2 + r0)
                    rows = pl.ds(pl.multiple_of(spot * piece, piece), piece)
                    outs[which][rows, cols] = result[at : at + piece, :]


def weight_grad(lhs_t, rhs_ref, core, outs, first, tile=512):
    for at in range(0, rhs_ref.shape[1], tile):
        result = dotf(lhs_t, rhs_ref[:, at : at + tile]).astype(BF)
        store_pieces(result, core, outs, slice(first + at, first + at + tile))


def normed(hidden):
    center = hidden - jnp.mean(hidden, axis=-1, keepdims=True)
    spread = jnp.mean(center * center, axis=-1, keepdims=True)
    rate = lax.rsqrt(spread + norm_eps)
    return center * rate, rate


def norm_back(grad, unit, rate):
    return rate * (
        grad
        - jnp.mean(grad, axis=-1, keepdims=True)
        - unit * jnp.mean(grad * unit, axis=-1, keepdims=True)
    )


def col_sum(values):
    return jnp.sum(values, axis=0, keepdims=True)


def middle_kernel(
    place,
    rows_ref,
    tok_hbm,
    cot_hbm,
    mixed_hbm,
    own_hbm,
    near_hbm,
    far_hbm,
    out_hbm,
    dh_hbm,
    do_hbm,
    keep_hbm,
    send_hbm,
    sums_ref,
    tok_ref,
    cot_ref,
    mixed_ref,
    out_ref,
    dh_ref,
    do_ref,
    keep_ref,
    send_ref,
    w_scr,
    act_scr,
    du_scr,
    z_scr,
    df_scr,
    da_scr,
    sems,
    out_sems,
    *,
    tile,
):
    length, model = tok_ref.shape
    core = place[1]
    hidden_count = act_scr.shape[1]
    w_up = slice(0, hidden_count)
    w_down = slice(hidden_count, 2 * hidden_count)
    w_out = slice(2 * hidden_count, w_scr.shape[1])
    waits = {}
    number = 0
    for name, sources in (
        ("out", w_out),
        (0, ((mixed_hbm, mixed_ref), (tok_hbm, tok_ref))),
        ("up", w_up),
        ("down", w_down),
        ("cot", ((cot_hbm, cot_ref),)),
        *((at, ((mixed_hbm, mixed_ref), (tok_hbm, tok_ref))) for at in range(tile, length, tile)),
    ):
        if isinstance(sources, slice):
            copies = gathered_rows(
                place, own_hbm, near_hbm, far_hbm, w_scr, sems, sources, number
            )
        else:
            rows = slice(None) if name == "cot" else slice(name, name + tile)
            copies = [
                pltpu.make_async_copy(source.at[rows, :], into.at[rows, :], sems.at[number + n])
                for n, (source, into) in enumerate(sources)
            ]
        number += len(copies)
        for copy in copies:
            copy.start()
        waits[name] = copies

    def ready(name):
        for copy in waits.pop(name, ()):
            copy.wait()

    pending = []

    def write_out(source, into):
        copy = pltpu.make_async_copy(source, into, out_sems.at[len(pending)])
        copy.start()
        pending.append(copy)

    row = lambda number: rows_ref[number : number + 1, :]
    bias_up = jnp.concatenate([row(8), row(9), row(10), row(11)], axis=1)
    sums = [jnp.zeros((1, model), F32)] * 6
    sum_up = jnp.zeros((1, hidden_count), F32)
    for at in range(0, length, tile):
        here = pl.ds(at, tile)
        ready("out")
        ready(at)
        attn_out = dotf(mixed_ref[here, :], w_scr[:, w_out], NT) + row(4)
        unit_one, rate_one = normed(tok_ref[here, :].astype(F32) + attn_out)
        z_one = unit_one * row(0) + row(1)
        z_low = z_one.astype(BF)
        z_scr[here, :] = z_low
        ready("up")
        up = dotf(z_low, w_scr[:, w_up]) + bias_up
        below = 0.5 * (1.0 + lax.erf(up * (0.5**0.5)))
        slope = below + up * (jnp.exp(-0.5 * up * up) * (1.0 / (2.0 * 3.141592653589793) ** 0.5))
        active = (up * below).astype(BF)
        act_scr[here, :] = active
        ready("down")
        ffn_out = dotf(active, w_scr[:, w_down], NT) + row(5)
        unit_two, rate_two = normed(z_one + ffn_out)
        out_ref[here, :] = (unit_two * row(2) + row(3)).astype(BF)
        ready("cot")
        upstream = cot_ref[here, :].astype(F32)
        grad_two = norm_back(upstream * row(2), unit_two, rate_two)
        down_low = grad_two.astype(BF)
        df_scr[here, :] = down_low
        grad_up = (dotf(down_low, w_scr[:, w_down]) * slope).astype(BF)
        du_scr[here, :] = grad_up
        grad_z = grad_two + dotf(grad_up, w_scr[:, w_up], NT)
        grad_one = norm_back(grad_z * row(0), unit_one, rate_one)
        dh_ref[here, :] = grad_one
        attn_low = grad_one.astype(BF)
        da_scr[here, :] = attn_low
        do_ref[here, :] = dotf(attn_low, w_scr[:, w_out]).astype(BF)
        for source, into in ((out_ref, out_hbm), (dh_ref, dh_hbm), (do_ref, do_hbm)):
            write_out(source.at[here, :], into.at[here, :])
        parts = (
            grad_z * unit_one,
            grad_z,
            upstream * unit_two,
            upstream,
            attn_low.astype(F32),
            down_low.astype(F32),
        )
        sums = [a + col_sum(b) for a, b in zip(sums, parts)]
        sum_up = sum_up + col_sum(grad_up.astype(F32))
    for number in range(6):
        sums_ref[number : number + 1, :] = sums[number]
    sums_ref[6:8, :] = jnp.zeros((2, model), F32)
    for number in range(4):
        sums_ref[8 + number : 9 + number, :] = sum_up[:, number * model : (number + 1) * model]
    sums_ref[12:16, :] = jnp.zeros((4, model), F32)
    outs = (keep_ref, send_ref)
    for lhs, rhs, cols in (
        (z_scr, du_scr, w_up),
        (df_scr, act_scr, w_down),
        (da_scr, mixed_ref, w_out),
    ):
        weight_grad(piece_order(lhs, core), rhs, core, outs, cols.start)
        for source, into in ((send_ref, send_hbm), (keep_ref, keep_hbm)):
            write_out(source.at[:, cols], into.at[:, cols])
    for copy in pending:
        copy.wait()


def middle(place, tokens, cotangent, mixed, rows, own, near, far):
    length, model = tokens.shape
    width = own.shape[1]
    hidden_count = (width - mixed.shape[1]) // 2
    tile = 512
    anywhere = pl.BlockSpec(memory_space=pl.ANY)
    outs = [
        shape((length, model), BF),
        shape((length, model), F32),
        shape((length, mixed.shape[1]), BF),
        shape((model // 2, width), BF),
        shape((model // 2, width), BF),
    ]
    vmem = lambda x: pltpu.VMEM(x.shape, x.dtype)
    return pl.pallas_call(
        functools.partial(middle_kernel, tile=tile),
        in_specs=[SM, VM] + [anywhere] * 6,
        out_specs=[anywhere] * 5 + [VM],
        out_shape=outs + [shape((16, model), F32)],
        scratch_shapes=[vmem(x) for x in (tokens, cotangent, mixed, *outs)]
        + [
            pltpu.VMEM((model, width), BF),
            pltpu.VMEM((length, hidden_count), BF),
            pltpu.VMEM((length, hidden_count), BF),
            pltpu.VMEM((length, model), BF),
            pltpu.VMEM((length, model), BF),
            pltpu.VMEM((length, model), BF),
            pltpu.SemaphoreType.DMA((10 + 2 * (length // tile),)),
            pltpu.SemaphoreType.DMA((3 * (length // tile) + 6,)),
        ],
        compiler_params=params(58),
        cost_estimate=cost(16e9, 16 << 20, 4 << 20, 1.0),
        name="middle",
    )(place, rows, tokens, cotangent, mixed, own, near, far)


def input_grad_kernel(
    place, dh_ref, d_ref, own_ref, near_ref, side_ref, far_ref, out_ref, w_scr, sems
):
    width = d_ref.shape[1]

    @pl.when(pl.program_id(0) == 0)
    def _():
        copies = gathered_eighths(place, own_ref, near_ref, side_ref, far_ref, w_scr, sems)
        for copy in copies:
            copy.start()
        for copy in copies:
            copy.wait()

    out_ref[...] = (dh_ref[...] + dotf(d_ref[...], w_scr[:, :width], NT)).astype(BF)


def input_gradient(place, dh, d, own, near, side, far):
    length, model = dh.shape
    tile = 256
    anywhere = pl.BlockSpec(memory_space=pl.ANY)
    rows = lambda width: pl.BlockSpec((tile, width), lambda i: (i, 0))
    return pl.pallas_call(
        input_grad_kernel,
        grid=(length // tile,),
        in_specs=[SM, rows(model), rows(d.shape[1])] + [anywhere] * 4,
        out_specs=rows(model),
        out_shape=shape((length, model), BF),
        scratch_shapes=[pltpu.VMEM((model, own.shape[1]), BF), pltpu.SemaphoreType.DMA((5,))],
        compiler_params=params(16),
        cost_estimate=cost(2 * length * model * d.shape[1], 8 << 20),
        name="input_gradient",
    )(place, dh, d, own, near, side, far)


def add_low(a, b):
    return (a.astype(F32) + b.astype(F32)).astype(BF)


def add_parts_kernel(place, *refs):
    total = refs[0][...].astype(F32)
    for ref in refs[1:-1]:
        total = total + ref[...].astype(F32)
    refs[-1][...] = total.astype(BF)


def add_parts(place, parts, give):
    rows = min(part.shape[0] for part in parts)
    rows = rows // 2 if give else rows
    width = parts[0].shape[1]

    def pick(part):
        if part.shape[0] == rows:
            return pl.BlockSpec((rows, width), lambda i, place: (0, 0))
        return pl.BlockSpec((rows, width), lambda i, place: (1 - place[6] if give else place[6], 0))

    return pl.pallas_call(
        add_parts_kernel,
        grid_spec=pltpu.PrefetchScalarGridSpec(
            num_scalar_prefetch=1,
            grid=(1,),
            in_specs=[pick(part) for part in parts],
            out_specs=pl.BlockSpec((rows, width), lambda i, place: (0, 0)),
        ),
        out_shape=shape((rows, width), BF),
        compiler_params=params(8),
        cost_estimate=cost(len(parts) * rows * width, 2 * len(parts) * rows * width),
        name="add_parts",
    )(place, *parts)


def flip(count, bit):
    return [(i, i ^ (1 << bit)) for i in range(count)]


def mixed_flip(count, even, odd):
    return [(i, i ^ (1 << (odd if (i >> 1) & 1 else even))) for i in range(2 * count)]


STEPS = ((0, 2), (2, 3), (3, 0))


def mixed_mask(count, mask):
    pairs = []
    for i in range(2 * count):
        partner = i
        for bit, step in zip((2, 1), STEPS):
            if mask & bit:
                partner ^= 1 << step[(i >> 1) & 1]
        pairs.append((i, partner))
    return pairs


def split_kernel(place, keep_ref, got_ref, *outs):
    piece = outs[0].shape[0]
    mine = place[3] * 2 + place[4]
    for mask, out in enumerate(outs):
        rows = pl.ds(pl.multiple_of((mine ^ mask) * piece, piece), piece)
        out[...] = add_low(keep_ref[rows, :], got_ref[rows, :])


def swap_two(value, count, mask):
    return lax.ppermute(value, ("dp", "shard"), mixed_mask(count, mask))


def split(place, keep, got):
    rows, width = keep.shape
    steps = 4 if width % (4 * LANES) == 0 else 1
    step = width // steps
    whole = pl.BlockSpec((rows, step), lambda i: (0, i))
    part = pl.BlockSpec((rows // 4, step), lambda i: (0, i))
    return pl.pallas_call(
        split_kernel,
        grid=(steps,),
        in_specs=[SM, whole, whole],
        out_specs=[part] * 4,
        out_shape=[shape((rows // 4, width), BF)] * 4,
        compiler_params=params(16),
        cost_estimate=cost(rows * width, 6 * rows * width),
        name="split",
    )(place, keep, got)


def swap_core(value, count):
    return lax.ppermute(value, "dp", flip(count, 0))


def swap_mixed(value, count, step):
    return lax.ppermute(value, ("dp", "shard"), mixed_flip(count, *step))


def swap_bit(value, count, bit):
    return lax.ppermute(value, "dp", flip(count, bit))


def after(value, *others):
    return lax.optimization_barrier((value,) + others)[0]


def adam_values(scalars, weight_ref, mean_ref, square_ref, grad, decay, outs):
    weight = weight_ref[...]
    mean_out = beta_one * mean_ref[...] + (1.0 - beta_one) * grad
    square_out = beta_two * square_ref[...] + (1.0 - beta_two) * grad * grad
    mean_hat = mean_out * scalars[2]
    square_hat = square_out * scalars[3]
    weight_out = weight - scalars[0] * (
        mean_hat / (jnp.sqrt(square_hat) + adam_eps) + decay * weight
    )
    outs[0][...] = weight_out
    outs[1][...] = mean_out
    outs[2][...] = square_out
    outs[3][...] = weight_out.astype(BF)


def piece_block(place, own, flips):
    bit2, bit3 = (place[4], place[5]) if own else (place[5], place[4])
    core = place[1] if own else 1 - place[1]
    return core * 4 + (bit2 ^ (flips >> 1)) * 2 + (bit3 ^ (flips & 1))


def chosen(index, values):
    result = values[-1]
    for number in range(len(values) - 2, -1, -1):
        result = jnp.where(index == number, values[number], result)
    return result


def adam_ffn_kernel(place, scalars, *refs, count):
    step = pl.program_id(0)
    stack, _, width = refs[count].shape
    for number in range(count):

        @pl.when(step == number)
        def _():
            grad = jnp.stack(
                [refs[number][:, w * width : (w + 1) * width].astype(F32) for w in range(stack)]
            )
            adam_values(scalars, *refs[count : count + 3], grad, scalars[1], refs[-4:])


def adam_ffn(place, scalars, pieces, state, before):
    count = len(pieces)
    stack, rows, width = state[0].shape
    step = rows // 8
    grads = [piece[0] for piece in pieces]
    take = pl.BlockSpec((step, stack * width), lambda p, place, sc: (0, 0))
    block = pl.BlockSpec(
        (stack, step, width),
        lambda p, place, sc: (0, chosen(p, [piece_block(place, *x[1:]) for x in pieces]), 0),
    )
    before = list(before or ())
    return pl.pallas_call(
        functools.partial(adam_ffn_kernel, count=count),
        grid_spec=pltpu.PrefetchScalarGridSpec(
            num_scalar_prefetch=2,
            grid=(count,),
            in_specs=[take] * count + [block] * 3 + [pl.BlockSpec(memory_space=pl.ANY)] * len(before),
            out_specs=[block] * 4,
        ),
        out_shape=[shape(state[0].shape, F32)] * 3 + [shape(state[0].shape, BF)],
        input_output_aliases={5 + count + n: n for n in range(len(before))},
        compiler_params=params(24),
        cost_estimate=cost(20 * count * step * width, 28 * count * step * width),
        name="adam_ffn",
    )(place, scalars, *grads, *state, *before)


def adam_attn_kernel(place, scalars, *refs, count, orders, small):
    grads, outer, state = refs[:count], refs[count : 2 * count], refs[2 * count : 2 * count + 3]
    rest = refs[2 * count + 3 :]
    step = pl.program_id(0)
    if small:
        little, (sw, sm, ss), rest = rest[:small], rest[small : small + 3], rest[small + 3 + 4 :]
        outs, small_outs, scr = rest[:4], rest[4:8], rest[8]

        @pl.when(step == 0)
        def _():
            for ref, order in zip(little, orders):
                rows = ref.shape[0]
                where = pl.ds(pl.multiple_of(piece_block(place, *order) * rows, rows), rows)
                scr[where, :] = ref[...].astype(F32)
            turned = jnp.transpose(scr[...])[: sw.shape[0], :]
            adam_values(scalars, sw, sm, ss, turned, 0.0 * scalars[1], small_outs)
    else:
        outs = rest[-4:]
    for number in range(count):

        @pl.when(step == number)
        def _():
            grad = grads[number][...].astype(F32)
            pairs = grad.shape[1] // (3 * LANES)
            parts = [
                grad[:, p * 3 * LANES + kind * LANES : p * 3 * LANES + (kind + 1) * LANES]
                for kind in range(3)
                for p in range(pairs)
            ]
            parts.append(outer[number][...].astype(F32))
            adam_values(scalars, *state, jnp.concatenate(parts, axis=1), scalars[1], outs)


def adam_attn(place, scalars, pieces, pieces_b, state, before, every=None, small=None):
    count = len(pieces)
    rows, width = state[0].shape
    step = rows // 8
    out_width = width // 4
    grads = [piece[0] for piece in pieces]
    outer = [piece[0] for piece in pieces_b]
    last = outer[0].shape[1] // out_width - 1
    block = pl.BlockSpec(
        (step, width),
        lambda p, place, sc: (chosen(p, [piece_block(place, *x[1:]) for x in pieces]), 0),
    )
    anywhere = pl.BlockSpec(memory_space=pl.ANY)
    in_specs = [pl.BlockSpec(grads[0].shape, lambda p, place, sc: (0, 0))] * count
    in_specs += [pl.BlockSpec((step, out_width), lambda p, place, sc: (0, last))] * count
    in_specs += [block] * 3
    operands = [place, scalars, *grads, *outer, *state]
    out_specs = [block] * 4
    out_shape = [shape(state[0].shape, F32)] * 3 + [shape(state[0].shape, BF)]
    scratch = []
    if small:
        whole = pl.BlockSpec(small[0].shape, lambda p, place, sc: (0, 0))
        at = grads[0].shape[1] // LANES - 1
        in_specs += [pl.BlockSpec((step, LANES), lambda p, place, sc: (0, at))] * len(every)
        in_specs += [whole] * 3
        operands += [piece[0] for piece in every] + list(small)
        out_specs += [whole] * 4
        out_shape += [shape(small[0].shape, F32)] * 3 + [shape(small[0].shape, BF)]
        scratch = [pltpu.VMEM((rows, LANES), F32)]
    before = list(before or ())
    aliases = {len(operands) + n: n for n in range(len(before))}
    return pl.pallas_call(
        functools.partial(
            adam_attn_kernel,
            count=count,
            orders=[piece[1:] for piece in every or ()],
            small=len(every or ()),
        ),
        grid_spec=pltpu.PrefetchScalarGridSpec(
            num_scalar_prefetch=2,
            grid=(count,),
            in_specs=in_specs + [anywhere] * len(before),
            out_specs=out_specs,
            scratch_shapes=scratch,
        ),
        out_shape=out_shape,
        input_output_aliases=aliases,
        compiler_params=params(24),
        cost_estimate=cost(20 * count * step * width, 28 * count * step * width),
        name="adam_attn",
    )(*operands, *before)


def from_neighbour(value):
    return lax.ppermute(value, "shard", [(0, 1), (1, 0)])


def local(
    count,
    tokens,
    cotangent,
    segments,
    random_blocks,
    step_count,
    adam_rates,
    attn_master,
    attn_mean,
    attn_square,
    ffn_master,
    ffn_mean,
    ffn_square,
    small_master,
    small_mean,
    small_square,
):
    replica = lax.axis_index("dp")
    shard = lax.axis_index("shard")
    core, low, high = replica & 1, (replica >> 1) & 1, (replica >> 2) & 1
    even = core == 0
    place = jnp.stack(
        [
            shard,
            core,
            low,
            jnp.where(even, shard, low),
            jnp.where(even, low, high),
            jnp.where(even, high, low),
            jnp.where(even, high, shard),
        ]
    ).astype(jnp.int32)
    pairs = attn_master.shape[1] // 4 // LANES
    near_a = from_neighbour(pack_eighth_a(place, attn_master, small_master))
    quarter_b = pack_quarter_b(place, attn_master, ffn_master)
    near_a = after(near_a, quarter_b)
    near_b = from_neighbour(after(quarter_b, near_a))
    side_a = swap_bit(near_a, count, 1)
    own_a, own_b = pack_own(attn_master, ffn_master, small_master)
    far_a = swap_core(jnp.concatenate([near_a, after(side_a, own_a)]), count)
    q, k, v, mixed, lse, rows, tok_t, marks, table = attend(
        place, tokens, own_a, near_a, side_a, far_a, segments, random_blocks
    )
    far_b = swap_core(after(near_b, lse), count)
    layer_out, dh, grad_mixed, keep_b, send_b, sums = middle(
        place, tokens, cotangent, mixed, rows, own_b, near_b, far_b
    )
    parts_b = list(split(place, keep_b, swap_core(send_b, count)))
    parts_b = parts_b[:1] + [swap_two(parts_b[mask], count, mask) for mask in (1, 2, 3)]
    keep_a, send_a, d = attend_back(
        place, q, k, v, after(grad_mixed, parts_b[0]), mixed, marks, table, lse, tok_t, sums
    )
    got_a = swap_core(send_a, count)
    parts_b = parts_b[:1] + [after(part, d) for part in parts_b[1:]]
    got_b = swap_mixed(add_parts(place, parts_b, True), count, STEPS[2])

    step_value = step_count[0].astype(F32)
    scalars = jnp.stack(
        [
            adam_rates[0],
            adam_rates[1],
            1.0 / (1.0 - beta_one**step_value),
            1.0 / (1.0 - beta_two**step_value),
        ]
    )
    ffn_state = (ffn_master, ffn_mean, ffn_square)
    attn_state = (attn_master, attn_mean, attn_square)
    small_state = (small_master, small_mean, small_square)
    bits = [bit for bit in range(3, count.bit_length() - 1)]

    parts_a = list(split(place, keep_a, got_a))
    parts_a = parts_a[:1] + [swap_two(parts_a[mask], count, mask) for mask in (1, 2, 3)]
    total_b = add_parts(place, parts_b + [after(got_b, parts_a[0])], False)
    got_b = swap_bit(total_b, count, bits[0])
    input_grad = input_gradient(place, after(dh, total_b), d, own_a, near_a, side_a, far_a)
    parts_a = parts_a[:1] + [after(part, input_grad) for part in parts_a[1:]]
    got_a = swap_mixed(add_parts(place, parts_a, True), count, STEPS[2])
    total_a = add_parts(place, parts_a + [got_a], False)
    got_a = swap_bit(total_a, count, bits[0])
    total_b = add_low(total_b, after(got_b, total_a))
    for bit in bits[1:]:
        total_b = add_low(total_b, swap_bit(total_b, count, bit))
    first, second = (3, 2), (2, 3)

    def wave(values, flips):
        return [(v, True, f) for v, f in zip(values, flips)] + [
            (swap_core(v, count), False, f) for v, f in zip(values, flips)
        ]

    b_one = wave([total_b], [0])
    got_b = [swap_mixed(total_b, count, first), swap_mixed(total_b, count, second)]
    total_a = add_low(total_a, after(got_a, total_b))
    for bit in bits[1:]:
        total_a = add_low(total_a, swap_bit(total_a, count, bit))
    ffn_new = adam_ffn(place, scalars, b_one, ffn_state, None)
    a_one = wave([total_a], [0])
    got_a = [swap_mixed(total_a, count, first), swap_mixed(total_a, count, second)]
    got_b = [after(piece, ffn_new[0], total_a) for piece in got_b]
    b_two = wave(got_b, [1, 2])
    got_b = swap_mixed(got_b[0], count, second)
    attn_new = adam_attn(place, scalars, a_one, b_one, attn_state, None)
    ffn_new = adam_ffn(place, scalars, b_two, ffn_state, ffn_new)
    got_a = [after(piece, attn_new[0]) for piece in got_a]
    a_two = wave(got_a, [1, 2])
    got_a = swap_mixed(got_a[0], count, second)
    b_three = wave([after(got_b, ffn_new[0])], [3])
    attn_new = adam_attn(place, scalars, a_two, b_two, attn_state, attn_new)
    a_three = wave([after(got_a, attn_new[0])], [3])
    ffn_new = adam_ffn(place, scalars, b_three, ffn_state, ffn_new)
    attn_new = adam_attn(
        place,
        scalars,
        a_three,
        b_three,
        attn_state,
        attn_new,
        a_one + a_two + a_three,
        small_state,
    )
    return (layer_out, input_grad) + tuple(attn_new[:4]) + tuple(ffn_new) + tuple(attn_new[4:])


def solution(mesh):
    tokens_in = P(("dp", "shard"), None)
    rows_in = P("shard", None)
    stack_in = P(None, "shard", None)
    cols_in = P(None, "shard")
    placed = (
        (tokens_in,) * 3
        + (P(("dp", "shard"), None, None, None), P(), P())
        + (rows_in,) * 3
        + (stack_in,) * 3
        + (cols_in,) * 3
    )
    return jax.shard_map(
        functools.partial(local, mesh.shape["dp"]),
        mesh=mesh,
        in_specs=placed,
        out_specs=(tokens_in,) * 2 + (rows_in,) * 4 + (stack_in,) * 4 + (cols_in,) * 4,
        check_vma=False,
    )
```

```python
import functools

import jax
import jax.numpy as jnp
from jax import lax
from jax.experimental import pallas as pl
from jax.experimental.pallas import tpu as pltpu
from jax.sharding import PartitionSpec as P

HD = 64
LANES = 128
BF = jnp.bfloat16
F32 = jnp.float32
BLOCKED = -(2.0**100)
NN = (((1,), (0,)), ((), ()))
NT = (((1,), (1,)), ((), ()))
TN = (((0,), (0,)), ((), ()))

norm_eps = 1e-12
beta_one = 0.9
beta_two = 0.999
adam_eps = 1e-08


def dotf(a, b, dims=NN):
    return lax.dot_general(a, b, dims, preferred_element_type=F32)


def params(mebibytes):
    return pltpu.CompilerParams(vmem_limit_bytes=mebibytes << 20)


def cost(flops, bytes_accessed, transcendentals=0, share=0.05):
    return pl.CostEstimate(
        flops=int(flops * share),
        bytes_accessed=int(bytes_accessed * share),
        transcendentals=int(transcendentals * share),
    )


def shape(dims, dtype):
    return jax.ShapeDtypeStruct(dims, dtype)


VM = pl.BlockSpec(memory_space=pltpu.VMEM)
SM = pl.BlockSpec(memory_space=pltpu.SMEM)


def token_marks(segments, blocks):
    length = segments.shape[1]
    row = lax.broadcasted_iota(jnp.int32, (LANES, length), 0)
    block_of = lax.broadcasted_iota(jnp.int32, (LANES, length), 1) // (length // blocks)
    marks = jnp.where((row == block_of) | (row == blocks + segments), 1.0, 0.0)
    return jnp.transpose(marks).astype(BF)


def head_table(picks, slots, blocks):
    row = lax.broadcasted_iota(jnp.int32, (LANES, LANES), 0)
    col = lax.broadcasted_iota(jnp.int32, (LANES, LANES), 1)
    seen = (jnp.abs(row - col) <= 1) | (row == 0) | (row == blocks - 1)
    seen = seen | (col == 0) | (col == blocks - 1)
    for slot in range(slots):
        seen = seen | (row == picks[slot : slot + 1, :])
    bad_block = (row < blocks) & (col < blocks) & ~seen
    bad_segment = (row >= blocks) & (col >= blocks) & (row != col)
    return jnp.where(bad_block | bad_segment, BLOCKED, 0.0).astype(BF)


def grouped_a(kinds):
    return [
        kind[:, at : at + LANES] for at in range(0, kinds[0].shape[1], LANES) for kind in kinds
    ]


def turned_small(small):
    fill = jnp.zeros((LANES - small.shape[0], small.shape[1]), F32)
    return jnp.transpose(jnp.concatenate([small, fill], axis=0))


def packed_b(attn_ref, ffn_ref, first):
    return jnp.concatenate([ffn_ref[0], ffn_ref[1], attn_ref[:, first:]], axis=1).astype(BF)


def pack_a_kernel(attn_hbm, small_hbm, out_ref, attn_ref, small_ref, sems):
    eighth, width = attn_ref.shape
    replica = lax.axis_index("dp")
    core, low = replica & 1, (replica >> 1) & 1
    rows = pl.ds(pl.multiple_of((2 * core + low) * eighth, eighth), eighth)
    cols = pl.ds(pl.multiple_of(core * 2 * eighth, 2 * eighth), 2 * eighth)
    copies = [pltpu.make_async_copy(small_hbm.at[:, cols], small_ref, sems.at[3])]
    feat = width // 3
    for kind in range(3):
        here = slice(kind * feat, (kind + 1) * feat)
        copies.append(
            pltpu.make_async_copy(attn_hbm.at[rows, here], attn_ref.at[:, here], sems.at[kind])
        )
    for copy in copies:
        copy.start()
    for copy in copies:
        copy.wait()
    small = turned_small(small_ref[...])
    small = jnp.where(low == 0, small[:eighth], small[eighth:])
    kinds = [attn_ref[:, kind * feat : (kind + 1) * feat] for kind in range(3)]
    out_ref[...] = jnp.concatenate(grouped_a(kinds) + [small], axis=1).astype(BF)


def pack_b_kernel(place, attn_ref, ffn_ref, out_ref):
    out_ref[...] = packed_b(attn_ref, ffn_ref, 0)


def pack_own_kernel(attn_ref, ffn_ref, small_ref, a_ref, b_ref):
    feat = attn_ref.shape[1] // 4
    kinds = [attn_ref[:, kind * feat : (kind + 1) * feat] for kind in range(3)]
    parts = grouped_a(kinds) + [turned_small(small_ref[...])]
    a_ref[...] = jnp.concatenate(parts, axis=1).astype(BF)
    b_ref[...] = packed_b(attn_ref, ffn_ref, attn_ref.shape[1] // 4 * 3)


def pack_eighth_a(attn, small):
    eighth = attn.shape[0] // 4
    width = attn.shape[1] // 4 * 3
    anywhere = pl.BlockSpec(memory_space=pl.ANY)
    return pl.pallas_call(
        pack_a_kernel,
        in_specs=[anywhere] * 2,
        out_specs=VM,
        out_shape=shape((eighth, width + LANES), BF),
        scratch_shapes=[
            pltpu.VMEM((eighth, width), F32),
            pltpu.VMEM((small.shape[0], 2 * eighth), F32),
            pltpu.SemaphoreType.DMA((4,)),
        ],
        compiler_params=params(58),
        cost_estimate=cost(1e6, 2 << 20),
        name="pack_eighth_a",
    )(attn, small)


def pack_quarter_b(place, attn, ffn):
    quarter = attn.shape[0] // 2
    feat = attn.shape[1] // 4
    hidden_count = ffn.shape[2]
    width = 2 * hidden_count + feat
    return pl.pallas_call(
        pack_b_kernel,
        grid_spec=pltpu.PrefetchScalarGridSpec(
            num_scalar_prefetch=1,
            grid=(1,),
            in_specs=[
                pl.BlockSpec((quarter, feat), lambda i, place: (place[1], 3)),
                pl.BlockSpec((2, quarter, hidden_count), lambda i, place: (0, place[1], 0)),
            ],
            out_specs=pl.BlockSpec((quarter, width), lambda i, place: (0, 0)),
        ),
        out_shape=shape((quarter, width), BF),
        compiler_params=params(12),
        cost_estimate=cost(1e6, 4 << 20),
        name="pack_quarter_b",
    )(place, attn, ffn)


def pack_own(attn, ffn, small):
    rows = attn.shape[0]
    step = rows // 2
    width_a = attn.shape[1] // 4 * 3 + LANES
    width_b = 2 * ffn.shape[2] + attn.shape[1] // 4
    return pl.pallas_call(
        pack_own_kernel,
        grid=(2,),
        in_specs=[
            pl.BlockSpec((step, attn.shape[1]), lambda i: (i, 0)),
            pl.BlockSpec((2, step, ffn.shape[2]), lambda i: (0, i, 0)),
            pl.BlockSpec((small.shape[0], step), lambda i: (0, i)),
        ],
        out_specs=[
            pl.BlockSpec((step, width_a), lambda i: (i, 0)),
            pl.BlockSpec((step, width_b), lambda i: (i, 0)),
        ],
        out_shape=[shape((rows, width_a), BF), shape((rows, width_b), BF)],
        compiler_params=params(16),
        cost_estimate=cost(1e6, 10 << 20),
        name="pack_own",
    )(attn, ffn, small)


def gathered_eighths(place, own_ref, near_ref, side_ref, far_near_ref, far_side_ref, into, sems):
    half = own_ref.shape[0]
    eighth = near_ref.shape[0]
    shard, core, low = place[0], place[1], place[2]
    other = (1 - shard) * half
    copies = []
    for number, (ref, start, count) in enumerate(
        (
            (own_ref, shard * half, half),
            (near_ref, other + (2 * core + low) * eighth, eighth),
            (side_ref, other + (2 * core + 1 - low) * eighth, eighth),
            (far_near_ref, other + (2 * (1 - core) + low) * eighth, eighth),
            (far_side_ref, other + (2 * (1 - core) + 1 - low) * eighth, eighth),
        )
    ):
        rows = pl.ds(pl.multiple_of(start, eighth), count)
        copies.append(pltpu.make_async_copy(ref, into.at[rows, :], sems.at[number]))
    return copies


def gathered_rows(place, own_ref, near_ref, far_ref, into, sems, cols=slice(None), first=0):
    half = own_ref.shape[0]
    quarter = near_ref.shape[0]
    shard = place[0]
    core = place[1]
    other = (1 - shard) * half
    copies = []
    for number, (ref, start, count) in enumerate(
        (
            (own_ref, shard * half, half),
            (near_ref, other + core * quarter, quarter),
            (far_ref, other + (1 - core) * quarter, quarter),
        )
    ):
        rows = pl.ds(pl.multiple_of(start, quarter), count)
        copies.append(
            pltpu.make_async_copy(ref.at[:, cols], into.at[rows, cols], sems.at[first + number])
        )
    return copies


def attend_kernel(
    place,
    tok_hbm,
    own_ref,
    near_ref,
    side_ref,
    far_near_ref,
    far_side_ref,
    seg_ref,
    picks_ref,
    q_ref,
    k_ref,
    v_ref,
    o_ref,
    lse_ref,
    rows_ref,
    tok_t_hbm,
    marks_ref,
    table_ref,
    tok_ref,
    tok_t_ref,
    w_scr,
    lse_scr,
    even,
    odd,
    sems,
    tok_sems,
    *,
    tile,
    slots,
    blocks,
):
    length = q_ref.shape[0]
    pair = pl.program_id(0)
    lane = lax.broadcasted_iota(jnp.int32, (1, LANES), 1)
    zero = jnp.zeros((), BF)

    eighth_refs = (own_ref, near_ref, side_ref, far_near_ref, far_side_ref)

    @pl.when(pair == 0)
    def _():
        copies = gathered_eighths(place, *eighth_refs, w_scr, sems)
        step = length // 4
        loads = [
            pltpu.make_async_copy(
                tok_hbm.at[n * step : (n + 1) * step, :],
                tok_ref.at[n * step : (n + 1) * step, :],
                tok_sems.at[n],
            )
            for n in range(4)
        ]
        for copy in copies + loads:
            copy.start()
        lse_scr[...] = jnp.zeros_like(lse_scr)
        marks_ref[...] = token_marks(seg_ref[...], blocks)
        for load in loads:
            load.wait()
        tok_t_ref[...] = piece_order(tok_ref, place[1])
        pltpu.make_async_copy(tok_t_ref, tok_t_hbm, tok_sems.at[4]).start()
        for copy in copies:
            copy.wait()
        small = w_scr[:, w_scr.shape[1] - LANES :].astype(F32)
        rows_ref[...] = jnp.transpose(small)[: rows_ref.shape[0], :]

    cols = pl.ds(pl.multiple_of(pair * 3 * LANES, LANES), 3 * LANES)
    here = pl.ds(pl.multiple_of(pair * LANES, LANES), LANES)
    bias = jnp.concatenate(
        [rows_ref[6:7, here], jnp.zeros((1, LANES), F32), rows_ref[7:8, here]], axis=1
    )
    qkv = (dotf(tok_ref[...], w_scr[:, cols]) + bias).astype(BF)
    q_ref[...] = qkv[:, :LANES]
    k_ref[...] = qkv[:, LANES : 2 * LANES]
    v_ref[...] = qkv[:, 2 * LANES :]
    keys, values = [], []
    for head in range(2):
        table_ref[head] = head_table(picks_ref[head], slots, blocks)
        key_marks = dotf(marks_ref[...], table_ref[head]).astype(BF)
        keys.append(jnp.concatenate([k_ref[...], key_marks], axis=1))
        values.append(jnp.where(lane // HD == head, v_ref[...], zero))
    steps = [(at, head) for at in range(0, length, tile) for head in range(2)]
    held = [even, odd]

    def score(index):
        at, head = steps[index]
        rows = pl.ds(at, tile)
        query = jnp.where(lane // HD == head, q_ref[rows, :] * jnp.asarray(HD**-0.5, BF), zero)
        return dotf(jnp.concatenate([query, marks_ref[rows, :]], axis=1), keys[head], NT)

    held[0][...] = score(0)
    first = None
    for index, (at, head) in enumerate(steps):
        rows = pl.ds(at, tile)
        if index + 1 < len(steps):
            held[(index + 1) % 2][...] = score(index + 1)
        now = held[index % 2]
        top = jnp.max(now[...], axis=1, keepdims=True)
        raised = jnp.exp(now[...] - top)
        total = jnp.sum(raised, axis=1, keepdims=True)
        mixed = dotf(raised.astype(BF), values[head]) * (1.0 / total)
        if head == 0:
            first = mixed
        else:
            o_ref[rows, :] = (first + mixed).astype(BF)
        lse_scr[rows, :] = jnp.where(
            lane == 2 * pair + head, top + jnp.log(total), lse_scr[rows, :]
        )

    @pl.when(pair == pl.num_programs(0) - 1)
    def _():
        lse_ref[...] = jnp.transpose(lse_scr[...])[: lse_ref.shape[0], :]
        pltpu.make_async_copy(tok_t_ref, tok_t_hbm, tok_sems.at[4]).wait()


def attend(place, tokens, rows_a, segments, random_blocks):
    length, model = tokens.shape
    blocks, heads, slots = random_blocks.shape[1:]
    picks = jnp.pad(
        random_blocks[0].transpose(1, 2, 0),
        ((0, 0), (0, 8 - slots), (0, LANES - blocks)),
        constant_values=-1,
    )
    width = rows_a[0].shape[1]
    pairs = (width - LANES) // (3 * LANES)
    tile = 256
    whole = lambda dims: pl.BlockSpec(dims, lambda i: (0,) * len(dims))
    anywhere = pl.BlockSpec(memory_space=pl.ANY)
    block = pl.BlockSpec((length, LANES), lambda i: (0, i))
    out_rows = 16
    return pl.pallas_call(
        functools.partial(attend_kernel, tile=tile, slots=slots, blocks=blocks),
        grid=(pairs,),
        in_specs=[
            SM,
            anywhere,
            anywhere,
            anywhere,
            anywhere,
            anywhere,
            anywhere,
            whole((1, length)),
            pl.BlockSpec((2, 8, LANES), lambda i: (i, 0, 0)),
        ],
        out_specs=[
            block,
            block,
            block,
            block,
            whole((out_rows, length)),
            whole((out_rows, model)),
            anywhere,
            whole((length, LANES)),
            pl.BlockSpec((2, LANES, LANES), lambda i: (i, 0, 0)),
        ],
        out_shape=[shape((length, pairs * LANES), BF)] * 4
        + [
            shape((out_rows, length), F32),
            shape((out_rows, model), F32),
            shape((model, length), BF),
            shape((length, LANES), BF),
            shape((heads, LANES, LANES), BF),
        ],
        scratch_shapes=[
            pltpu.VMEM((length, model), BF),
            pltpu.VMEM((model, length), BF),
            pltpu.VMEM((model, width), BF),
            pltpu.VMEM((length, LANES), F32),
            pltpu.VMEM((tile, length), F32),
            pltpu.VMEM((tile, length), F32),
            pltpu.SemaphoreType.DMA((5,)),
            pltpu.SemaphoreType.DMA((5,)),
        ],
        compiler_params=params(58),
        cost_estimate=cost(18e9, 12 << 20, 8 << 20),
        name="attend",
    )(place, tokens, *rows_a, segments, picks)


def attend_back_kernel(
    place,
    q_ref,
    k_ref,
    v_ref,
    do_ref,
    o_ref,
    marks_ref,
    table_ref,
    lse_ref,
    tok_t_hbm,
    mid_ref,
    keep_hbm,
    send_hbm,
    d_ref,
    keep_ref,
    send_ref,
    tok_t_ref,
    dq_sum,
    dv_sum,
    dk_sum,
    bias_scr,
    load_sem,
    out_sems,
    *,
    tile,
):
    length = q_ref.shape[0]
    pair = pl.program_id(0)
    load = pltpu.make_async_copy(tok_t_hbm, tok_t_ref, load_sem)

    @pl.when(pair == 0)
    def _():
        load.start()

    core = place[1]
    lane = lax.broadcasted_iota(jnp.int32, (1, LANES), 1)
    zero = jnp.zeros((), BF)
    scale = jnp.asarray(HD**-0.5, BF)
    prod = do_ref[...].astype(F32) * o_ref[...].astype(F32)
    high = prod.astype(BF)
    low = (prod - high.astype(F32)).astype(BF)
    pick = (
        lax.broadcasted_iota(jnp.int32, (8, LANES), 0)
        == lax.broadcasted_iota(jnp.int32, (8, LANES), 1) // HD
    ).astype(BF)
    inner = dotf(pick, high, NT) + dotf(pick, low, NT)
    keys_t = jnp.transpose(k_ref[...] * scale)
    for head in range(2):
        mine = lane // HD == head
        key_marks = dotf(marks_ref[...], table_ref[head]).astype(BF)
        keys = jnp.concatenate([k_ref[...], key_marks], axis=1)
        log_total = lse_ref[pl.ds(2 * pair + head, 1), :]
        for at in range(0, length, tile):
            here = pl.ds(at, tile)
            query = jnp.where(mine, q_ref[here, :] * scale, zero)
            upstream = jnp.where(mine, do_ref[here, :], zero)
            scores = dotf(keys, jnp.concatenate([query, marks_ref[here, :]], axis=1), NT)
            probs = jnp.exp(scores - log_total[:, at : at + tile])
            grad_probs = dotf(v_ref[...], upstream, NT)
            grad_scores = (probs * (grad_probs - inner[head : head + 1, at : at + tile])).astype(BF)
            grad_v = dotf(probs.astype(BF), upstream)
            grad_k = dotf(grad_scores, query)
            dq_sum[head * HD : (head + 1) * HD, here] = dotf(
                keys_t[head * HD : (head + 1) * HD], grad_scores
            )
            if head == 0 and at == 0:
                dv_sum[...] = grad_v
                dk_sum[...] = grad_k
            else:
                dv_sum[...] += grad_v
                dk_sum[...] += grad_k
    d_ref[:, :LANES] = jnp.transpose(dq_sum[...]).astype(BF)
    d_ref[:, LANES : 2 * LANES] = dk_sum[...].astype(BF)
    d_ref[:, 2 * LANES :] = dv_sum[...].astype(BF)
    outs = (keep_ref, send_ref)
    width = 3 * LANES

    @pl.when(pair == 0)
    def _():
        load.wait()

    def write_out(group, count):
        cols = pl.ds(pl.multiple_of(group * width, LANES), count)
        return [
            pltpu.make_async_copy(source.at[:, cols], into.at[:, cols], out_sems.at[number, group])
            for number, (source, into) in enumerate(((send_ref, send_hbm), (keep_ref, keep_hbm)))
        ]

    result = dotf(tok_t_ref[...], d_ref[...]).astype(BF)
    store_pieces(result, core, outs, pl.ds(pl.multiple_of(pair * width, LANES), width))
    for copy in write_out(pair, width):
        copy.start()
    here = pl.ds(pl.multiple_of(pair * LANES, LANES), LANES)
    bias_scr[0:1, here] = col_sum(d_ref[:, :LANES].astype(F32))
    bias_scr[1:2, here] = col_sum(d_ref[:, 2 * LANES :].astype(F32))

    @pl.when(pair == pl.num_programs(0) - 1)
    def _():
        model = mid_ref.shape[1]
        sums = jnp.concatenate(
            [
                mid_ref[0:6, :],
                bias_scr[0:2, :],
                mid_ref[8:16, :],
                jnp.zeros((LANES - 16, model), F32),
            ],
            axis=0,
        )
        quarter = model // 4
        turned = jnp.transpose(sums)
        kept, sent = [], []
        for r0 in range(2):
            lower = turned[r0 * 2 * quarter : r0 * 2 * quarter + quarter]
            upper = turned[r0 * 2 * quarter + quarter : (r0 + 1) * 2 * quarter]
            kept.append(jnp.where(core == 0, lower, upper))
            sent.append(jnp.where(core == 0, upper, lower))
        total = keep_ref.shape[1]
        store_pieces(
            jnp.concatenate(kept + sent, axis=0).astype(BF), core, outs, slice(total - LANES, total)
        )
        groups = (total - LANES) // width
        last = write_out(groups, LANES)
        for copy in last:
            copy.start()
        for group in range(groups):
            for copy in write_out(group, width):
                copy.wait()
        for copy in last:
            copy.wait()


def attend_back(place, q, k, v, grad_mixed, mixed, marks, table, lse, tok_t, sums):
    length = q.shape[0]
    model = tok_t.shape[0]
    pairs = q.shape[1] // LANES
    width = 3 * LANES
    total = pairs * width + LANES
    whole = lambda dims: pl.BlockSpec(dims, lambda i: (0,) * len(dims))
    block = pl.BlockSpec((length, LANES), lambda i: (0, i))
    return pl.pallas_call(
        functools.partial(attend_back_kernel, tile=512),
        grid=(pairs,),
        in_specs=[SM]
        + [block] * 5
        + [whole(marks.shape), pl.BlockSpec((2, LANES, LANES), lambda i: (i, 0, 0))]
        + [whole(lse.shape), pl.BlockSpec(memory_space=pl.ANY), whole(sums.shape)],
        out_specs=[
            pl.BlockSpec(memory_space=pl.ANY),
            pl.BlockSpec(memory_space=pl.ANY),
            pl.BlockSpec((length, width), lambda i: (0, i)),
        ],
        out_shape=[
            shape((model // 2, total), BF),
            shape((model // 2, total), BF),
            shape((length, pairs * width), BF),
        ],
        scratch_shapes=[
            pltpu.VMEM((model // 2, total), BF),
            pltpu.VMEM((model // 2, total), BF),
            pltpu.VMEM((model, length), BF),
            pltpu.VMEM((LANES, length), F32),
            pltpu.VMEM((length, LANES), F32),
            pltpu.VMEM((length, LANES), F32),
            pltpu.VMEM((8, model), F32),
            pltpu.SemaphoreType.DMA,
            pltpu.SemaphoreType.DMA((2, pairs + 1)),
        ],
        compiler_params=params(56),
        cost_estimate=cost(30e9, 10 << 20, 8 << 20, 1.0),
        name="attend_back",
    )(place, q, k, v, grad_mixed, mixed, marks, table, lse, tok_t, sums)


def piece_order(lhs_ref, core):
    quarter = lhs_ref.shape[1] // 4
    cols = []
    for target in (core, 1 - core):
        for half in range(2):
            start = pl.multiple_of(half * 2 * quarter + target * quarter, quarter)
            cols.append(lhs_ref[:, pl.ds(start, quarter)])
    return jnp.transpose(jnp.concatenate(cols, axis=1))


def store_pieces(result, core, outs, cols):
    quarter = result.shape[0] // 4
    piece = quarter // 4
    for which, target in enumerate((core, 1 - core)):
        for r0 in range(2):
            for r2 in range(2):
                for r3 in range(2):
                    at = which * 2 * quarter + r0 * quarter + r2 * 2 * piece + r3 * piece
                    spot = jnp.where(target == 0, r0 * 4 + r2 * 2 + r3, r3 * 4 + r2 * 2 + r0)
                    rows = pl.ds(pl.multiple_of(spot * piece, piece), piece)
                    outs[which][rows, cols] = result[at : at + piece, :]


def weight_grad(lhs_t, rhs_ref, core, outs, first, tile=512):
    for at in range(0, rhs_ref.shape[1], tile):
        result = dotf(lhs_t, rhs_ref[:, at : at + tile]).astype(BF)
        store_pieces(result, core, outs, slice(first + at, first + at + tile))


def normed(hidden):
    center = hidden - jnp.mean(hidden, axis=-1, keepdims=True)
    spread = jnp.mean(center * center, axis=-1, keepdims=True)
    rate = lax.rsqrt(spread + norm_eps)
    return center * rate, rate


def norm_back(grad, unit, rate):
    return rate * (
        grad
        - jnp.mean(grad, axis=-1, keepdims=True)
        - unit * jnp.mean(grad * unit, axis=-1, keepdims=True)
    )


def col_sum(values):
    return jnp.sum(values, axis=0, keepdims=True)


def middle_kernel(
    place,
    rows_ref,
    tok_hbm,
    cot_hbm,
    mixed_hbm,
    own_hbm,
    near_hbm,
    far_hbm,
    out_hbm,
    dh_hbm,
    do_hbm,
    keep_hbm,
    send_hbm,
    sums_ref,
    tok_ref,
    cot_ref,
    mixed_ref,
    out_ref,
    dh_ref,
    do_ref,
    keep_ref,
    send_ref,
    w_scr,
    act_scr,
    du_scr,
    z_scr,
    df_scr,
    da_scr,
    sems,
    out_sems,
    *,
    tile,
):
    length, model = tok_ref.shape
    core = place[1]
    hidden_count = act_scr.shape[1]
    w_up = slice(0, hidden_count)
    w_down = slice(hidden_count, 2 * hidden_count)
    w_out = slice(2 * hidden_count, w_scr.shape[1])
    waits = {}
    number = 0
    for name, sources in (
        ("out", w_out),
        (0, ((mixed_hbm, mixed_ref), (tok_hbm, tok_ref))),
        ("up", w_up),
        ("down", w_down),
        ("cot", ((cot_hbm, cot_ref),)),
        *((at, ((mixed_hbm, mixed_ref), (tok_hbm, tok_ref))) for at in range(tile, length, tile)),
    ):
        if isinstance(sources, slice):
            copies = gathered_rows(
                place, own_hbm, near_hbm, far_hbm, w_scr, sems, sources, number
            )
        else:
            rows = slice(None) if name == "cot" else slice(name, name + tile)
            copies = [
                pltpu.make_async_copy(source.at[rows, :], into.at[rows, :], sems.at[number + n])
                for n, (source, into) in enumerate(sources)
            ]
        number += len(copies)
        for copy in copies:
            copy.start()
        waits[name] = copies

    def ready(name):
        for copy in waits.pop(name, ()):
            copy.wait()

    pending = []

    def write_out(source, into):
        copy = pltpu.make_async_copy(source, into, out_sems.at[len(pending)])
        copy.start()
        pending.append(copy)

    row = lambda number: rows_ref[number : number + 1, :]
    bias_up = jnp.concatenate([row(8), row(9), row(10), row(11)], axis=1)
    sums = [jnp.zeros((1, model), F32)] * 6
    sum_up = jnp.zeros((1, hidden_count), F32)
    for at in range(0, length, tile):
        here = pl.ds(at, tile)
        ready("out")
        ready(at)
        attn_out = dotf(mixed_ref[here, :], w_scr[:, w_out], NT) + row(4)
        unit_one, rate_one = normed(tok_ref[here, :].astype(F32) + attn_out)
        z_one = unit_one * row(0) + row(1)
        z_low = z_one.astype(BF)
        z_scr[here, :] = z_low
        ready("up")
        up = dotf(z_low, w_scr[:, w_up]) + bias_up
        below = 0.5 * (1.0 + lax.erf(up * (0.5**0.5)))
        slope = below + up * (jnp.exp(-0.5 * up * up) * (1.0 / (2.0 * 3.141592653589793) ** 0.5))
        active = (up * below).astype(BF)
        act_scr[here, :] = active
        ready("down")
        ffn_out = dotf(active, w_scr[:, w_down], NT) + row(5)
        unit_two, rate_two = normed(z_one + ffn_out)
        out_ref[here, :] = (unit_two * row(2) + row(3)).astype(BF)
        ready("cot")
        upstream = cot_ref[here, :].astype(F32)
        grad_two = norm_back(upstream * row(2), unit_two, rate_two)
        down_low = grad_two.astype(BF)
        df_scr[here, :] = down_low
        grad_up = (dotf(down_low, w_scr[:, w_down]) * slope).astype(BF)
        du_scr[here, :] = grad_up
        grad_z = grad_two + dotf(grad_up, w_scr[:, w_up], NT)
        grad_one = norm_back(grad_z * row(0), unit_one, rate_one)
        dh_ref[here, :] = grad_one
        attn_low = grad_one.astype(BF)
        da_scr[here, :] = attn_low
        do_ref[here, :] = dotf(attn_low, w_scr[:, w_out]).astype(BF)
        for source, into in ((out_ref, out_hbm), (dh_ref, dh_hbm), (do_ref, do_hbm)):
            write_out(source.at[here, :], into.at[here, :])
        parts = (
            grad_z * unit_one,
            grad_z,
            upstream * unit_two,
            upstream,
            attn_low.astype(F32),
            down_low.astype(F32),
        )
        sums = [a + col_sum(b) for a, b in zip(sums, parts)]
        sum_up = sum_up + col_sum(grad_up.astype(F32))
    for number in range(6):
        sums_ref[number : number + 1, :] = sums[number]
    sums_ref[6:8, :] = jnp.zeros((2, model), F32)
    for number in range(4):
        sums_ref[8 + number : 9 + number, :] = sum_up[:, number * model : (number + 1) * model]
    sums_ref[12:16, :] = jnp.zeros((4, model), F32)
    outs = (keep_ref, send_ref)
    for lhs, rhs, cols in (
        (z_scr, du_scr, w_up),
        (df_scr, act_scr, w_down),
        (da_scr, mixed_ref, w_out),
    ):
        weight_grad(piece_order(lhs, core), rhs, core, outs, cols.start)
        for source, into in ((send_ref, send_hbm), (keep_ref, keep_hbm)):
            write_out(source.at[:, cols], into.at[:, cols])
    for copy in pending:
        copy.wait()


def middle(place, tokens, cotangent, mixed, rows, own, near, far):
    length, model = tokens.shape
    width = own.shape[1]
    hidden_count = (width - mixed.shape[1]) // 2
    tile = 512
    anywhere = pl.BlockSpec(memory_space=pl.ANY)
    outs = [
        shape((length, model), BF),
        shape((length, model), F32),
        shape((length, mixed.shape[1]), BF),
        shape((model // 2, width), BF),
        shape((model // 2, width), BF),
    ]
    vmem = lambda x: pltpu.VMEM(x.shape, x.dtype)
    return pl.pallas_call(
        functools.partial(middle_kernel, tile=tile),
        in_specs=[SM, VM] + [anywhere] * 5 + [VM],
        out_specs=[anywhere] * 5 + [VM],
        out_shape=outs + [shape((16, model), F32)],
        scratch_shapes=[vmem(x) for x in (tokens, cotangent, mixed, *outs)]
        + [
            pltpu.VMEM((model, width), BF),
            pltpu.VMEM((length, hidden_count), BF),
            pltpu.VMEM((length, hidden_count), BF),
            pltpu.VMEM((length, model), BF),
            pltpu.VMEM((length, model), BF),
            pltpu.VMEM((length, model), BF),
            pltpu.SemaphoreType.DMA((10 + 2 * (length // tile),)),
            pltpu.SemaphoreType.DMA((3 * (length // tile) + 6,)),
        ],
        compiler_params=params(58),
        cost_estimate=cost(16e9, 16 << 20, 4 << 20, 1.0),
        name="middle",
    )(place, rows, tokens, cotangent, mixed, own, near, far)


def input_grad_kernel(
    place, dh_ref, d_ref, own_ref, near_ref, side_ref, far_near_ref, far_side_ref, out_ref, w_scr, sems
):
    eighth_refs = (own_ref, near_ref, side_ref, far_near_ref, far_side_ref)
    width = d_ref.shape[1]

    @pl.when(pl.program_id(0) == 0)
    def _():
        copies = gathered_eighths(place, *eighth_refs, w_scr, sems)
        for copy in copies:
            copy.start()
        for copy in copies:
            copy.wait()

    out_ref[...] = (dh_ref[...] + dotf(d_ref[...], w_scr[:, :width], NT)).astype(BF)


def input_gradient(place, dh, d, rows_a):
    length, model = dh.shape
    tile = 256
    anywhere = pl.BlockSpec(memory_space=pl.ANY)
    rows = lambda width: pl.BlockSpec((tile, width), lambda i: (i, 0))
    return pl.pallas_call(
        input_grad_kernel,
        grid=(length // tile,),
        in_specs=[SM, rows(model), rows(d.shape[1])] + [anywhere] * 5,
        out_specs=rows(model),
        out_shape=shape((length, model), BF),
        scratch_shapes=[pltpu.VMEM((model, rows_a[0].shape[1]), BF), pltpu.SemaphoreType.DMA((5,))],
        compiler_params=params(16),
        cost_estimate=cost(2 * length * model * d.shape[1], 8 << 20),
        name="input_gradient",
    )(place, dh, d, *rows_a)


def add_low(a, b):
    return (a.astype(F32) + b.astype(F32)).astype(BF)


def add_parts_kernel(place, *refs):
    total = refs[0][...].astype(F32)
    for ref in refs[1:-1]:
        total = total + ref[...].astype(F32)
    refs[-1][...] = total.astype(BF)


def add_parts(place, parts, give):
    rows = min(part.shape[0] for part in parts)
    rows = rows // 2 if give else rows
    width = parts[0].shape[1]

    def pick(part):
        if part.shape[0] == rows:
            return pl.BlockSpec((rows, width), lambda i, place: (0, 0))
        return pl.BlockSpec((rows, width), lambda i, place: (1 - place[6] if give else place[6], 0))

    return pl.pallas_call(
        add_parts_kernel,
        grid_spec=pltpu.PrefetchScalarGridSpec(
            num_scalar_prefetch=1,
            grid=(1,),
            in_specs=[pick(part) for part in parts],
            out_specs=pl.BlockSpec((rows, width), lambda i, place: (0, 0)),
        ),
        out_shape=shape((rows, width), BF),
        compiler_params=params(8),
        cost_estimate=cost(len(parts) * rows * width, 2 * len(parts) * rows * width),
        name="add_parts",
    )(place, *parts)


def flip(count, bit):
    return [(i, i ^ (1 << bit)) for i in range(count)]


def mixed_flip(count, even, odd):
    return [(i, i ^ (1 << (odd if (i >> 1) & 1 else even))) for i in range(2 * count)]


STEPS = ((0, 2), (2, 3), (3, 0))


def mixed_mask(count, mask):
    pairs = []
    for i in range(2 * count):
        partner = i
        for bit, step in zip((2, 1), STEPS):
            if mask & bit:
                partner ^= 1 << step[(i >> 1) & 1]
        pairs.append((i, partner))
    return pairs


def split_kernel(place, keep_ref, got_ref, *outs):
    piece = outs[0].shape[0]
    mine = place[3] * 2 + place[4]
    for mask, out in enumerate(outs):
        rows = pl.ds(pl.multiple_of((mine ^ mask) * piece, piece), piece)
        out[...] = add_low(keep_ref[rows, :], got_ref[rows, :])


def swap_two(value, count, mask):
    return lax.ppermute(value, ("dp", "shard"), mixed_mask(count, mask))


def split(place, keep, got):
    rows, width = keep.shape
    steps = 4 if width % (4 * LANES) == 0 else 1
    step = width // steps
    whole = pl.BlockSpec((rows, step), lambda i: (0, i))
    part = pl.BlockSpec((rows // 4, step), lambda i: (0, i))
    return pl.pallas_call(
        split_kernel,
        grid=(steps,),
        in_specs=[SM, whole, whole],
        out_specs=[part] * 4,
        out_shape=[shape((rows // 4, width), BF)] * 4,
        compiler_params=params(16),
        cost_estimate=cost(rows * width, 6 * rows * width),
        name="split",
    )(place, keep, got)


def swap_core(value, count):
    return lax.ppermute(value, "dp", flip(count, 0))


def swap_mixed(value, count, step):
    return lax.ppermute(value, ("dp", "shard"), mixed_flip(count, *step))


def swap_bit(value, count, bit):
    return lax.ppermute(value, "dp", flip(count, bit))


def after(value, *others):
    return lax.optimization_barrier((value,) + others)[0]


def adam_values(scalars, weight_ref, mean_ref, square_ref, grad, decay, outs):
    weight = weight_ref[...]
    mean_out = beta_one * mean_ref[...] + (1.0 - beta_one) * grad
    square_out = beta_two * square_ref[...] + (1.0 - beta_two) * grad * grad
    mean_hat = mean_out * scalars[2]
    square_hat = square_out * scalars[3]
    weight_out = weight - scalars[0] * (
        mean_hat / (jnp.sqrt(square_hat) + adam_eps) + decay * weight
    )
    outs[0][...] = weight_out
    outs[1][...] = mean_out
    outs[2][...] = square_out
    outs[3][...] = weight_out.astype(BF)


def piece_block(place, own, flips):
    bit2, bit3 = (place[4], place[5]) if own else (place[5], place[4])
    core = place[1] if own else 1 - place[1]
    return core * 4 + (bit2 ^ (flips >> 1)) * 2 + (bit3 ^ (flips & 1))


def chosen(index, values):
    result = values[-1]
    for number in range(len(values) - 2, -1, -1):
        result = jnp.where(index == number, values[number], result)
    return result


def adam_ffn_kernel(place, scalars, *refs, count):
    step = pl.program_id(0)
    stack, _, width = refs[count].shape
    for number in range(count):

        @pl.when(step == number)
        def _():
            grad = jnp.stack(
                [refs[number][:, w * width : (w + 1) * width].astype(F32) for w in range(stack)]
            )
            adam_values(scalars, *refs[count : count + 3], grad, scalars[1], refs[-4:])


def adam_ffn(place, scalars, pieces, state, before):
    count = len(pieces)
    stack, rows, width = state[0].shape
    step = rows // 8
    grads = [piece[0] for piece in pieces]
    take = pl.BlockSpec((step, stack * width), lambda p, place, sc: (0, 0))
    block = pl.BlockSpec(
        (stack, step, width),
        lambda p, place, sc: (0, chosen(p, [piece_block(place, *x[1:]) for x in pieces]), 0),
    )
    before = list(before or ())
    return pl.pallas_call(
        functools.partial(adam_ffn_kernel, count=count),
        grid_spec=pltpu.PrefetchScalarGridSpec(
            num_scalar_prefetch=2,
            grid=(count,),
            in_specs=[take] * count + [block] * 3 + [pl.BlockSpec(memory_space=pl.ANY)] * len(before),
            out_specs=[block] * 4,
        ),
        out_shape=[shape(state[0].shape, F32)] * 3 + [shape(state[0].shape, BF)],
        input_output_aliases={5 + count + n: n for n in range(len(before))},
        compiler_params=params(24),
        cost_estimate=cost(20 * count * step * width, 28 * count * step * width),
        name="adam_ffn",
    )(place, scalars, *grads, *state, *before)


def adam_attn_kernel(place, scalars, *refs, count, orders, small):
    grads, outer, state = refs[:count], refs[count : 2 * count], refs[2 * count : 2 * count + 3]
    rest = refs[2 * count + 3 :]
    step = pl.program_id(0)
    if small:
        little, (sw, sm, ss), rest = rest[:small], rest[small : small + 3], rest[small + 3 + 4 :]
        outs, small_outs, scr = rest[:4], rest[4:8], rest[8]

        @pl.when(step == 0)
        def _():
            for ref, order in zip(little, orders):
                rows = ref.shape[0]
                where = pl.ds(pl.multiple_of(piece_block(place, *order) * rows, rows), rows)
                scr[where, :] = ref[...].astype(F32)
            turned = jnp.transpose(scr[...])[: sw.shape[0], :]
            adam_values(scalars, sw, sm, ss, turned, 0.0 * scalars[1], small_outs)
    else:
        outs = rest[-4:]
    for number in range(count):

        @pl.when(step == number)
        def _():
            grad = grads[number][...].astype(F32)
            pairs = grad.shape[1] // (3 * LANES)
            parts = [
                grad[:, p * 3 * LANES + kind * LANES : p * 3 * LANES + (kind + 1) * LANES]
                for kind in range(3)
                for p in range(pairs)
            ]
            parts.append(outer[number][...].astype(F32))
            adam_values(scalars, *state, jnp.concatenate(parts, axis=1), scalars[1], outs)


def adam_attn(place, scalars, pieces, pieces_b, state, before, every=None, small=None):
    count = len(pieces)
    rows, width = state[0].shape
    step = rows // 8
    out_width = width // 4
    grads = [piece[0] for piece in pieces]
    outer = [piece[0] for piece in pieces_b]
    last = outer[0].shape[1] // out_width - 1
    block = pl.BlockSpec(
        (step, width),
        lambda p, place, sc: (chosen(p, [piece_block(place, *x[1:]) for x in pieces]), 0),
    )
    anywhere = pl.BlockSpec(memory_space=pl.ANY)
    in_specs = [pl.BlockSpec(grads[0].shape, lambda p, place, sc: (0, 0))] * count
    in_specs += [pl.BlockSpec((step, out_width), lambda p, place, sc: (0, last))] * count
    in_specs += [block] * 3
    operands = [place, scalars, *grads, *outer, *state]
    out_specs = [block] * 4
    out_shape = [shape(state[0].shape, F32)] * 3 + [shape(state[0].shape, BF)]
    scratch = []
    if small:
        whole = pl.BlockSpec(small[0].shape, lambda p, place, sc: (0, 0))
        at = grads[0].shape[1] // LANES - 1
        in_specs += [pl.BlockSpec((step, LANES), lambda p, place, sc: (0, at))] * len(every)
        in_specs += [whole] * 3
        operands += [piece[0] for piece in every] + list(small)
        out_specs += [whole] * 4
        out_shape += [shape(small[0].shape, F32)] * 3 + [shape(small[0].shape, BF)]
        scratch = [pltpu.VMEM((rows, LANES), F32)]
    before = list(before or ())
    aliases = {len(operands) + n: n for n in range(len(before))}
    return pl.pallas_call(
        functools.partial(
            adam_attn_kernel,
            count=count,
            orders=[piece[1:] for piece in every or ()],
            small=len(every or ()),
        ),
        grid_spec=pltpu.PrefetchScalarGridSpec(
            num_scalar_prefetch=2,
            grid=(count,),
            in_specs=in_specs + [anywhere] * len(before),
            out_specs=out_specs,
            scratch_shapes=scratch,
        ),
        out_shape=out_shape,
        input_output_aliases=aliases,
        compiler_params=params(24),
        cost_estimate=cost(20 * count * step * width, 28 * count * step * width),
        name="adam_attn",
    )(*operands, *before)


def from_neighbour(value):
    return lax.ppermute(value, "shard", [(0, 1), (1, 0)])


def local(
    count,
    tokens,
    cotangent,
    segments,
    random_blocks,
    step_count,
    adam_rates,
    attn_master,
    attn_mean,
    attn_square,
    ffn_master,
    ffn_mean,
    ffn_square,
    small_master,
    small_mean,
    small_square,
):
    replica = lax.axis_index("dp")
    shard = lax.axis_index("shard")
    core, low, high = replica & 1, (replica >> 1) & 1, (replica >> 2) & 1
    even = core == 0
    place = jnp.stack(
        [
            shard,
            core,
            low,
            jnp.where(even, shard, low),
            jnp.where(even, low, high),
            jnp.where(even, high, low),
            jnp.where(even, high, shard),
        ]
    ).astype(jnp.int32)
    pairs = attn_master.shape[1] // 4 // LANES
    near_a = from_neighbour(pack_eighth_a(attn_master, small_master))
    quarter_b = pack_quarter_b(place, attn_master, ffn_master)
    near_a = after(near_a, quarter_b)
    near_b = from_neighbour(after(quarter_b, near_a))
    side_a = swap_bit(near_a, count, 1)
    own_a, own_b = pack_own(attn_master, ffn_master, small_master)
    side_a = after(side_a, own_a)
    rows_a = (own_a, near_a, side_a, swap_core(near_a, count), swap_core(side_a, count))
    q, k, v, mixed, lse, rows, tok_t, marks, table = attend(
        place, tokens, rows_a, segments, random_blocks
    )
    far_b = swap_core(after(near_b, lse), count)
    layer_out, dh, grad_mixed, keep_b, send_b, sums = middle(
        place, tokens, cotangent, mixed, rows, own_b, near_b, far_b
    )
    parts_b = list(split(place, keep_b, swap_core(send_b, count)))
    parts_b = parts_b[:1] + [swap_two(parts_b[mask], count, mask) for mask in (1, 2, 3)]
    keep_a, send_a, d = attend_back(
        place, q, k, v, after(grad_mixed, parts_b[0]), mixed, marks, table, lse, tok_t, sums
    )
    got_a = swap_core(send_a, count)
    parts_b = parts_b[:1] + [after(part, d) for part in parts_b[1:]]
    got_b = swap_mixed(add_parts(place, parts_b, True), count, STEPS[2])

    step_value = step_count[0].astype(F32)
    scalars = jnp.stack(
        [
            adam_rates[0],
            adam_rates[1],
            1.0 / (1.0 - beta_one**step_value),
            1.0 / (1.0 - beta_two**step_value),
        ]
    )
    ffn_state = (ffn_master, ffn_mean, ffn_square)
    attn_state = (attn_master, attn_mean, attn_square)
    small_state = (small_master, small_mean, small_square)
    bits = [bit for bit in range(3, count.bit_length() - 1)]

    parts_a = list(split(place, keep_a, got_a))
    parts_a = parts_a[:1] + [swap_two(parts_a[mask], count, mask) for mask in (1, 2, 3)]
    total_b = add_parts(place, parts_b + [after(got_b, parts_a[0])], False)
    got_b = swap_bit(total_b, count, bits[0])
    input_grad = input_gradient(place, after(dh, total_b), d, rows_a)
    parts_a = parts_a[:1] + [after(part, input_grad) for part in parts_a[1:]]
    got_a = swap_mixed(add_parts(place, parts_a, True), count, STEPS[2])
    total_a = add_parts(place, parts_a + [got_a], False)
    got_a = swap_bit(total_a, count, bits[0])
    total_b = add_low(total_b, after(got_b, total_a))
    for bit in bits[1:]:
        total_b = add_low(total_b, swap_bit(total_b, count, bit))
    first, second = (3, 2), (2, 3)

    def wave(values, flips):
        return [(v, True, f) for v, f in zip(values, flips)] + [
            (swap_core(v, count), False, f) for v, f in zip(values, flips)
        ]

    b_one = wave([total_b], [0])
    got_b = [swap_mixed(total_b, count, first), swap_mixed(total_b, count, second)]
    total_a = add_low(total_a, after(got_a, total_b))
    for bit in bits[1:]:
        total_a = add_low(total_a, swap_bit(total_a, count, bit))
    ffn_new = adam_ffn(place, scalars, b_one, ffn_state, None)
    a_one = wave([total_a], [0])
    got_a = [swap_mixed(total_a, count, first), swap_mixed(total_a, count, second)]
    got_b = [after(piece, ffn_new[0], total_a) for piece in got_b]
    b_two = wave(got_b, [1, 2])
    got_b = swap_mixed(got_b[0], count, second)
    attn_new = adam_attn(place, scalars, a_one, b_one, attn_state, None)
    ffn_new = adam_ffn(place, scalars, b_two, ffn_state, ffn_new)
    got_a = [after(piece, attn_new[0]) for piece in got_a]
    a_two = wave(got_a, [1, 2])
    got_a = swap_mixed(got_a[0], count, second)
    b_three = wave([after(got_b, ffn_new[0])], [3])
    attn_new = adam_attn(place, scalars, a_two, b_two, attn_state, attn_new)
    a_three = wave([after(got_a, attn_new[0])], [3])
    ffn_new = adam_ffn(place, scalars, b_three, ffn_state, ffn_new)
    attn_new = adam_attn(
        place,
        scalars,
        a_three,
        b_three,
        attn_state,
        attn_new,
        a_one + a_two + a_three,
        small_state,
    )
    return (layer_out, input_grad) + tuple(attn_new[:4]) + tuple(ffn_new) + tuple(attn_new[4:])


def solution(mesh):
    tokens_in = P(("dp", "shard"), None)
    rows_in = P("shard", None)
    stack_in = P(None, "shard", None)
    cols_in = P(None, "shard")
    placed = (
        (tokens_in,) * 3
        + (P(("dp", "shard"), None, None, None), P(), P())
        + (rows_in,) * 3
        + (stack_in,) * 3
        + (cols_in,) * 3
    )
    return jax.shard_map(
        functools.partial(local, mesh.shape["dp"]),
        mesh=mesh,
        in_specs=placed,
        out_specs=(tokens_in,) * 2 + (rows_in,) * 4 + (stack_in,) * 4 + (cols_in,) * 4,
        check_vma=False,
    )
```

```python
import functools

import jax
import jax.numpy as jnp
from jax import lax
from jax.experimental import pallas as pl
from jax.experimental.pallas import tpu as pltpu
from jax.sharding import PartitionSpec as P

HD = 64
LANES = 128
PARAMS = 16
BF = jnp.bfloat16
F32 = jnp.float32
BLOCKED = -(2.0**100)
NN = (((1,), (0,)), ((), ()))
NT = (((1,), (1,)), ((), ()))
TN = (((0,), (0,)), ((), ()))

norm_eps = 1e-12
beta_one = 0.9
beta_two = 0.999
adam_eps = 1e-08


def dotf(a, b, dims=NN):
    return lax.dot_general(a, b, dims, preferred_element_type=F32)


def params(mebibytes):
    return pltpu.CompilerParams(vmem_limit_bytes=mebibytes << 20)


def cost(flops, bytes_accessed, transcendentals=0, share=0.05):
    return pl.CostEstimate(
        flops=int(flops * share),
        bytes_accessed=int(bytes_accessed * share),
        transcendentals=int(transcendentals * share),
    )


def shape(dims, dtype):
    return jax.ShapeDtypeStruct(dims, dtype)


VM = pl.BlockSpec(memory_space=pltpu.VMEM)
SM = pl.BlockSpec(memory_space=pltpu.SMEM)


def token_marks(segments, blocks):
    length = segments.shape[1]
    row = lax.broadcasted_iota(jnp.int32, (LANES, length), 0)
    block_of = lax.broadcasted_iota(jnp.int32, (LANES, length), 1) // (length // blocks)
    marks = jnp.where((row == block_of) | (row == blocks + segments), 1.0, 0.0)
    return jnp.transpose(marks).astype(BF)


def head_table(picks, slots, blocks):
    row = lax.broadcasted_iota(jnp.int32, (LANES, LANES), 0)
    col = lax.broadcasted_iota(jnp.int32, (LANES, LANES), 1)
    seen = (jnp.abs(row - col) <= 1) | (row == 0) | (row == blocks - 1)
    seen = seen | (col == 0) | (col == blocks - 1)
    for slot in range(slots):
        seen = seen | (row == picks[slot : slot + 1, :])
    bad_block = (row < blocks) & (col < blocks) & ~seen
    bad_segment = (row >= blocks) & (col >= blocks) & (row != col)
    return jnp.where(bad_block | bad_segment, BLOCKED, 0.0).astype(BF)


def grouped_a(kinds):
    return [
        kind[:, at : at + LANES] for at in range(0, kinds[0].shape[1], LANES) for kind in kinds
    ]


def turned_small(small):
    fill = jnp.zeros((LANES - small.shape[0], small.shape[1]), F32)
    return jnp.transpose(jnp.concatenate([small, fill], axis=0))


def packed_b(attn_ref, ffn_ref, first):
    return jnp.concatenate([ffn_ref[0], ffn_ref[1], attn_ref[:, first:]], axis=1).astype(BF)


def pack_a_kernel(attn_hbm, small_hbm, out_ref, attn_ref, small_ref, sems):
    eighth, width = attn_ref.shape
    replica = lax.axis_index("dp")
    core, low = replica & 1, (replica >> 1) & 1
    rows = pl.ds(pl.multiple_of((2 * core + low) * eighth, eighth), eighth)
    cols = pl.ds(pl.multiple_of(core * 2 * eighth, 2 * eighth), 2 * eighth)
    copies = [pltpu.make_async_copy(small_hbm.at[:, cols], small_ref, sems.at[3])]
    feat = width // 3
    for kind in range(3):
        here = slice(kind * feat, (kind + 1) * feat)
        copies.append(
            pltpu.make_async_copy(attn_hbm.at[rows, here], attn_ref.at[:, here], sems.at[kind])
        )
    for copy in copies:
        copy.start()
    for copy in copies:
        copy.wait()
    small = turned_small(small_ref[...])
    small = jnp.where(low == 0, small[:eighth], small[eighth:])
    kinds = [attn_ref[:, kind * feat : (kind + 1) * feat] for kind in range(3)]
    out_ref[...] = jnp.concatenate(grouped_a(kinds) + [small], axis=1).astype(BF)


def pack_b_kernel(place, attn_ref, ffn_ref, out_ref):
    out_ref[...] = packed_b(attn_ref, ffn_ref, 0)


def pack_own_kernel(attn_ref, ffn_ref, small_ref, a_ref, b_ref):
    feat = attn_ref.shape[1] // 4
    kinds = [attn_ref[:, kind * feat : (kind + 1) * feat] for kind in range(3)]
    parts = grouped_a(kinds) + [turned_small(small_ref[...])]
    a_ref[...] = jnp.concatenate(parts, axis=1).astype(BF)
    b_ref[...] = packed_b(attn_ref, ffn_ref, attn_ref.shape[1] // 4 * 3)


def pack_eighth_a(attn, small):
    eighth = attn.shape[0] // 4
    width = attn.shape[1] // 4 * 3
    anywhere = pl.BlockSpec(memory_space=pl.ANY)
    return pl.pallas_call(
        pack_a_kernel,
        in_specs=[anywhere] * 2,
        out_specs=VM,
        out_shape=shape((eighth, width + LANES), BF),
        scratch_shapes=[
            pltpu.VMEM((eighth, width), F32),
            pltpu.VMEM((small.shape[0], 2 * eighth), F32),
            pltpu.SemaphoreType.DMA((4,)),
        ],
        compiler_params=params(58),
        cost_estimate=cost(1e6, 2 << 20),
        name="pack_eighth_a",
    )(attn, small)


def pack_quarter_b(place, attn, ffn):
    quarter = attn.shape[0] // 2
    feat = attn.shape[1] // 4
    hidden_count = ffn.shape[2]
    width = 2 * hidden_count + feat
    return pl.pallas_call(
        pack_b_kernel,
        grid_spec=pltpu.PrefetchScalarGridSpec(
            num_scalar_prefetch=1,
            grid=(1,),
            in_specs=[
                pl.BlockSpec((quarter, feat), lambda i, place: (place[1], 3)),
                pl.BlockSpec((2, quarter, hidden_count), lambda i, place: (0, place[1], 0)),
            ],
            out_specs=pl.BlockSpec((quarter, width), lambda i, place: (0, 0)),
        ),
        out_shape=shape((quarter, width), BF),
        compiler_params=params(12),
        cost_estimate=cost(1e6, 4 << 20),
        name="pack_quarter_b",
    )(place, attn, ffn)


def pack_own(attn, ffn, small):
    rows = attn.shape[0]
    step = rows // 2
    width_a = attn.shape[1] // 4 * 3 + LANES
    width_b = 2 * ffn.shape[2] + attn.shape[1] // 4
    return pl.pallas_call(
        pack_own_kernel,
        grid=(2,),
        in_specs=[
            pl.BlockSpec((step, attn.shape[1]), lambda i: (i, 0)),
            pl.BlockSpec((2, step, ffn.shape[2]), lambda i: (0, i, 0)),
            pl.BlockSpec((small.shape[0], step), lambda i: (0, i)),
        ],
        out_specs=[
            pl.BlockSpec((step, width_a), lambda i: (i, 0)),
            pl.BlockSpec((step, width_b), lambda i: (i, 0)),
        ],
        out_shape=[shape((rows, width_a), BF), shape((rows, width_b), BF)],
        compiler_params=params(16),
        cost_estimate=cost(1e6, 10 << 20),
        name="pack_own",
    )(attn, ffn, small)


def gathered_eighths(place, own_ref, near_ref, side_ref, far_near_ref, far_side_ref, into, sems):
    half = own_ref.shape[0]
    eighth = near_ref.shape[0]
    shard, core, low = place[0], place[1], place[2]
    other = (1 - shard) * half
    copies = []
    for number, (ref, start, count) in enumerate(
        (
            (own_ref, shard * half, half),
            (near_ref, other + (2 * core + low) * eighth, eighth),
            (side_ref, other + (2 * core + 1 - low) * eighth, eighth),
            (far_near_ref, other + (2 * (1 - core) + low) * eighth, eighth),
            (far_side_ref, other + (2 * (1 - core) + 1 - low) * eighth, eighth),
        )
    ):
        rows = pl.ds(pl.multiple_of(start, eighth), count)
        copies.append(pltpu.make_async_copy(ref, into.at[rows, :], sems.at[number]))
    return copies


def gathered_rows(place, own_ref, near_ref, far_ref, into, sems, cols=slice(None), first=0):
    half = own_ref.shape[0]
    quarter = near_ref.shape[0]
    shard = place[0]
    core = place[1]
    other = (1 - shard) * half
    copies = []
    for number, (ref, start, count) in enumerate(
        (
            (own_ref, shard * half, half),
            (near_ref, other + core * quarter, quarter),
            (far_ref, other + (1 - core) * quarter, quarter),
        )
    ):
        rows = pl.ds(pl.multiple_of(start, quarter), count)
        copies.append(
            pltpu.make_async_copy(ref.at[:, cols], into.at[rows, cols], sems.at[first + number])
        )
    return copies


def attend_kernel(
    place,
    tok_hbm,
    own_ref,
    near_ref,
    side_ref,
    far_near_ref,
    far_side_ref,
    seg_ref,
    picks_ref,
    q_ref,
    k_ref,
    v_ref,
    o_ref,
    lse_ref,
    rows_ref,
    tok_t_hbm,
    marks_ref,
    table_ref,
    tok_ref,
    tok_t_ref,
    w_scr,
    lse_scr,
    even,
    odd,
    sems,
    tok_sems,
    *,
    tile,
    slots,
    blocks,
):
    length = q_ref.shape[0]
    pair = pl.program_id(0)
    lane = lax.broadcasted_iota(jnp.int32, (1, LANES), 1)
    zero = jnp.zeros((), BF)

    eighth_refs = (own_ref, near_ref, side_ref, far_near_ref, far_side_ref)

    @pl.when(pair == 0)
    def _():
        copies = gathered_eighths(place, *eighth_refs, w_scr, sems)
        step = length // 4
        loads = [
            pltpu.make_async_copy(
                tok_hbm.at[n * step : (n + 1) * step, :],
                tok_ref.at[n * step : (n + 1) * step, :],
                tok_sems.at[n],
            )
            for n in range(4)
        ]
        for copy in copies + loads:
            copy.start()
        lse_scr[...] = jnp.zeros_like(lse_scr)
        marks_ref[...] = token_marks(seg_ref[...], blocks)
        for load in loads:
            load.wait()
        tok_t_ref[...] = piece_order(tok_ref, place[1])
        pltpu.make_async_copy(tok_t_ref, tok_t_hbm, tok_sems.at[4]).start()
        for copy in copies:
            copy.wait()
        small = w_scr[:, w_scr.shape[1] - LANES :].astype(F32)
        rows_ref[...] = jnp.transpose(small)[: rows_ref.shape[0], :]

    cols = pl.ds(pl.multiple_of(pair * 3 * LANES, LANES), 3 * LANES)
    here = pl.ds(pl.multiple_of(pair * LANES, LANES), LANES)
    bias = jnp.concatenate(
        [rows_ref[6:7, here], jnp.zeros((1, LANES), F32), rows_ref[7:8, here]], axis=1
    )
    qkv = (dotf(tok_ref[...], w_scr[:, cols]) + bias).astype(BF)
    q_ref[...] = qkv[:, :LANES]
    k_ref[...] = qkv[:, LANES : 2 * LANES]
    v_ref[...] = qkv[:, 2 * LANES :]
    keys, values = [], []
    for head in range(2):
        table_ref[head] = head_table(picks_ref[head], slots, blocks)
        key_marks = dotf(marks_ref[...], table_ref[head]).astype(BF)
        keys.append(jnp.concatenate([k_ref[...], key_marks], axis=1))
        values.append(jnp.where(lane // HD == head, v_ref[...], zero))
    steps = [(at, head) for at in range(0, length, tile) for head in range(2)]
    held = [even, odd]

    def score(index):
        at, head = steps[index]
        rows = pl.ds(at, tile)
        query = jnp.where(lane // HD == head, q_ref[rows, :] * jnp.asarray(HD**-0.5, BF), zero)
        return dotf(jnp.concatenate([query, marks_ref[rows, :]], axis=1), keys[head], NT)

    held[0][...] = score(0)
    first = None
    for index, (at, head) in enumerate(steps):
        rows = pl.ds(at, tile)
        if index + 1 < len(steps):
            held[(index + 1) % 2][...] = score(index + 1)
        now = held[index % 2]
        top = jnp.max(now[...], axis=1, keepdims=True)
        raised = jnp.exp(now[...] - top)
        total = jnp.sum(raised, axis=1, keepdims=True)
        mixed = dotf(raised.astype(BF), values[head]) * (1.0 / total)
        if head == 0:
            first = mixed
        else:
            o_ref[rows, :] = (first + mixed).astype(BF)
        lse_scr[rows, :] = jnp.where(
            lane == 2 * pair + head, top + jnp.log(total), lse_scr[rows, :]
        )

    @pl.when(pair == pl.num_programs(0) - 1)
    def _():
        lse_ref[...] = jnp.transpose(lse_scr[...])[: lse_ref.shape[0], :]
        pltpu.make_async_copy(tok_t_ref, tok_t_hbm, tok_sems.at[4]).wait()


def attend(place, tokens, rows_a, segments, random_blocks):
    length, model = tokens.shape
    blocks, heads, slots = random_blocks.shape[1:]
    picks = jnp.pad(
        random_blocks[0].transpose(1, 2, 0),
        ((0, 0), (0, 8 - slots), (0, LANES - blocks)),
        constant_values=-1,
    )
    width = rows_a[0].shape[1]
    pairs = (width - LANES) // (3 * LANES)
    tile = 256
    whole = lambda dims: pl.BlockSpec(dims, lambda i: (0,) * len(dims))
    anywhere = pl.BlockSpec(memory_space=pl.ANY)
    block = pl.BlockSpec((length, LANES), lambda i: (0, i))
    out_rows = 16
    return pl.pallas_call(
        functools.partial(attend_kernel, tile=tile, slots=slots, blocks=blocks),
        grid=(pairs,),
        in_specs=[
            SM,
            anywhere,
            anywhere,
            anywhere,
            anywhere,
            anywhere,
            anywhere,
            whole((1, length)),
            pl.BlockSpec((2, 8, LANES), lambda i: (i, 0, 0)),
        ],
        out_specs=[
            block,
            block,
            block,
            block,
            whole((out_rows, length)),
            whole((out_rows, model)),
            anywhere,
            whole((length, LANES)),
            pl.BlockSpec((2, LANES, LANES), lambda i: (i, 0, 0)),
        ],
        out_shape=[shape((length, pairs * LANES), BF)] * 4
        + [
            shape((out_rows, length), F32),
            shape((out_rows, model), F32),
            shape((model, length), BF),
            shape((length, LANES), BF),
            shape((heads, LANES, LANES), BF),
        ],
        scratch_shapes=[
            pltpu.VMEM((length, model), BF),
            pltpu.VMEM((model, length), BF),
            pltpu.VMEM((model, width), BF),
            pltpu.VMEM((length, LANES), F32),
            pltpu.VMEM((tile, length), F32),
            pltpu.VMEM((tile, length), F32),
            pltpu.SemaphoreType.DMA((5,)),
            pltpu.SemaphoreType.DMA((5,)),
        ],
        compiler_params=params(58),
        cost_estimate=cost(18e9, 12 << 20, 8 << 20),
        name="attend",
    )(place, tokens, *rows_a, segments, picks)


def attend_back_kernel(
    place,
    q_ref,
    k_ref,
    v_ref,
    do_ref,
    o_ref,
    marks_ref,
    table_ref,
    lse_ref,
    tok_t_hbm,
    mid_ref,
    keep_hbm,
    send_hbm,
    d_ref,
    keep_ref,
    send_ref,
    tok_t_ref,
    dq_sum,
    dv_sum,
    dk_sum,
    bias_scr,
    load_sem,
    out_sems,
    *,
    tile,
):
    length = q_ref.shape[0]
    pair = pl.program_id(0)
    load = pltpu.make_async_copy(tok_t_hbm, tok_t_ref, load_sem)

    @pl.when(pair == 0)
    def _():
        load.start()

    core = place[1]
    lane = lax.broadcasted_iota(jnp.int32, (1, LANES), 1)
    zero = jnp.zeros((), BF)
    scale = jnp.asarray(HD**-0.5, BF)
    prod = do_ref[...].astype(F32) * o_ref[...].astype(F32)
    high = prod.astype(BF)
    low = (prod - high.astype(F32)).astype(BF)
    pick = (
        lax.broadcasted_iota(jnp.int32, (8, LANES), 0)
        == lax.broadcasted_iota(jnp.int32, (8, LANES), 1) // HD
    ).astype(BF)
    inner = dotf(pick, high, NT) + dotf(pick, low, NT)
    keys_t = jnp.transpose(k_ref[...] * scale)
    for head in range(2):
        mine = lane // HD == head
        key_marks = dotf(marks_ref[...], table_ref[head]).astype(BF)
        keys = jnp.concatenate([k_ref[...], key_marks], axis=1)
        log_total = lse_ref[pl.ds(2 * pair + head, 1), :]
        for at in range(0, length, tile):
            here = pl.ds(at, tile)
            query = jnp.where(mine, q_ref[here, :] * scale, zero)
            upstream = jnp.where(mine, do_ref[here, :], zero)
            scores = dotf(keys, jnp.concatenate([query, marks_ref[here, :]], axis=1), NT)
            probs = jnp.exp(scores - log_total[:, at : at + tile])
            grad_probs = dotf(v_ref[...], upstream, NT)
            grad_scores = (probs * (grad_probs - inner[head : head + 1, at : at + tile])).astype(BF)
            grad_v = dotf(probs.astype(BF), upstream)
            grad_k = dotf(grad_scores, query)
            dq_sum[head * HD : (head + 1) * HD, here] = dotf(
                keys_t[head * HD : (head + 1) * HD], grad_scores
            )
            if head == 0 and at == 0:
                dv_sum[...] = grad_v
                dk_sum[...] = grad_k
            else:
                dv_sum[...] += grad_v
                dk_sum[...] += grad_k
    d_ref[:, :LANES] = jnp.transpose(dq_sum[...]).astype(BF)
    d_ref[:, LANES : 2 * LANES] = dk_sum[...].astype(BF)
    d_ref[:, 2 * LANES :] = dv_sum[...].astype(BF)
    outs = (keep_ref, send_ref)
    width = 3 * LANES

    @pl.when(pair == 0)
    def _():
        load.wait()

    def write_out(group, count):
        cols = pl.ds(pl.multiple_of(group * width, LANES), count)
        return [
            pltpu.make_async_copy(source.at[:, cols], into.at[:, cols], out_sems.at[number, group])
            for number, (source, into) in enumerate(((send_ref, send_hbm), (keep_ref, keep_hbm)))
        ]

    result = dotf(tok_t_ref[...], d_ref[...]).astype(BF)
    store_pieces(result, core, outs, pl.ds(pl.multiple_of(pair * width, LANES), width))
    for copy in write_out(pair, width):
        copy.start()
    here = pl.ds(pl.multiple_of(pair * LANES, LANES), LANES)
    bias_scr[0:1, here] = col_sum(d_ref[:, :LANES].astype(F32))
    bias_scr[1:2, here] = col_sum(d_ref[:, 2 * LANES :].astype(F32))

    @pl.when(pair == pl.num_programs(0) - 1)
    def _():
        model = mid_ref.shape[1]
        sums = jnp.concatenate(
            [
                mid_ref[0:6, :],
                bias_scr[0:2, :],
                mid_ref[8:16, :],
            ],
            axis=0,
        )
        sums = jnp.concatenate([sums, sums, jnp.zeros((LANES - 2 * PARAMS, model), F32)], axis=0)
        quarter = model // 4
        turned = jnp.transpose(sums)
        kept, sent = [], []
        for r0 in range(2):
            lower = turned[r0 * 2 * quarter : r0 * 2 * quarter + quarter]
            upper = turned[r0 * 2 * quarter + quarter : (r0 + 1) * 2 * quarter]
            kept.append(jnp.where(core == 0, lower, upper))
            sent.append(jnp.where(core == 0, upper, lower))
        total = keep_ref.shape[1]
        store_pieces(
            two_parts(jnp.concatenate(kept + sent, axis=0)), core, outs, slice(total - LANES, total)
        )
        groups = (total - LANES) // width
        last = write_out(groups, LANES)
        for copy in last:
            copy.start()
        for group in range(groups):
            for copy in write_out(group, width):
                copy.wait()
        for copy in last:
            copy.wait()


def attend_back(place, q, k, v, grad_mixed, mixed, marks, table, lse, tok_t, sums):
    length = q.shape[0]
    model = tok_t.shape[0]
    pairs = q.shape[1] // LANES
    width = 3 * LANES
    total = pairs * width + LANES
    whole = lambda dims: pl.BlockSpec(dims, lambda i: (0,) * len(dims))
    block = pl.BlockSpec((length, LANES), lambda i: (0, i))
    return pl.pallas_call(
        functools.partial(attend_back_kernel, tile=512),
        grid=(pairs,),
        in_specs=[SM]
        + [block] * 5
        + [whole(marks.shape), pl.BlockSpec((2, LANES, LANES), lambda i: (i, 0, 0))]
        + [whole(lse.shape), pl.BlockSpec(memory_space=pl.ANY), whole(sums.shape)],
        out_specs=[
            pl.BlockSpec(memory_space=pl.ANY),
            pl.BlockSpec(memory_space=pl.ANY),
            pl.BlockSpec((length, width), lambda i: (0, i)),
        ],
        out_shape=[
            shape((model // 2, total), BF),
            shape((model // 2, total), BF),
            shape((length, pairs * width), BF),
        ],
        scratch_shapes=[
            pltpu.VMEM((model // 2, total), BF),
            pltpu.VMEM((model // 2, total), BF),
            pltpu.VMEM((model, length), BF),
            pltpu.VMEM((LANES, length), F32),
            pltpu.VMEM((length, LANES), F32),
            pltpu.VMEM((length, LANES), F32),
            pltpu.VMEM((8, model), F32),
            pltpu.SemaphoreType.DMA,
            pltpu.SemaphoreType.DMA((2, pairs + 1)),
        ],
        compiler_params=params(56),
        cost_estimate=cost(30e9, 10 << 20, 8 << 20, 1.0),
        name="attend_back",
    )(place, q, k, v, grad_mixed, mixed, marks, table, lse, tok_t, sums)


def two_parts(values):
    lane = lax.broadcasted_iota(jnp.int32, (1, LANES), 1)
    rounded = values.astype(BF)
    return jnp.where(lane < PARAMS, rounded, (values - rounded.astype(F32)).astype(BF))


def both_lanes(values):
    lane = lax.broadcasted_iota(jnp.int32, (1, LANES), 1)
    later = pltpu.roll(values, LANES - PARAMS, 1)
    earlier = pltpu.roll(values, PARAMS, 1)
    return values + jnp.where(lane < PARAMS, later, jnp.where(lane < 2 * PARAMS, earlier, 0.0))


def summed(parts, small):
    total = parts[0].astype(F32)
    for part in parts[1:]:
        total = total + part.astype(F32)
    if not small:
        return total.astype(BF)
    at = total.shape[1] - LANES
    return jnp.concatenate([total[:, :at].astype(BF), two_parts(both_lanes(total[:, at:]))], axis=1)


def piece_order(lhs_ref, core):
    quarter = lhs_ref.shape[1] // 4
    cols = []
    for target in (core, 1 - core):
        for half in range(2):
            start = pl.multiple_of(half * 2 * quarter + target * quarter, quarter)
            cols.append(lhs_ref[:, pl.ds(start, quarter)])
    return jnp.transpose(jnp.concatenate(cols, axis=1))


def store_pieces(result, core, outs, cols):
    quarter = result.shape[0] // 4
    piece = quarter // 4
    for which, target in enumerate((core, 1 - core)):
        for r0 in range(2):
            for r2 in range(2):
                for r3 in range(2):
                    at = which * 2 * quarter + r0 * quarter + r2 * 2 * piece + r3 * piece
                    spot = jnp.where(target == 0, r0 * 4 + r2 * 2 + r3, r3 * 4 + r2 * 2 + r0)
                    rows = pl.ds(pl.multiple_of(spot * piece, piece), piece)
                    outs[which][rows, cols] = result[at : at + piece, :]


def weight_grad(lhs_t, rhs_ref, core, outs, first, tile=512):
    for at in range(0, rhs_ref.shape[1], tile):
        result = dotf(lhs_t, rhs_ref[:, at : at + tile]).astype(BF)
        store_pieces(result, core, outs, slice(first + at, first + at + tile))


def normed(hidden):
    center = hidden - jnp.mean(hidden, axis=-1, keepdims=True)
    spread = jnp.mean(center * center, axis=-1, keepdims=True)
    rate = lax.rsqrt(spread + norm_eps)
    return center * rate, rate


def norm_back(grad, unit, rate):
    return rate * (
        grad
        - jnp.mean(grad, axis=-1, keepdims=True)
        - unit * jnp.mean(grad * unit, axis=-1, keepdims=True)
    )


def col_sum(values):
    return jnp.sum(values, axis=0, keepdims=True)


def middle_kernel(
    place,
    rows_ref,
    tok_hbm,
    cot_hbm,
    mixed_hbm,
    own_hbm,
    near_hbm,
    far_hbm,
    out_hbm,
    dh_hbm,
    do_hbm,
    keep_hbm,
    send_hbm,
    sums_ref,
    tok_ref,
    cot_ref,
    mixed_ref,
    out_ref,
    dh_ref,
    do_ref,
    keep_ref,
    send_ref,
    w_scr,
    act_scr,
    du_scr,
    z_scr,
    df_scr,
    da_scr,
    sems,
    out_sems,
    *,
    tile,
):
    length, model = tok_ref.shape
    core = place[1]
    hidden_count = act_scr.shape[1]
    w_up = slice(0, hidden_count)
    w_down = slice(hidden_count, 2 * hidden_count)
    w_out = slice(2 * hidden_count, w_scr.shape[1])
    waits = {}
    number = 0
    for name, sources in (
        ("out", w_out),
        (0, ((mixed_hbm, mixed_ref), (tok_hbm, tok_ref))),
        ("up", w_up),
        ("down", w_down),
        ("cot", ((cot_hbm, cot_ref),)),
        *((at, ((mixed_hbm, mixed_ref), (tok_hbm, tok_ref))) for at in range(tile, length, tile)),
    ):
        if isinstance(sources, slice):
            copies = gathered_rows(
                place, own_hbm, near_hbm, far_hbm, w_scr, sems, sources, number
            )
        else:
            rows = slice(None) if name == "cot" else slice(name, name + tile)
            copies = [
                pltpu.make_async_copy(source.at[rows, :], into.at[rows, :], sems.at[number + n])
                for n, (source, into) in enumerate(sources)
            ]
        number += len(copies)
        for copy in copies:
            copy.start()
        waits[name] = copies

    def ready(name):
        for copy in waits.pop(name, ()):
            copy.wait()

    pending = []

    def write_out(source, into):
        copy = pltpu.make_async_copy(source, into, out_sems.at[len(pending)])
        copy.start()
        pending.append(copy)

    row = lambda number: rows_ref[number : number + 1, :]
    bias_up = jnp.concatenate([row(8), row(9), row(10), row(11)], axis=1)
    sums = [jnp.zeros((1, model), F32)] * 6
    sum_up = jnp.zeros((1, hidden_count), F32)
    for at in range(0, length, tile):
        here = pl.ds(at, tile)
        ready("out")
        ready(at)
        attn_out = dotf(mixed_ref[here, :], w_scr[:, w_out], NT) + row(4)
        unit_one, rate_one = normed(tok_ref[here, :].astype(F32) + attn_out)
        z_one = unit_one * row(0) + row(1)
        z_low = z_one.astype(BF)
        z_scr[here, :] = z_low
        ready("up")
        up = dotf(z_low, w_scr[:, w_up]) + bias_up
        below = 0.5 * (1.0 + lax.erf(up * (0.5**0.5)))
        slope = below + up * (jnp.exp(-0.5 * up * up) * (1.0 / (2.0 * 3.141592653589793) ** 0.5))
        active = (up * below).astype(BF)
        act_scr[here, :] = active
        ready("down")
        ffn_out = dotf(active, w_scr[:, w_down], NT) + row(5)
        unit_two, rate_two = normed(z_one + ffn_out)
        out_ref[here, :] = (unit_two * row(2) + row(3)).astype(BF)
        ready("cot")
        upstream = cot_ref[here, :].astype(F32)
        grad_two = norm_back(upstream * row(2), unit_two, rate_two)
        down_low = grad_two.astype(BF)
        df_scr[here, :] = down_low
        grad_up = (dotf(down_low, w_scr[:, w_down]) * slope).astype(BF)
        du_scr[here, :] = grad_up
        grad_z = grad_two + dotf(grad_up, w_scr[:, w_up], NT)
        grad_one = norm_back(grad_z * row(0), unit_one, rate_one)
        dh_ref[here, :] = grad_one
        attn_low = grad_one.astype(BF)
        da_scr[here, :] = attn_low
        do_ref[here, :] = dotf(attn_low, w_scr[:, w_out]).astype(BF)
        for source, into in ((out_ref, out_hbm), (dh_ref, dh_hbm), (do_ref, do_hbm)):
            write_out(source.at[here, :], into.at[here, :])
        parts = (
            grad_z * unit_one,
            grad_z,
            upstream * unit_two,
            upstream,
            attn_low.astype(F32),
            down_low.astype(F32),
        )
        sums = [a + col_sum(b) for a, b in zip(sums, parts)]
        sum_up = sum_up + col_sum(grad_up.astype(F32))
    for number in range(6):
        sums_ref[number : number + 1, :] = sums[number]
    sums_ref[6:8, :] = jnp.zeros((2, model), F32)
    for number in range(4):
        sums_ref[8 + number : 9 + number, :] = sum_up[:, number * model : (number + 1) * model]
    sums_ref[12:16, :] = jnp.zeros((4, model), F32)
    outs = (keep_ref, send_ref)
    for lhs, rhs, cols in (
        (z_scr, du_scr, w_up),
        (df_scr, act_scr, w_down),
        (da_scr, mixed_ref, w_out),
    ):
        weight_grad(piece_order(lhs, core), rhs, core, outs, cols.start)
        for source, into in ((send_ref, send_hbm), (keep_ref, keep_hbm)):
            write_out(source.at[:, cols], into.at[:, cols])
    for copy in pending:
        copy.wait()


def middle(place, tokens, cotangent, mixed, rows, own, near, far):
    length, model = tokens.shape
    width = own.shape[1]
    hidden_count = (width - mixed.shape[1]) // 2
    tile = 512
    anywhere = pl.BlockSpec(memory_space=pl.ANY)
    outs = [
        shape((length, model), BF),
        shape((length, model), F32),
        shape((length, mixed.shape[1]), BF),
        shape((model // 2, width), BF),
        shape((model // 2, width), BF),
    ]
    vmem = lambda x: pltpu.VMEM(x.shape, x.dtype)
    return pl.pallas_call(
        functools.partial(middle_kernel, tile=tile),
        in_specs=[SM, VM] + [anywhere] * 5 + [VM],
        out_specs=[anywhere] * 5 + [VM],
        out_shape=outs + [shape((16, model), F32)],
        scratch_shapes=[vmem(x) for x in (tokens, cotangent, mixed, *outs)]
        + [
            pltpu.VMEM((model, width), BF),
            pltpu.VMEM((length, hidden_count), BF),
            pltpu.VMEM((length, hidden_count), BF),
            pltpu.VMEM((length, model), BF),
            pltpu.VMEM((length, model), BF),
            pltpu.VMEM((length, model), BF),
            pltpu.SemaphoreType.DMA((10 + 2 * (length // tile),)),
            pltpu.SemaphoreType.DMA((3 * (length // tile) + 6,)),
        ],
        compiler_params=params(58),
        cost_estimate=cost(16e9, 16 << 20, 4 << 20, 1.0),
        name="middle",
    )(place, rows, tokens, cotangent, mixed, own, near, far)


def input_grad_kernel(
    place, dh_ref, d_ref, own_ref, near_ref, side_ref, far_near_ref, far_side_ref, out_ref, w_scr, sems
):
    eighth_refs = (own_ref, near_ref, side_ref, far_near_ref, far_side_ref)
    width = d_ref.shape[1]

    @pl.when(pl.program_id(0) == 0)
    def _():
        copies = gathered_eighths(place, *eighth_refs, w_scr, sems)
        for copy in copies:
            copy.start()
        for copy in copies:
            copy.wait()

    out_ref[...] = (dh_ref[...] + dotf(d_ref[...], w_scr[:, :width], NT)).astype(BF)


def input_gradient(place, dh, d, rows_a):
    length, model = dh.shape
    tile = 256
    anywhere = pl.BlockSpec(memory_space=pl.ANY)
    rows = lambda width: pl.BlockSpec((tile, width), lambda i: (i, 0))
    return pl.pallas_call(
        input_grad_kernel,
        grid=(length // tile,),
        in_specs=[SM, rows(model), rows(d.shape[1])] + [anywhere] * 5,
        out_specs=rows(model),
        out_shape=shape((length, model), BF),
        scratch_shapes=[pltpu.VMEM((model, rows_a[0].shape[1]), BF), pltpu.SemaphoreType.DMA((5,))],
        compiler_params=params(16),
        cost_estimate=cost(2 * length * model * d.shape[1], 8 << 20),
        name="input_gradient",
    )(place, dh, d, *rows_a)


def add_low(a, b):
    return (a.astype(F32) + b.astype(F32)).astype(BF)


def add_parts_kernel(place, *refs, small):
    refs[-1][...] = summed([ref[...] for ref in refs[:-1]], small)


def add_parts(place, parts, give, small):
    rows = min(part.shape[0] for part in parts)
    rows = rows // 2 if give else rows
    width = parts[0].shape[1]

    def pick(part):
        if part.shape[0] == rows:
            return pl.BlockSpec((rows, width), lambda i, place: (0, 0))
        return pl.BlockSpec((rows, width), lambda i, place: (1 - place[6] if give else place[6], 0))

    return pl.pallas_call(
        functools.partial(add_parts_kernel, small=small),
        grid_spec=pltpu.PrefetchScalarGridSpec(
            num_scalar_prefetch=1,
            grid=(1,),
            in_specs=[pick(part) for part in parts],
            out_specs=pl.BlockSpec((rows, width), lambda i, place: (0, 0)),
        ),
        out_shape=shape((rows, width), BF),
        compiler_params=params(8),
        cost_estimate=cost(len(parts) * rows * width, 2 * len(parts) * rows * width),
        name="add_parts",
    )(place, *parts)


def flip(count, bit):
    return [(i, i ^ (1 << bit)) for i in range(count)]


def mixed_flip(count, even, odd):
    return [(i, i ^ (1 << (odd if (i >> 1) & 1 else even))) for i in range(2 * count)]


STEPS = ((0, 2), (2, 3), (3, 0))


def mixed_mask(count, mask):
    pairs = []
    for i in range(2 * count):
        partner = i
        for bit, step in zip((2, 1), STEPS):
            if mask & bit:
                partner ^= 1 << step[(i >> 1) & 1]
        pairs.append((i, partner))
    return pairs


def split_kernel(place, keep_ref, got_ref, *outs, small):
    piece = outs[0].shape[0]
    mine = place[3] * 2 + place[4]
    for mask, out in enumerate(outs):
        rows = pl.ds(pl.multiple_of((mine ^ mask) * piece, piece), piece)
        out[...] = summed([keep_ref[rows, :], got_ref[rows, :]], small)


def swap_two(value, count, mask):
    return lax.ppermute(value, ("dp", "shard"), mixed_mask(count, mask))


def split(place, keep, got, small):
    rows, width = keep.shape
    steps = 1 if small else 4
    step = width // steps
    whole = pl.BlockSpec((rows, step), lambda i: (0, i))
    part = pl.BlockSpec((rows // 4, step), lambda i: (0, i))
    return pl.pallas_call(
        functools.partial(split_kernel, small=small),
        grid=(steps,),
        in_specs=[SM, whole, whole],
        out_specs=[part] * 4,
        out_shape=[shape((rows // 4, width), BF)] * 4,
        compiler_params=params(16),
        cost_estimate=cost(rows * width, 6 * rows * width),
        name="split",
    )(place, keep, got)


def swap_core(value, count):
    return lax.ppermute(value, "dp", flip(count, 0))


def swap_mixed(value, count, step):
    return lax.ppermute(value, ("dp", "shard"), mixed_flip(count, *step))


def swap_bit(value, count, bit):
    return lax.ppermute(value, "dp", flip(count, bit))


def after(value, *others):
    return lax.optimization_barrier((value,) + others)[0]


def adam_values(scalars, weight_ref, mean_ref, square_ref, grad, decay, outs):
    weight = weight_ref[...]
    mean_out = beta_one * mean_ref[...] + (1.0 - beta_one) * grad
    square_out = beta_two * square_ref[...] + (1.0 - beta_two) * grad * grad
    mean_hat = mean_out * scalars[2]
    square_hat = square_out * scalars[3]
    weight_out = weight - scalars[0] * (
        mean_hat / (jnp.sqrt(square_hat) + adam_eps) + decay * weight
    )
    outs[0][...] = weight_out
    outs[1][...] = mean_out
    outs[2][...] = square_out
    outs[3][...] = weight_out.astype(BF)


def piece_block(place, own, flips):
    bit2, bit3 = (place[4], place[5]) if own else (place[5], place[4])
    core = place[1] if own else 1 - place[1]
    return core * 4 + (bit2 ^ (flips >> 1)) * 2 + (bit3 ^ (flips & 1))


def chosen(index, values):
    result = values[-1]
    for number in range(len(values) - 2, -1, -1):
        result = jnp.where(index == number, values[number], result)
    return result


def adam_ffn_kernel(place, scalars, *refs, count):
    step = pl.program_id(0)
    stack, _, width = refs[count].shape
    for number in range(count):

        @pl.when(step == number)
        def _():
            grad = jnp.stack(
                [refs[number][:, w * width : (w + 1) * width].astype(F32) for w in range(stack)]
            )
            adam_values(scalars, *refs[count : count + 3], grad, scalars[1], refs[-4:])


def adam_ffn(place, scalars, pieces, state, before):
    count = len(pieces)
    stack, rows, width = state[0].shape
    step = rows // 8
    grads = [piece[0] for piece in pieces]
    take = pl.BlockSpec((step, stack * width), lambda p, place, sc: (0, 0))
    block = pl.BlockSpec(
        (stack, step, width),
        lambda p, place, sc: (0, chosen(p, [piece_block(place, *x[1:]) for x in pieces]), 0),
    )
    before = list(before or ())
    return pl.pallas_call(
        functools.partial(adam_ffn_kernel, count=count),
        grid_spec=pltpu.PrefetchScalarGridSpec(
            num_scalar_prefetch=2,
            grid=(count,),
            in_specs=[take] * count + [block] * 3 + [pl.BlockSpec(memory_space=pl.ANY)] * len(before),
            out_specs=[block] * 4,
        ),
        out_shape=[shape(state[0].shape, F32)] * 3 + [shape(state[0].shape, BF)],
        input_output_aliases={5 + count + n: n for n in range(len(before))},
        compiler_params=params(24),
        cost_estimate=cost(20 * count * step * width, 28 * count * step * width),
        name="adam_ffn",
    )(place, scalars, *grads, *state, *before)


def adam_attn_kernel(place, scalars, *refs, count, orders, small):
    grads, outer, state = refs[:count], refs[count : 2 * count], refs[2 * count : 2 * count + 3]
    rest = refs[2 * count + 3 :]
    step = pl.program_id(0)
    if small:
        little, (sw, sm, ss), rest = rest[:small], rest[small : small + 3], rest[small + 3 + 4 :]
        outs, small_outs, scr = rest[:4], rest[4:8], rest[8]

        @pl.when(step == 0)
        def _():
            for ref, order in zip(little, orders):
                rows = ref.shape[0]
                where = pl.ds(pl.multiple_of(piece_block(place, *order) * rows, rows), rows)
                scr[where, :] = ref[...].astype(F32)
            turned = jnp.transpose(both_lanes(scr[...]))[: sw.shape[0], :]
            adam_values(scalars, sw, sm, ss, turned, 0.0 * scalars[1], small_outs)
    else:
        outs = rest[-4:]
    for number in range(count):

        @pl.when(step == number)
        def _():
            grad = grads[number][...].astype(F32)
            pairs = grad.shape[1] // (3 * LANES)
            parts = [
                grad[:, p * 3 * LANES + kind * LANES : p * 3 * LANES + (kind + 1) * LANES]
                for kind in range(3)
                for p in range(pairs)
            ]
            parts.append(outer[number][...].astype(F32))
            adam_values(scalars, *state, jnp.concatenate(parts, axis=1), scalars[1], outs)


def adam_attn(place, scalars, pieces, pieces_b, state, before, every=None, small=None):
    count = len(pieces)
    rows, width = state[0].shape
    step = rows // 8
    out_width = width // 4
    grads = [piece[0] for piece in pieces]
    outer = [piece[0] for piece in pieces_b]
    last = outer[0].shape[1] // out_width - 1
    block = pl.BlockSpec(
        (step, width),
        lambda p, place, sc: (chosen(p, [piece_block(place, *x[1:]) for x in pieces]), 0),
    )
    anywhere = pl.BlockSpec(memory_space=pl.ANY)
    in_specs = [pl.BlockSpec(grads[0].shape, lambda p, place, sc: (0, 0))] * count
    in_specs += [pl.BlockSpec((step, out_width), lambda p, place, sc: (0, last))] * count
    in_specs += [block] * 3
    operands = [place, scalars, *grads, *outer, *state]
    out_specs = [block] * 4
    out_shape = [shape(state[0].shape, F32)] * 3 + [shape(state[0].shape, BF)]
    scratch = []
    if small:
        whole = pl.BlockSpec(small[0].shape, lambda p, place, sc: (0, 0))
        at = grads[0].shape[1] // LANES - 1
        in_specs += [pl.BlockSpec((step, LANES), lambda p, place, sc: (0, at))] * len(every)
        in_specs += [whole] * 3
        operands += [piece[0] for piece in every] + list(small)
        out_specs += [whole] * 4
        out_shape += [shape(small[0].shape, F32)] * 3 + [shape(small[0].shape, BF)]
        scratch = [pltpu.VMEM((rows, LANES), F32)]
    before = list(before or ())
    aliases = {len(operands) + n: n for n in range(len(before))}
    return pl.pallas_call(
        functools.partial(
            adam_attn_kernel,
            count=count,
            orders=[piece[1:] for piece in every or ()],
            small=len(every or ()),
        ),
        grid_spec=pltpu.PrefetchScalarGridSpec(
            num_scalar_prefetch=2,
            grid=(count,),
            in_specs=in_specs + [anywhere] * len(before),
            out_specs=out_specs,
            scratch_shapes=scratch,
        ),
        out_shape=out_shape,
        input_output_aliases=aliases,
        compiler_params=params(24),
        cost_estimate=cost(20 * count * step * width, 28 * count * step * width),
        name="adam_attn",
    )(*operands, *before)


def from_neighbour(value):
    return lax.ppermute(value, "shard", [(0, 1), (1, 0)])


def local(
    count,
    tokens,
    cotangent,
    segments,
    random_blocks,
    step_count,
    adam_rates,
    attn_master,
    attn_mean,
    attn_square,
    ffn_master,
    ffn_mean,
    ffn_square,
    small_master,
    small_mean,
    small_square,
):
    replica = lax.axis_index("dp")
    shard = lax.axis_index("shard")
    core, low, high = replica & 1, (replica >> 1) & 1, (replica >> 2) & 1
    even = core == 0
    place = jnp.stack(
        [
            shard,
            core,
            low,
            jnp.where(even, shard, low),
            jnp.where(even, low, high),
            jnp.where(even, high, low),
            jnp.where(even, high, shard),
        ]
    ).astype(jnp.int32)
    pairs = attn_master.shape[1] // 4 // LANES
    near_a = from_neighbour(pack_eighth_a(attn_master, small_master))
    quarter_b = pack_quarter_b(place, attn_master, ffn_master)
    near_a = after(near_a, quarter_b)
    near_b = from_neighbour(after(quarter_b, near_a))
    side_a = swap_bit(near_a, count, 1)
    own_a, own_b = pack_own(attn_master, ffn_master, small_master)
    side_a = after(side_a, own_a)
    rows_a = (own_a, near_a, side_a, swap_core(near_a, count), swap_core(side_a, count))
    q, k, v, mixed, lse, rows, tok_t, marks, table = attend(
        place, tokens, rows_a, segments, random_blocks
    )
    far_b = swap_core(after(near_b, lse), count)
    layer_out, dh, grad_mixed, keep_b, send_b, sums = middle(
        place, tokens, cotangent, mixed, rows, own_b, near_b, far_b
    )
    parts_b = list(split(place, keep_b, swap_core(send_b, count), False))
    parts_b = parts_b[:1] + [swap_two(parts_b[mask], count, mask) for mask in (1, 2, 3)]
    keep_a, send_a, d = attend_back(
        place, q, k, v, after(grad_mixed, parts_b[0]), mixed, marks, table, lse, tok_t, sums
    )
    got_a = swap_core(send_a, count)
    parts_b = parts_b[:1] + [after(part, d) for part in parts_b[1:]]
    got_b = swap_mixed(add_parts(place, parts_b, True, False), count, STEPS[2])

    step_value = step_count[0].astype(F32)
    scalars = jnp.stack(
        [
            adam_rates[0],
            adam_rates[1],
            1.0 / (1.0 - beta_one**step_value),
            1.0 / (1.0 - beta_two**step_value),
        ]
    )
    ffn_state = (ffn_master, ffn_mean, ffn_square)
    attn_state = (attn_master, attn_mean, attn_square)
    small_state = (small_master, small_mean, small_square)
    bits = [bit for bit in range(3, count.bit_length() - 1)]

    parts_a = list(split(place, keep_a, got_a, True))
    parts_a = parts_a[:1] + [swap_two(parts_a[mask], count, mask) for mask in (1, 2, 3)]
    total_b = add_parts(place, parts_b + [after(got_b, parts_a[0])], False, False)
    got_b = swap_bit(total_b, count, bits[0])
    input_grad = input_gradient(place, after(dh, total_b), d, rows_a)
    parts_a = parts_a[:1] + [after(part, input_grad) for part in parts_a[1:]]
    got_a = swap_mixed(add_parts(place, parts_a, True, True), count, STEPS[2])
    total_a = add_parts(place, parts_a + [got_a], False, True)
    got_a = swap_bit(total_a, count, bits[0])
    total_b = add_low(total_b, after(got_b, total_a))
    for bit in bits[1:]:
        total_b = add_low(total_b, swap_bit(total_b, count, bit))
    first, second = (3, 2), (2, 3)

    def wave(values, flips):
        return [(v, True, f) for v, f in zip(values, flips)] + [
            (swap_core(v, count), False, f) for v, f in zip(values, flips)
        ]

    b_one = wave([total_b], [0])
    got_b = [swap_mixed(total_b, count, first), swap_mixed(total_b, count, second)]
    ffn_new = adam_ffn(place, scalars, b_one, ffn_state, None)
    total_a = add_parts(place, [total_a, after(got_a, ffn_new[0])], False, True)
    for bit in bits[1:]:
        total_a = add_parts(place, [total_a, swap_bit(total_a, count, bit)], False, True)
    a_one = wave([total_a], [0])
    got_a = [swap_mixed(total_a, count, first), swap_mixed(total_a, count, second)]
    got_b = [after(piece, ffn_new[0], total_a) for piece in got_b]
    b_two = wave(got_b, [1, 2])
    got_b = swap_mixed(got_b[0], count, second)
    attn_new = adam_attn(place, scalars, a_one, b_one, attn_state, None)
    ffn_new = adam_ffn(place, scalars, b_two, ffn_state, ffn_new)
    got_a = [after(piece, attn_new[0]) for piece in got_a]
    a_two = wave(got_a, [1, 2])
    got_a = swap_mixed(got_a[0], count, second)
    b_three = wave([after(got_b, ffn_new[0])], [3])
    attn_new = adam_attn(place, scalars, a_two, b_two, attn_state, attn_new)
    a_three = wave([after(got_a, attn_new[0])], [3])
    ffn_new = adam_ffn(place, scalars, b_three, ffn_state, ffn_new)
    attn_new = adam_attn(
        place,
        scalars,
        a_three,
        b_three,
        attn_state,
        attn_new,
        a_one + a_two + a_three,
        small_state,
    )
    return (layer_out, input_grad) + tuple(attn_new[:4]) + tuple(ffn_new) + tuple(attn_new[4:])


def solution(mesh):
    tokens_in = P(("dp", "shard"), None)
    rows_in = P("shard", None)
    stack_in = P(None, "shard", None)
    cols_in = P(None, "shard")
    placed = (
        (tokens_in,) * 3
        + (P(("dp", "shard"), None, None, None), P(), P())
        + (rows_in,) * 3
        + (stack_in,) * 3
        + (cols_in,) * 3
    )
    return jax.shard_map(
        functools.partial(local, mesh.shape["dp"]),
        mesh=mesh,
        in_specs=placed,
        out_specs=(tokens_in,) * 2 + (rows_in,) * 4 + (stack_in,) * 4 + (cols_in,) * 4,
        check_vma=False,
    )
```

```python
import functools

import jax
import jax.numpy as jnp
from jax import lax
from jax.experimental import pallas as pl
from jax.experimental.pallas import tpu as pltpu
from jax.sharding import PartitionSpec as P

HD = 64
LANES = 128
PARAMS = 16
BF = jnp.bfloat16
F32 = jnp.float32
BLOCKED = -(2.0**100)
NN = (((1,), (0,)), ((), ()))
NT = (((1,), (1,)), ((), ()))
TN = (((0,), (0,)), ((), ()))

norm_eps = 1e-12
beta_one = 0.9
beta_two = 0.999
adam_eps = 1e-08


def dotf(a, b, dims=NN):
    return lax.dot_general(a, b, dims, preferred_element_type=F32)


def params(mebibytes):
    return pltpu.CompilerParams(vmem_limit_bytes=mebibytes << 20)


def cost(flops, bytes_accessed, transcendentals=0, share=0.05):
    return pl.CostEstimate(
        flops=int(flops * share),
        bytes_accessed=int(bytes_accessed * share),
        transcendentals=int(transcendentals * share),
    )


def shape(dims, dtype):
    return jax.ShapeDtypeStruct(dims, dtype)


VM = pl.BlockSpec(memory_space=pltpu.VMEM)
SM = pl.BlockSpec(memory_space=pltpu.SMEM)


def token_marks(segments, blocks):
    length = segments.shape[1]
    row = lax.broadcasted_iota(jnp.int32, (LANES, length), 0)
    block_of = lax.broadcasted_iota(jnp.int32, (LANES, length), 1) // (length // blocks)
    marks = jnp.where((row == block_of) | (row == blocks + segments), 1.0, 0.0)
    return jnp.transpose(marks).astype(BF)


def head_table(picks, slots, blocks):
    row = lax.broadcasted_iota(jnp.int32, (LANES, LANES), 0)
    col = lax.broadcasted_iota(jnp.int32, (LANES, LANES), 1)
    seen = (jnp.abs(row - col) <= 1) | (row == 0) | (row == blocks - 1)
    seen = seen | (col == 0) | (col == blocks - 1)
    for slot in range(slots):
        seen = seen | (row == picks[slot : slot + 1, :])
    bad_block = (row < blocks) & (col < blocks) & ~seen
    bad_segment = (row >= blocks) & (col >= blocks) & (row != col)
    return jnp.where(bad_block | bad_segment, BLOCKED, 0.0).astype(BF)


def grouped_a(kinds):
    return [
        kind[:, at : at + LANES] for at in range(0, kinds[0].shape[1], LANES) for kind in kinds
    ]


def turned_small(small):
    fill = jnp.zeros((LANES - small.shape[0], small.shape[1]), F32)
    return jnp.transpose(jnp.concatenate([small, fill], axis=0))


def packed_b(attn_ref, ffn_ref, first):
    return jnp.concatenate([ffn_ref[0], ffn_ref[1], attn_ref[:, first:]], axis=1).astype(BF)


def pack_a_kernel(attn_hbm, small_hbm, out_ref, attn_ref, small_ref, sems):
    eighth, width = attn_ref.shape
    replica = lax.axis_index("dp")
    core, low = replica & 1, (replica >> 1) & 1
    rows = pl.ds(pl.multiple_of((2 * core + low) * eighth, eighth), eighth)
    cols = pl.ds(pl.multiple_of(core * 2 * eighth, 2 * eighth), 2 * eighth)
    copies = [pltpu.make_async_copy(small_hbm.at[:, cols], small_ref, sems.at[3])]
    feat = width // 3
    for kind in range(3):
        here = slice(kind * feat, (kind + 1) * feat)
        copies.append(
            pltpu.make_async_copy(attn_hbm.at[rows, here], attn_ref.at[:, here], sems.at[kind])
        )
    for copy in copies:
        copy.start()
    for copy in copies:
        copy.wait()
    small = turned_small(small_ref[...])
    small = jnp.where(low == 0, small[:eighth], small[eighth:])
    kinds = [attn_ref[:, kind * feat : (kind + 1) * feat] for kind in range(3)]
    out_ref[...] = jnp.concatenate(grouped_a(kinds) + [small], axis=1).astype(BF)


def pack_b_kernel(place, attn_ref, ffn_ref, out_ref):
    out_ref[...] = packed_b(attn_ref, ffn_ref, 0)


def pack_own_kernel(attn_ref, ffn_ref, small_ref, a_ref, b_ref):
    feat = attn_ref.shape[1] // 4
    kinds = [attn_ref[:, kind * feat : (kind + 1) * feat] for kind in range(3)]
    parts = grouped_a(kinds) + [turned_small(small_ref[...])]
    a_ref[...] = jnp.concatenate(parts, axis=1).astype(BF)
    b_ref[...] = packed_b(attn_ref, ffn_ref, attn_ref.shape[1] // 4 * 3)


def pack_eighth_a(attn, small):
    eighth = attn.shape[0] // 4
    width = attn.shape[1] // 4 * 3
    anywhere = pl.BlockSpec(memory_space=pl.ANY)
    return pl.pallas_call(
        pack_a_kernel,
        in_specs=[anywhere] * 2,
        out_specs=VM,
        out_shape=shape((eighth, width + LANES), BF),
        scratch_shapes=[
            pltpu.VMEM((eighth, width), F32),
            pltpu.VMEM((small.shape[0], 2 * eighth), F32),
            pltpu.SemaphoreType.DMA((4,)),
        ],
        compiler_params=params(58),
        cost_estimate=cost(1e6, 2 << 20),
        name="pack_eighth_a",
    )(attn, small)


def pack_quarter_b(place, attn, ffn):
    quarter = attn.shape[0] // 2
    feat = attn.shape[1] // 4
    hidden_count = ffn.shape[2]
    width = 2 * hidden_count + feat
    return pl.pallas_call(
        pack_b_kernel,
        grid_spec=pltpu.PrefetchScalarGridSpec(
            num_scalar_prefetch=1,
            grid=(1,),
            in_specs=[
                pl.BlockSpec((quarter, feat), lambda i, place: (place[1], 3)),
                pl.BlockSpec((2, quarter, hidden_count), lambda i, place: (0, place[1], 0)),
            ],
            out_specs=pl.BlockSpec((quarter, width), lambda i, place: (0, 0)),
        ),
        out_shape=shape((quarter, width), BF),
        compiler_params=params(12),
        cost_estimate=cost(1e6, 4 << 20),
        name="pack_quarter_b",
    )(place, attn, ffn)


def pack_own(attn, ffn, small):
    rows = attn.shape[0]
    step = rows // 2
    width_a = attn.shape[1] // 4 * 3 + LANES
    width_b = 2 * ffn.shape[2] + attn.shape[1] // 4
    return pl.pallas_call(
        pack_own_kernel,
        grid=(2,),
        in_specs=[
            pl.BlockSpec((step, attn.shape[1]), lambda i: (i, 0)),
            pl.BlockSpec((2, step, ffn.shape[2]), lambda i: (0, i, 0)),
            pl.BlockSpec((small.shape[0], step), lambda i: (0, i)),
        ],
        out_specs=[
            pl.BlockSpec((step, width_a), lambda i: (i, 0)),
            pl.BlockSpec((step, width_b), lambda i: (i, 0)),
        ],
        out_shape=[shape((rows, width_a), BF), shape((rows, width_b), BF)],
        compiler_params=params(16),
        cost_estimate=cost(1e6, 10 << 20),
        name="pack_own",
    )(attn, ffn, small)


def gathered_eighths(place, own_ref, near_ref, side_ref, far_near_ref, far_side_ref, into, sems):
    half = own_ref.shape[0]
    eighth = near_ref.shape[0]
    shard, core, low = place[0], place[1], place[2]
    other = (1 - shard) * half
    copies = []
    for number, (ref, start, count) in enumerate(
        (
            (own_ref, shard * half, half),
            (near_ref, other + (2 * core + low) * eighth, eighth),
            (side_ref, other + (2 * core + 1 - low) * eighth, eighth),
            (far_near_ref, other + (2 * (1 - core) + low) * eighth, eighth),
            (far_side_ref, other + (2 * (1 - core) + 1 - low) * eighth, eighth),
        )
    ):
        rows = pl.ds(pl.multiple_of(start, eighth), count)
        copies.append(pltpu.make_async_copy(ref, into.at[rows, :], sems.at[number]))
    return copies


def gathered_rows(place, own_ref, near_ref, far_ref, into, sems, cols=slice(None), first=0):
    half = own_ref.shape[0]
    quarter = near_ref.shape[0]
    shard = place[0]
    core = place[1]
    other = (1 - shard) * half
    copies = []
    for number, (ref, start, count) in enumerate(
        (
            (own_ref, shard * half, half),
            (near_ref, other + core * quarter, quarter),
            (far_ref, other + (1 - core) * quarter, quarter),
        )
    ):
        rows = pl.ds(pl.multiple_of(start, quarter), count)
        copies.append(
            pltpu.make_async_copy(ref.at[:, cols], into.at[rows, cols], sems.at[first + number])
        )
    return copies


def attend_kernel(
    place,
    tok_hbm,
    own_ref,
    near_ref,
    side_ref,
    far_near_ref,
    far_side_ref,
    seg_ref,
    picks_ref,
    q_ref,
    k_ref,
    v_ref,
    o_ref,
    lse_ref,
    rows_ref,
    tok_t_hbm,
    marks_ref,
    table_ref,
    tok_ref,
    tok_t_ref,
    w_scr,
    lse_scr,
    even,
    odd,
    sems,
    tok_sems,
    *,
    tile,
    slots,
    blocks,
):
    length = q_ref.shape[0]
    pair = pl.program_id(0)
    lane = lax.broadcasted_iota(jnp.int32, (1, LANES), 1)
    zero = jnp.zeros((), BF)

    eighth_refs = (own_ref, near_ref, side_ref, far_near_ref, far_side_ref)

    @pl.when(pair == 0)
    def _():
        copies = gathered_eighths(place, *eighth_refs, w_scr, sems)
        step = length // 4
        loads = [
            pltpu.make_async_copy(
                tok_hbm.at[n * step : (n + 1) * step, :],
                tok_ref.at[n * step : (n + 1) * step, :],
                tok_sems.at[n],
            )
            for n in range(4)
        ]
        for copy in copies + loads:
            copy.start()
        lse_scr[...] = jnp.zeros_like(lse_scr)
        marks_ref[...] = token_marks(seg_ref[...], blocks)
        for load in loads:
            load.wait()
        tok_t_ref[...] = piece_order(tok_ref, place[1])
        pltpu.make_async_copy(tok_t_ref, tok_t_hbm, tok_sems.at[4]).start()
        for copy in copies:
            copy.wait()
        small = w_scr[:, w_scr.shape[1] - LANES :].astype(F32)
        rows_ref[...] = jnp.transpose(small)[: rows_ref.shape[0], :]

    cols = pl.ds(pl.multiple_of(pair * 3 * LANES, LANES), 3 * LANES)
    here = pl.ds(pl.multiple_of(pair * LANES, LANES), LANES)
    bias = jnp.concatenate(
        [rows_ref[6:7, here], jnp.zeros((1, LANES), F32), rows_ref[7:8, here]], axis=1
    )
    qkv = (dotf(tok_ref[...], w_scr[:, cols]) + bias).astype(BF)
    q_ref[...] = qkv[:, :LANES]
    k_ref[...] = qkv[:, LANES : 2 * LANES]
    v_ref[...] = qkv[:, 2 * LANES :]
    keys, values = [], []
    for head in range(2):
        table_ref[head] = head_table(picks_ref[head], slots, blocks)
        key_marks = dotf(marks_ref[...], table_ref[head]).astype(BF)
        keys.append(jnp.concatenate([k_ref[...], key_marks], axis=1))
        values.append(jnp.where(lane // HD == head, v_ref[...], zero))
    steps = [(at, head) for at in range(0, length, tile) for head in range(2)]
    held = [even, odd]

    def score(index):
        at, head = steps[index]
        rows = pl.ds(at, tile)
        query = jnp.where(lane // HD == head, q_ref[rows, :] * jnp.asarray(HD**-0.5, BF), zero)
        return dotf(jnp.concatenate([query, marks_ref[rows, :]], axis=1), keys[head], NT)

    held[0][...] = score(0)
    first = None
    for index, (at, head) in enumerate(steps):
        rows = pl.ds(at, tile)
        if index + 1 < len(steps):
            held[(index + 1) % 2][...] = score(index + 1)
        now = held[index % 2]
        top = jnp.max(now[...], axis=1, keepdims=True)
        raised = jnp.exp(now[...] - top)
        total = jnp.sum(raised, axis=1, keepdims=True)
        mixed = dotf(raised.astype(BF), values[head]) * (1.0 / total)
        if head == 0:
            first = mixed
        else:
            o_ref[rows, :] = (first + mixed).astype(BF)
        lse_scr[rows, :] = jnp.where(
            lane == 2 * pair + head, top + jnp.log(total), lse_scr[rows, :]
        )

    @pl.when(pair == pl.num_programs(0) - 1)
    def _():
        lse_ref[...] = jnp.transpose(lse_scr[...])[: lse_ref.shape[0], :]
        pltpu.make_async_copy(tok_t_ref, tok_t_hbm, tok_sems.at[4]).wait()


def attend(place, tokens, rows_a, segments, random_blocks):
    length, model = tokens.shape
    blocks, heads, slots = random_blocks.shape[1:]
    picks = jnp.pad(
        random_blocks[0].transpose(1, 2, 0),
        ((0, 0), (0, 8 - slots), (0, LANES - blocks)),
        constant_values=-1,
    )
    width = rows_a[0].shape[1]
    pairs = (width - LANES) // (3 * LANES)
    tile = 256
    whole = lambda dims: pl.BlockSpec(dims, lambda i: (0,) * len(dims))
    anywhere = pl.BlockSpec(memory_space=pl.ANY)
    block = pl.BlockSpec((length, LANES), lambda i: (0, i))
    out_rows = 16
    return pl.pallas_call(
        functools.partial(attend_kernel, tile=tile, slots=slots, blocks=blocks),
        grid=(pairs,),
        in_specs=[
            SM,
            anywhere,
            anywhere,
            anywhere,
            anywhere,
            anywhere,
            anywhere,
            whole((1, length)),
            pl.BlockSpec((2, 8, LANES), lambda i: (i, 0, 0)),
        ],
        out_specs=[
            block,
            block,
            block,
            block,
            whole((out_rows, length)),
            whole((out_rows, model)),
            anywhere,
            whole((length, LANES)),
            pl.BlockSpec((2, LANES, LANES), lambda i: (i, 0, 0)),
        ],
        out_shape=[shape((length, pairs * LANES), BF)] * 4
        + [
            shape((out_rows, length), F32),
            shape((out_rows, model), F32),
            shape((model, length), BF),
            shape((length, LANES), BF),
            shape((heads, LANES, LANES), BF),
        ],
        scratch_shapes=[
            pltpu.VMEM((length, model), BF),
            pltpu.VMEM((model, length), BF),
            pltpu.VMEM((model, width), BF),
            pltpu.VMEM((length, LANES), F32),
            pltpu.VMEM((tile, length), F32),
            pltpu.VMEM((tile, length), F32),
            pltpu.SemaphoreType.DMA((5,)),
            pltpu.SemaphoreType.DMA((5,)),
        ],
        compiler_params=params(58),
        cost_estimate=cost(18e9, 12 << 20, 8 << 20),
        name="attend",
    )(place, tokens, *rows_a, segments, picks)


def attend_back_kernel(
    place,
    q_ref,
    k_ref,
    v_ref,
    do_ref,
    o_ref,
    marks_ref,
    table_ref,
    lse_ref,
    tok_t_hbm,
    mid_ref,
    keep_hbm,
    send_hbm,
    d_ref,
    keep_ref,
    send_ref,
    tok_t_ref,
    dq_sum,
    dv_sum,
    dk_sum,
    bias_scr,
    load_sem,
    out_sems,
    *,
    tile,
):
    length = q_ref.shape[0]
    pair = pl.program_id(0)
    load = pltpu.make_async_copy(tok_t_hbm, tok_t_ref, load_sem)

    @pl.when(pair == 0)
    def _():
        load.start()

    core = place[1]
    lane = lax.broadcasted_iota(jnp.int32, (1, LANES), 1)
    zero = jnp.zeros((), BF)
    scale = jnp.asarray(HD**-0.5, BF)
    prod = do_ref[...].astype(F32) * o_ref[...].astype(F32)
    high = prod.astype(BF)
    low = (prod - high.astype(F32)).astype(BF)
    pick = (
        lax.broadcasted_iota(jnp.int32, (8, LANES), 0)
        == lax.broadcasted_iota(jnp.int32, (8, LANES), 1) // HD
    ).astype(BF)
    inner = dotf(pick, high, NT) + dotf(pick, low, NT)
    keys_t = jnp.transpose(k_ref[...] * scale)
    for head in range(2):
        mine = lane // HD == head
        key_marks = dotf(marks_ref[...], table_ref[head]).astype(BF)
        keys = jnp.concatenate([k_ref[...], key_marks], axis=1)
        log_total = lse_ref[pl.ds(2 * pair + head, 1), :]
        for at in range(0, length, tile):
            here = pl.ds(at, tile)
            query = jnp.where(mine, q_ref[here, :] * scale, zero)
            upstream = jnp.where(mine, do_ref[here, :], zero)
            scores = dotf(keys, jnp.concatenate([query, marks_ref[here, :]], axis=1), NT)
            probs = jnp.exp(scores - log_total[:, at : at + tile])
            grad_probs = dotf(v_ref[...], upstream, NT)
            grad_scores = (probs * (grad_probs - inner[head : head + 1, at : at + tile])).astype(BF)
            grad_v = dotf(probs.astype(BF), upstream)
            grad_k = dotf(grad_scores, query)
            dq_sum[head * HD : (head + 1) * HD, here] = dotf(
                keys_t[head * HD : (head + 1) * HD], grad_scores
            )
            if head == 0 and at == 0:
                dv_sum[...] = grad_v
                dk_sum[...] = grad_k
            else:
                dv_sum[...] += grad_v
                dk_sum[...] += grad_k
    d_ref[:, :LANES] = jnp.transpose(dq_sum[...]).astype(BF)
    d_ref[:, LANES : 2 * LANES] = dk_sum[...].astype(BF)
    d_ref[:, 2 * LANES :] = dv_sum[...].astype(BF)
    outs = (keep_ref, send_ref)
    width = 3 * LANES

    @pl.when(pair == 0)
    def _():
        load.wait()

    def write_out(group, count):
        cols = pl.ds(pl.multiple_of(group * width, LANES), count)
        return [
            pltpu.make_async_copy(source.at[:, cols], into.at[:, cols], out_sems.at[number, group])
            for number, (source, into) in enumerate(((send_ref, send_hbm), (keep_ref, keep_hbm)))
        ]

    result = dotf(tok_t_ref[...], d_ref[...]).astype(BF)
    store_pieces(result, core, outs, pl.ds(pl.multiple_of(pair * width, LANES), width))
    for copy in write_out(pair, width):
        copy.start()
    here = pl.ds(pl.multiple_of(pair * LANES, LANES), LANES)
    bias_scr[0:1, here] = col_sum(d_ref[:, :LANES].astype(F32))
    bias_scr[1:2, here] = col_sum(d_ref[:, 2 * LANES :].astype(F32))

    @pl.when(pair == pl.num_programs(0) - 1)
    def _():
        model = mid_ref.shape[1]
        sums = jnp.concatenate(
            [
                mid_ref[0:6, :],
                bias_scr[0:2, :],
                mid_ref[8:16, :],
            ],
            axis=0,
        )
        sums = jnp.concatenate([sums, sums, jnp.zeros((LANES - 2 * PARAMS, model), F32)], axis=0)
        quarter = model // 4
        turned = jnp.transpose(sums)
        kept, sent = [], []
        for r0 in range(2):
            lower = turned[r0 * 2 * quarter : r0 * 2 * quarter + quarter]
            upper = turned[r0 * 2 * quarter + quarter : (r0 + 1) * 2 * quarter]
            kept.append(jnp.where(core == 0, lower, upper))
            sent.append(jnp.where(core == 0, upper, lower))
        total = keep_ref.shape[1]
        store_pieces(
            two_parts(jnp.concatenate(kept + sent, axis=0)), core, outs, slice(total - LANES, total)
        )
        groups = (total - LANES) // width
        last = write_out(groups, LANES)
        for copy in last:
            copy.start()
        for group in range(groups):
            for copy in write_out(group, width):
                copy.wait()
        for copy in last:
            copy.wait()


def attend_back(place, q, k, v, grad_mixed, mixed, marks, table, lse, tok_t, sums):
    length = q.shape[0]
    model = tok_t.shape[0]
    pairs = q.shape[1] // LANES
    width = 3 * LANES
    total = pairs * width + LANES
    whole = lambda dims: pl.BlockSpec(dims, lambda i: (0,) * len(dims))
    block = pl.BlockSpec((length, LANES), lambda i: (0, i))
    return pl.pallas_call(
        functools.partial(attend_back_kernel, tile=512),
        grid=(pairs,),
        in_specs=[SM]
        + [block] * 5
        + [whole(marks.shape), pl.BlockSpec((2, LANES, LANES), lambda i: (i, 0, 0))]
        + [whole(lse.shape), pl.BlockSpec(memory_space=pl.ANY), whole(sums.shape)],
        out_specs=[
            pl.BlockSpec(memory_space=pl.ANY),
            pl.BlockSpec(memory_space=pl.ANY),
            pl.BlockSpec((length, width), lambda i: (0, i)),
        ],
        out_shape=[
            shape((model // 2, total), BF),
            shape((model // 2, total), BF),
            shape((length, pairs * width), BF),
        ],
        scratch_shapes=[
            pltpu.VMEM((model // 2, total), BF),
            pltpu.VMEM((model // 2, total), BF),
            pltpu.VMEM((model, length), BF),
            pltpu.VMEM((LANES, length), F32),
            pltpu.VMEM((length, LANES), F32),
            pltpu.VMEM((length, LANES), F32),
            pltpu.VMEM((8, model), F32),
            pltpu.SemaphoreType.DMA,
            pltpu.SemaphoreType.DMA((2, pairs + 1)),
        ],
        compiler_params=params(54),
        cost_estimate=cost(30e9, 10 << 20, 8 << 20, 1.0),
        name="attend_back",
    )(place, q, k, v, grad_mixed, mixed, marks, table, lse, tok_t, sums)


def two_parts(values):
    lane = lax.broadcasted_iota(jnp.int32, (1, LANES), 1)
    rounded = values.astype(BF)
    return jnp.where(lane < PARAMS, rounded, (values - rounded.astype(F32)).astype(BF))


def both_lanes(values):
    lane = lax.broadcasted_iota(jnp.int32, (1, LANES), 1)
    later = pltpu.roll(values, LANES - PARAMS, 1)
    earlier = pltpu.roll(values, PARAMS, 1)
    return values + jnp.where(lane < PARAMS, later, jnp.where(lane < 2 * PARAMS, earlier, 0.0))


def summed(parts, small):
    total = parts[0].astype(F32)
    for part in parts[1:]:
        total = total + part.astype(F32)
    if not small:
        return total.astype(BF)
    at = total.shape[1] - LANES
    return jnp.concatenate([total[:, :at].astype(BF), two_parts(both_lanes(total[:, at:]))], axis=1)


def piece_order(lhs_ref, core):
    quarter = lhs_ref.shape[1] // 4
    cols = []
    for target in (core, 1 - core):
        for half in range(2):
            start = pl.multiple_of(half * 2 * quarter + target * quarter, quarter)
            cols.append(lhs_ref[:, pl.ds(start, quarter)])
    return jnp.transpose(jnp.concatenate(cols, axis=1))


def store_pieces(result, core, outs, cols):
    quarter = result.shape[0] // 4
    piece = quarter // 4
    for which, target in enumerate((core, 1 - core)):
        for r0 in range(2):
            for r2 in range(2):
                for r3 in range(2):
                    at = which * 2 * quarter + r0 * quarter + r2 * 2 * piece + r3 * piece
                    spot = jnp.where(target == 0, r0 * 4 + r2 * 2 + r3, r3 * 4 + r2 * 2 + r0)
                    rows = pl.ds(pl.multiple_of(spot * piece, piece), piece)
                    outs[which][rows, cols] = result[at : at + piece, :]


def weight_grad(lhs_t, rhs_ref, core, outs, first, tile=512):
    for at in range(0, rhs_ref.shape[1], tile):
        result = dotf(lhs_t, rhs_ref[:, at : at + tile]).astype(BF)
        store_pieces(result, core, outs, slice(first + at, first + at + tile))


def normed(hidden):
    center = hidden - jnp.mean(hidden, axis=-1, keepdims=True)
    spread = jnp.mean(center * center, axis=-1, keepdims=True)
    rate = lax.rsqrt(spread + norm_eps)
    return center * rate, rate


def norm_back(grad, unit, rate):
    return rate * (
        grad
        - jnp.mean(grad, axis=-1, keepdims=True)
        - unit * jnp.mean(grad * unit, axis=-1, keepdims=True)
    )


def col_sum(values):
    return jnp.sum(values, axis=0, keepdims=True)


def middle_kernel(
    place,
    rows_ref,
    tok_hbm,
    cot_hbm,
    mixed_hbm,
    own_hbm,
    near_hbm,
    far_hbm,
    out_hbm,
    dh_hbm,
    do_hbm,
    keep_hbm,
    send_hbm,
    sums_ref,
    tok_ref,
    cot_ref,
    mixed_ref,
    out_ref,
    dh_ref,
    do_ref,
    keep_ref,
    send_ref,
    w_scr,
    act_scr,
    du_scr,
    z_scr,
    df_scr,
    da_scr,
    sems,
    out_sems,
    *,
    tile,
):
    length, model = tok_ref.shape
    core = place[1]
    hidden_count = act_scr.shape[1]
    w_up = slice(0, hidden_count)
    w_down = slice(hidden_count, 2 * hidden_count)
    w_out = slice(2 * hidden_count, w_scr.shape[1])
    waits = {}
    number = 0
    for name, sources in (
        ("out", w_out),
        (0, ((mixed_hbm, mixed_ref), (tok_hbm, tok_ref))),
        ("up", w_up),
        ("down", w_down),
        ("cot", ((cot_hbm, cot_ref),)),
        *((at, ((mixed_hbm, mixed_ref), (tok_hbm, tok_ref))) for at in range(tile, length, tile)),
    ):
        if isinstance(sources, slice):
            copies = gathered_rows(
                place, own_hbm, near_hbm, far_hbm, w_scr, sems, sources, number
            )
        else:
            rows = slice(None) if name == "cot" else slice(name, name + tile)
            copies = [
                pltpu.make_async_copy(source.at[rows, :], into.at[rows, :], sems.at[number + n])
                for n, (source, into) in enumerate(sources)
            ]
        number += len(copies)
        for copy in copies:
            copy.start()
        waits[name] = copies

    def ready(name):
        for copy in waits.pop(name, ()):
            copy.wait()

    pending = []

    def write_out(source, into):
        copy = pltpu.make_async_copy(source, into, out_sems.at[len(pending)])
        copy.start()
        pending.append(copy)

    row = lambda number: rows_ref[number : number + 1, :]
    bias_up = jnp.concatenate([row(8), row(9), row(10), row(11)], axis=1)
    sums = [jnp.zeros((1, model), F32)] * 6
    sum_up = jnp.zeros((1, hidden_count), F32)
    for at in range(0, length, tile):
        here = pl.ds(at, tile)
        ready("out")
        ready(at)
        attn_out = dotf(mixed_ref[here, :], w_scr[:, w_out], NT) + row(4)
        unit_one, rate_one = normed(tok_ref[here, :].astype(F32) + attn_out)
        z_one = unit_one * row(0) + row(1)
        z_low = z_one.astype(BF)
        z_scr[here, :] = z_low
        ready("up")
        up = dotf(z_low, w_scr[:, w_up]) + bias_up
        below = 0.5 * (1.0 + lax.erf(up * (0.5**0.5)))
        slope = below + up * (jnp.exp(-0.5 * up * up) * (1.0 / (2.0 * 3.141592653589793) ** 0.5))
        active = (up * below).astype(BF)
        act_scr[here, :] = active
        ready("down")
        ffn_out = dotf(active, w_scr[:, w_down], NT) + row(5)
        unit_two, rate_two = normed(z_one + ffn_out)
        out_ref[here, :] = (unit_two * row(2) + row(3)).astype(BF)
        ready("cot")
        upstream = cot_ref[here, :].astype(F32)
        grad_two = norm_back(upstream * row(2), unit_two, rate_two)
        down_low = grad_two.astype(BF)
        df_scr[here, :] = down_low
        grad_up = (dotf(down_low, w_scr[:, w_down]) * slope).astype(BF)
        du_scr[here, :] = grad_up
        grad_z = grad_two + dotf(grad_up, w_scr[:, w_up], NT)
        grad_one = norm_back(grad_z * row(0), unit_one, rate_one)
        dh_ref[here, :] = grad_one
        attn_low = grad_one.astype(BF)
        da_scr[here, :] = attn_low
        do_ref[here, :] = dotf(attn_low, w_scr[:, w_out]).astype(BF)
        for source, into in ((out_ref, out_hbm), (dh_ref, dh_hbm), (do_ref, do_hbm)):
            write_out(source.at[here, :], into.at[here, :])
        parts = (
            grad_z * unit_one,
            grad_z,
            upstream * unit_two,
            upstream,
            attn_low.astype(F32),
            down_low.astype(F32),
        )
        sums = [a + col_sum(b) for a, b in zip(sums, parts)]
        sum_up = sum_up + col_sum(grad_up.astype(F32))
    for number in range(6):
        sums_ref[number : number + 1, :] = sums[number]
    sums_ref[6:8, :] = jnp.zeros((2, model), F32)
    for number in range(4):
        sums_ref[8 + number : 9 + number, :] = sum_up[:, number * model : (number + 1) * model]
    sums_ref[12:16, :] = jnp.zeros((4, model), F32)
    outs = (keep_ref, send_ref)
    for lhs, rhs, cols in (
        (z_scr, du_scr, w_up),
        (df_scr, act_scr, w_down),
        (da_scr, mixed_ref, w_out),
    ):
        weight_grad(piece_order(lhs, core), rhs, core, outs, cols.start)
        for source, into in ((send_ref, send_hbm), (keep_ref, keep_hbm)):
            write_out(source.at[:, cols], into.at[:, cols])
    for copy in pending:
        copy.wait()


def middle(place, tokens, cotangent, mixed, rows, own, near, far):
    length, model = tokens.shape
    width = own.shape[1]
    hidden_count = (width - mixed.shape[1]) // 2
    tile = 512
    anywhere = pl.BlockSpec(memory_space=pl.ANY)
    outs = [
        shape((length, model), BF),
        shape((length, model), F32),
        shape((length, mixed.shape[1]), BF),
        shape((model // 2, width), BF),
        shape((model // 2, width), BF),
    ]
    vmem = lambda x: pltpu.VMEM(x.shape, x.dtype)
    return pl.pallas_call(
        functools.partial(middle_kernel, tile=tile),
        in_specs=[SM, VM] + [anywhere] * 5 + [VM],
        out_specs=[anywhere] * 5 + [VM],
        out_shape=outs + [shape((16, model), F32)],
        scratch_shapes=[vmem(x) for x in (tokens, cotangent, mixed, *outs)]
        + [
            pltpu.VMEM((model, width), BF),
            pltpu.VMEM((length, hidden_count), BF),
            pltpu.VMEM((length, hidden_count), BF),
            pltpu.VMEM((length, model), BF),
            pltpu.VMEM((length, model), BF),
            pltpu.VMEM((length, model), BF),
            pltpu.SemaphoreType.DMA((10 + 2 * (length // tile),)),
            pltpu.SemaphoreType.DMA((3 * (length // tile) + 6,)),
        ],
        compiler_params=params(58),
        cost_estimate=cost(16e9, 16 << 20, 4 << 20, 1.0),
        name="middle",
    )(place, rows, tokens, cotangent, mixed, own, near, far)


def input_grad_kernel(
    place, dh_ref, d_ref, own_ref, near_ref, side_ref, far_near_ref, far_side_ref, out_ref, w_scr, sems
):
    eighth_refs = (own_ref, near_ref, side_ref, far_near_ref, far_side_ref)
    width = d_ref.shape[1]

    @pl.when(pl.program_id(0) == 0)
    def _():
        copies = gathered_eighths(place, *eighth_refs, w_scr, sems)
        for copy in copies:
            copy.start()
        for copy in copies:
            copy.wait()

    out_ref[...] = (dh_ref[...] + dotf(d_ref[...], w_scr[:, :width], NT)).astype(BF)


def input_gradient(place, dh, d, rows_a):
    length, model = dh.shape
    tile = 256
    anywhere = pl.BlockSpec(memory_space=pl.ANY)
    rows = lambda width: pl.BlockSpec((tile, width), lambda i: (i, 0))
    return pl.pallas_call(
        input_grad_kernel,
        grid=(length // tile,),
        in_specs=[SM, rows(model), rows(d.shape[1])] + [anywhere] * 5,
        out_specs=rows(model),
        out_shape=shape((length, model), BF),
        scratch_shapes=[pltpu.VMEM((model, rows_a[0].shape[1]), BF), pltpu.SemaphoreType.DMA((5,))],
        compiler_params=params(16),
        cost_estimate=cost(2 * length * model * d.shape[1], 8 << 20),
        name="input_gradient",
    )(place, dh, d, *rows_a)


def add_low(a, b):
    return (a.astype(F32) + b.astype(F32)).astype(BF)


def add_parts_kernel(place, *refs, small):
    refs[-1][...] = summed([ref[...] for ref in refs[:-1]], small)


def add_parts(place, parts, give, small):
    rows = min(part.shape[0] for part in parts)
    rows = rows // 2 if give else rows
    width = parts[0].shape[1]

    def pick(part):
        if part.shape[0] == rows:
            return pl.BlockSpec((rows, width), lambda i, place: (0, 0))
        return pl.BlockSpec((rows, width), lambda i, place: (1 - place[6] if give else place[6], 0))

    return pl.pallas_call(
        functools.partial(add_parts_kernel, small=small),
        grid_spec=pltpu.PrefetchScalarGridSpec(
            num_scalar_prefetch=1,
            grid=(1,),
            in_specs=[pick(part) for part in parts],
            out_specs=pl.BlockSpec((rows, width), lambda i, place: (0, 0)),
        ),
        out_shape=shape((rows, width), BF),
        compiler_params=params(8),
        cost_estimate=cost(len(parts) * rows * width, 2 * len(parts) * rows * width),
        name="add_parts",
    )(place, *parts)


def flip(count, bit):
    return [(i, i ^ (1 << bit)) for i in range(count)]


def mixed_flip(count, even, odd):
    return [(i, i ^ (1 << (odd if (i >> 1) & 1 else even))) for i in range(2 * count)]


STEPS = ((0, 2), (2, 3), (3, 0))


def mixed_mask(count, mask):
    pairs = []
    for i in range(2 * count):
        partner = i
        for bit, step in zip((2, 1), STEPS):
            if mask & bit:
                partner ^= 1 << step[(i >> 1) & 1]
        pairs.append((i, partner))
    return pairs


def split_kernel(place, keep_ref, got_ref, *outs, small):
    piece = outs[0].shape[0]
    mine = place[3] * 2 + place[4]
    for mask, out in enumerate(outs):
        rows = pl.ds(pl.multiple_of((mine ^ mask) * piece, piece), piece)
        out[...] = summed([keep_ref[rows, :], got_ref[rows, :]], small)


def swap_two(value, count, mask):
    return lax.ppermute(value, ("dp", "shard"), mixed_mask(count, mask))


def split(place, keep, got, small):
    rows, width = keep.shape
    steps = 1 if small else 4
    step = width // steps
    whole = pl.BlockSpec((rows, step), lambda i: (0, i))
    part = pl.BlockSpec((rows // 4, step), lambda i: (0, i))
    return pl.pallas_call(
        functools.partial(split_kernel, small=small),
        grid=(steps,),
        in_specs=[SM, whole, whole],
        out_specs=[part] * 4,
        out_shape=[shape((rows // 4, width), BF)] * 4,
        compiler_params=params(16),
        cost_estimate=cost(rows * width, 6 * rows * width),
        name="split",
    )(place, keep, got)


def swap_core(value, count):
    return lax.ppermute(value, "dp", flip(count, 0))


def swap_mixed(value, count, step):
    return lax.ppermute(value, ("dp", "shard"), mixed_flip(count, *step))


def swap_bit(value, count, bit):
    return lax.ppermute(value, "dp", flip(count, bit))


def after(value, *others):
    return lax.optimization_barrier((value,) + others)[0]


def adam_values(scalars, weight_ref, mean_ref, square_ref, grad, decay, outs):
    weight = weight_ref[...]
    mean_out = beta_one * mean_ref[...] + (1.0 - beta_one) * grad
    square_out = beta_two * square_ref[...] + (1.0 - beta_two) * grad * grad
    mean_hat = mean_out * scalars[2]
    square_hat = square_out * scalars[3]
    weight_out = weight - scalars[0] * (
        mean_hat / (jnp.sqrt(square_hat) + adam_eps) + decay * weight
    )
    outs[0][...] = weight_out
    outs[1][...] = mean_out
    outs[2][...] = square_out
    outs[3][...] = weight_out.astype(BF)


def piece_block(place, own, flips):
    bit2, bit3 = (place[4], place[5]) if own else (place[5], place[4])
    core = place[1] if own else 1 - place[1]
    return core * 4 + (bit2 ^ (flips >> 1)) * 2 + (bit3 ^ (flips & 1))


def chosen(index, values):
    result = values[-1]
    for number in range(len(values) - 2, -1, -1):
        result = jnp.where(index == number, values[number], result)
    return result


def adam_ffn_kernel(place, scalars, *refs, count):
    step = pl.program_id(0)
    stack, _, width = refs[count].shape
    for number in range(count):

        @pl.when(step == number)
        def _():
            grad = jnp.stack(
                [refs[number][:, w * width : (w + 1) * width].astype(F32) for w in range(stack)]
            )
            adam_values(scalars, *refs[count : count + 3], grad, scalars[1], refs[-4:])


def adam_ffn(place, scalars, pieces, state, before):
    count = len(pieces)
    stack, rows, width = state[0].shape
    step = rows // 8
    grads = [piece[0] for piece in pieces]
    take = pl.BlockSpec((step, stack * width), lambda p, place, sc: (0, 0))
    block = pl.BlockSpec(
        (stack, step, width),
        lambda p, place, sc: (0, chosen(p, [piece_block(place, *x[1:]) for x in pieces]), 0),
    )
    before = list(before or ())
    return pl.pallas_call(
        functools.partial(adam_ffn_kernel, count=count),
        grid_spec=pltpu.PrefetchScalarGridSpec(
            num_scalar_prefetch=2,
            grid=(count,),
            in_specs=[take] * count + [block] * 3 + [pl.BlockSpec(memory_space=pl.ANY)] * len(before),
            out_specs=[block] * 4,
        ),
        out_shape=[shape(state[0].shape, F32)] * 3 + [shape(state[0].shape, BF)],
        input_output_aliases={5 + count + n: n for n in range(len(before))},
        compiler_params=params(24),
        cost_estimate=cost(20 * count * step * width, 28 * count * step * width),
        name="adam_ffn",
    )(place, scalars, *grads, *state, *before)


def adam_attn_kernel(place, scalars, *refs, count, orders, small):
    grads, outer, state = refs[:count], refs[count : 2 * count], refs[2 * count : 2 * count + 3]
    rest = refs[2 * count + 3 :]
    step = pl.program_id(0)
    if small:
        little, (sw, sm, ss), rest = rest[:small], rest[small : small + 3], rest[small + 3 + 4 :]
        outs, small_outs, scr = rest[:4], rest[4:8], rest[8]

        @pl.when(step == 0)
        def _():
            for ref, order in zip(little, orders):
                rows = ref.shape[0]
                where = pl.ds(pl.multiple_of(piece_block(place, *order) * rows, rows), rows)
                scr[where, :] = ref[...].astype(F32)
            turned = jnp.transpose(both_lanes(scr[...]))[: sw.shape[0], :]
            adam_values(scalars, sw, sm, ss, turned, 0.0 * scalars[1], small_outs)
    else:
        outs = rest[-4:]
    for number in range(count):

        @pl.when(step == number)
        def _():
            grad = grads[number][...].astype(F32)
            pairs = grad.shape[1] // (3 * LANES)
            parts = [
                grad[:, p * 3 * LANES + kind * LANES : p * 3 * LANES + (kind + 1) * LANES]
                for kind in range(3)
                for p in range(pairs)
            ]
            parts.append(outer[number][...].astype(F32))
            adam_values(scalars, *state, jnp.concatenate(parts, axis=1), scalars[1], outs)


def adam_attn(place, scalars, pieces, pieces_b, state, before, every=None, small=None):
    count = len(pieces)
    rows, width = state[0].shape
    step = rows // 8
    out_width = width // 4
    grads = [piece[0] for piece in pieces]
    outer = [piece[0] for piece in pieces_b]
    last = outer[0].shape[1] // out_width - 1
    block = pl.BlockSpec(
        (step, width),
        lambda p, place, sc: (chosen(p, [piece_block(place, *x[1:]) for x in pieces]), 0),
    )
    anywhere = pl.BlockSpec(memory_space=pl.ANY)
    in_specs = [pl.BlockSpec(grads[0].shape, lambda p, place, sc: (0, 0))] * count
    in_specs += [pl.BlockSpec((step, out_width), lambda p, place, sc: (0, last))] * count
    in_specs += [block] * 3
    operands = [place, scalars, *grads, *outer, *state]
    out_specs = [block] * 4
    out_shape = [shape(state[0].shape, F32)] * 3 + [shape(state[0].shape, BF)]
    scratch = []
    if small:
        whole = pl.BlockSpec(small[0].shape, lambda p, place, sc: (0, 0))
        at = grads[0].shape[1] // LANES - 1
        in_specs += [pl.BlockSpec((step, LANES), lambda p, place, sc: (0, at))] * len(every)
        in_specs += [whole] * 3
        operands += [piece[0] for piece in every] + list(small)
        out_specs += [whole] * 4
        out_shape += [shape(small[0].shape, F32)] * 3 + [shape(small[0].shape, BF)]
        scratch = [pltpu.VMEM((rows, LANES), F32)]
    before = list(before or ())
    aliases = {len(operands) + n: n for n in range(len(before))}
    return pl.pallas_call(
        functools.partial(
            adam_attn_kernel,
            count=count,
            orders=[piece[1:] for piece in every or ()],
            small=len(every or ()),
        ),
        grid_spec=pltpu.PrefetchScalarGridSpec(
            num_scalar_prefetch=2,
            grid=(count,),
            in_specs=in_specs + [anywhere] * len(before),
            out_specs=out_specs,
            scratch_shapes=scratch,
        ),
        out_shape=out_shape,
        input_output_aliases=aliases,
        compiler_params=params(24),
        cost_estimate=cost(20 * count * step * width, 28 * count * step * width),
        name="adam_attn",
    )(*operands, *before)


def from_neighbour(value):
    return lax.ppermute(value, "shard", [(0, 1), (1, 0)])


def local(
    count,
    tokens,
    cotangent,
    segments,
    random_blocks,
    step_count,
    adam_rates,
    attn_master,
    attn_mean,
    attn_square,
    ffn_master,
    ffn_mean,
    ffn_square,
    small_master,
    small_mean,
    small_square,
):
    replica = lax.axis_index("dp")
    shard = lax.axis_index("shard")
    core, low, high = replica & 1, (replica >> 1) & 1, (replica >> 2) & 1
    even = core == 0
    place = jnp.stack(
        [
            shard,
            core,
            low,
            jnp.where(even, shard, low),
            jnp.where(even, low, high),
            jnp.where(even, high, low),
            jnp.where(even, high, shard),
        ]
    ).astype(jnp.int32)
    pairs = attn_master.shape[1] // 4 // LANES
    near_a = from_neighbour(pack_eighth_a(attn_master, small_master))
    quarter_b = pack_quarter_b(place, attn_master, ffn_master)
    near_a = after(near_a, quarter_b)
    near_b = from_neighbour(after(quarter_b, near_a))
    side_a = swap_bit(near_a, count, 1)
    own_a, own_b = pack_own(attn_master, ffn_master, small_master)
    side_a = after(side_a, own_a)
    rows_a = (own_a, near_a, side_a, swap_core(near_a, count), swap_core(side_a, count))
    q, k, v, mixed, lse, rows, tok_t, marks, table = attend(
        place, tokens, rows_a, segments, random_blocks
    )
    far_b = swap_core(after(near_b, lse), count)
    layer_out, dh, grad_mixed, keep_b, send_b, sums = middle(
        place, tokens, cotangent, mixed, rows, own_b, near_b, far_b
    )
    parts_b = list(split(place, keep_b, swap_core(send_b, count), False))
    parts_b = parts_b[:1] + [swap_two(parts_b[mask], count, mask) for mask in (1, 2, 3)]
    keep_a, send_a, d = attend_back(
        place, q, k, v, after(grad_mixed, parts_b[0]), mixed, marks, table, lse, tok_t, sums
    )
    got_a = swap_core(send_a, count)
    parts_b = parts_b[:1] + [after(part, d) for part in parts_b[1:]]
    got_b = swap_mixed(add_parts(place, parts_b, True, False), count, STEPS[2])

    step_value = step_count[0].astype(F32)
    scalars = jnp.stack(
        [
            adam_rates[0],
            adam_rates[1],
            1.0 / (1.0 - beta_one**step_value),
            1.0 / (1.0 - beta_two**step_value),
        ]
    )
    ffn_state = (ffn_master, ffn_mean, ffn_square)
    attn_state = (attn_master, attn_mean, attn_square)
    small_state = (small_master, small_mean, small_square)
    bits = [bit for bit in range(3, count.bit_length() - 1)]

    parts_a = list(split(place, keep_a, got_a, True))
    parts_a = parts_a[:1] + [swap_two(parts_a[mask], count, mask) for mask in (1, 2, 3)]
    total_b = add_parts(place, parts_b + [after(got_b, parts_a[0])], False, False)
    got_b = swap_bit(total_b, count, bits[0])
    input_grad = input_gradient(place, after(dh, total_b), d, rows_a)
    parts_a = parts_a[:1] + [after(part, input_grad) for part in parts_a[1:]]
    got_a = swap_mixed(add_parts(place, parts_a, True, True), count, STEPS[2])
    total_a = add_parts(place, parts_a + [got_a], False, True)
    got_a = swap_bit(total_a, count, bits[0])
    total_b = add_low(total_b, after(got_b, total_a))
    for bit in bits[1:]:
        total_b = add_low(total_b, swap_bit(total_b, count, bit))
    first, second = (3, 2), (2, 3)

    def wave(values, flips):
        return [(v, True, f) for v, f in zip(values, flips)] + [
            (swap_core(v, count), False, f) for v, f in zip(values, flips)
        ]

    b_one = wave([total_b], [0])
    got_b = [swap_mixed(total_b, count, first), swap_mixed(total_b, count, second)]
    ffn_new = adam_ffn(place, scalars, b_one, ffn_state, None)
    total_a = add_parts(place, [total_a, after(got_a, ffn_new[0])], False, True)
    for bit in bits[1:]:
        total_a = add_parts(place, [total_a, swap_bit(total_a, count, bit)], False, True)
    a_one = wave([total_a], [0])
    got_a = [swap_mixed(total_a, count, first), swap_mixed(total_a, count, second)]
    got_b = [after(piece, ffn_new[0], total_a) for piece in got_b]
    b_two = wave(got_b, [1, 2])
    got_b = swap_mixed(got_b[0], count, second)
    attn_new = adam_attn(place, scalars, a_one, b_one, attn_state, None)
    ffn_new = adam_ffn(place, scalars, b_two, ffn_state, ffn_new)
    got_a = [after(piece, attn_new[0]) for piece in got_a]
    a_two = wave(got_a, [1, 2])
    got_a = swap_mixed(got_a[0], count, second)
    b_three = wave([after(got_b, ffn_new[0])], [3])
    attn_new = adam_attn(place, scalars, a_two, b_two, attn_state, attn_new)
    a_three = wave([after(got_a, attn_new[0])], [3])
    ffn_new = adam_ffn(place, scalars, b_three, ffn_state, ffn_new)
    attn_new = adam_attn(
        place,
        scalars,
        a_three,
        b_three,
        attn_state,
        attn_new,
        a_one + a_two + a_three,
        small_state,
    )
    return (layer_out, input_grad) + tuple(attn_new[:4]) + tuple(ffn_new) + tuple(attn_new[4:])


def solution(mesh):
    tokens_in = P(("dp", "shard"), None)
    rows_in = P("shard", None)
    stack_in = P(None, "shard", None)
    cols_in = P(None, "shard")
    placed = (
        (tokens_in,) * 3
        + (P(("dp", "shard"), None, None, None), P(), P())
        + (rows_in,) * 3
        + (stack_in,) * 3
        + (cols_in,) * 3
    )
    return jax.shard_map(
        functools.partial(local, mesh.shape["dp"]),
        mesh=mesh,
        in_specs=placed,
        out_specs=(tokens_in,) * 2 + (rows_in,) * 4 + (stack_in,) * 4 + (cols_in,) * 4,
        check_vma=False,
    )
```

```python
import functools

import jax
import jax.numpy as jnp
from jax import lax
from jax.experimental import pallas as pl
from jax.experimental.pallas import tpu as pltpu
from jax.sharding import PartitionSpec as P

HD = 64
LANES = 128
PARAMS = 16
BF = jnp.bfloat16
F32 = jnp.float32
BLOCKED = -(2.0**100)
NN = (((1,), (0,)), ((), ()))
NT = (((1,), (1,)), ((), ()))
TN = (((0,), (0,)), ((), ()))

norm_eps = 1e-12
beta_one = 0.9
beta_two = 0.999
adam_eps = 1e-08


def dotf(a, b, dims=NN):
    return lax.dot_general(a, b, dims, preferred_element_type=F32)


def params(mebibytes):
    return pltpu.CompilerParams(vmem_limit_bytes=mebibytes << 20)


def cost(flops, bytes_accessed, transcendentals=0, share=0.05):
    return pl.CostEstimate(
        flops=int(flops * share),
        bytes_accessed=int(bytes_accessed * share),
        transcendentals=int(transcendentals * share),
    )


def shape(dims, dtype):
    return jax.ShapeDtypeStruct(dims, dtype)


VM = pl.BlockSpec(memory_space=pltpu.VMEM)
SM = pl.BlockSpec(memory_space=pltpu.SMEM)


def token_marks(segments, blocks):
    length = segments.shape[1]
    row = lax.broadcasted_iota(jnp.int32, (LANES, length), 0)
    block_of = lax.broadcasted_iota(jnp.int32, (LANES, length), 1) // (length // blocks)
    marks = jnp.where((row == block_of) | (row == blocks + segments), 1.0, 0.0)
    return jnp.transpose(marks).astype(BF)


def head_table(picks, slots, blocks):
    row = lax.broadcasted_iota(jnp.int32, (LANES, LANES), 0)
    col = lax.broadcasted_iota(jnp.int32, (LANES, LANES), 1)
    seen = (jnp.abs(row - col) <= 1) | (row == 0) | (row == blocks - 1)
    seen = seen | (col == 0) | (col == blocks - 1)
    for slot in range(slots):
        seen = seen | (row == picks[slot : slot + 1, :])
    bad_block = (row < blocks) & (col < blocks) & ~seen
    bad_segment = (row >= blocks) & (col >= blocks) & (row != col)
    return jnp.where(bad_block | bad_segment, BLOCKED, 0.0).astype(BF)


def grouped_a(kinds):
    return [
        kind[:, at : at + LANES] for at in range(0, kinds[0].shape[1], LANES) for kind in kinds
    ]


def turned_small(small):
    fill = jnp.zeros((LANES - small.shape[0], small.shape[1]), F32)
    return jnp.transpose(jnp.concatenate([small, fill], axis=0))


def packed_b(attn_ref, ffn_ref, first):
    return jnp.concatenate([ffn_ref[0], ffn_ref[1], attn_ref[:, first:]], axis=1).astype(BF)


def pack_a_kernel(attn_hbm, small_hbm, out_ref, attn_ref, small_ref, sems):
    eighth, width = attn_ref.shape
    replica = lax.axis_index("dp")
    core, low = replica & 1, (replica >> 1) & 1
    rows = pl.ds(pl.multiple_of((2 * core + low) * eighth, eighth), eighth)
    cols = pl.ds(pl.multiple_of(core * 2 * eighth, 2 * eighth), 2 * eighth)
    copies = [pltpu.make_async_copy(small_hbm.at[:, cols], small_ref, sems.at[3])]
    feat = width // 3
    for kind in range(3):
        here = slice(kind * feat, (kind + 1) * feat)
        copies.append(
            pltpu.make_async_copy(attn_hbm.at[rows, here], attn_ref.at[:, here], sems.at[kind])
        )
    for copy in copies:
        copy.start()
    for copy in copies:
        copy.wait()
    small = turned_small(small_ref[...])
    small = jnp.where(low == 0, small[:eighth], small[eighth:])
    kinds = [attn_ref[:, kind * feat : (kind + 1) * feat] for kind in range(3)]
    out_ref[...] = jnp.concatenate(grouped_a(kinds) + [small], axis=1).astype(BF)


def pack_b_kernel(place, attn_ref, ffn_ref, out_ref):
    out_ref[...] = packed_b(attn_ref, ffn_ref, 0)


def pack_own_kernel(attn_ref, ffn_ref, small_ref, a_ref, b_ref):
    feat = attn_ref.shape[1] // 4
    kinds = [attn_ref[:, kind * feat : (kind + 1) * feat] for kind in range(3)]
    parts = grouped_a(kinds) + [turned_small(small_ref[...])]
    a_ref[...] = jnp.concatenate(parts, axis=1).astype(BF)
    b_ref[...] = packed_b(attn_ref, ffn_ref, attn_ref.shape[1] // 4 * 3)


def pack_eighth_a(attn, small):
    eighth = attn.shape[0] // 4
    width = attn.shape[1] // 4 * 3
    anywhere = pl.BlockSpec(memory_space=pl.ANY)
    return pl.pallas_call(
        pack_a_kernel,
        in_specs=[anywhere] * 2,
        out_specs=VM,
        out_shape=shape((eighth, width + LANES), BF),
        scratch_shapes=[
            pltpu.VMEM((eighth, width), F32),
            pltpu.VMEM((small.shape[0], 2 * eighth), F32),
            pltpu.SemaphoreType.DMA((4,)),
        ],
        compiler_params=params(58),
        cost_estimate=cost(1e6, 2 << 20),
        name="pack_eighth_a",
    )(attn, small)


def pack_quarter_b(place, attn, ffn):
    quarter = attn.shape[0] // 2
    feat = attn.shape[1] // 4
    hidden_count = ffn.shape[2]
    width = 2 * hidden_count + feat
    return pl.pallas_call(
        pack_b_kernel,
        grid_spec=pltpu.PrefetchScalarGridSpec(
            num_scalar_prefetch=1,
            grid=(1,),
            in_specs=[
                pl.BlockSpec((quarter, feat), lambda i, place: (place[1], 3)),
                pl.BlockSpec((2, quarter, hidden_count), lambda i, place: (0, place[1], 0)),
            ],
            out_specs=pl.BlockSpec((quarter, width), lambda i, place: (0, 0)),
        ),
        out_shape=shape((quarter, width), BF),
        compiler_params=params(12),
        cost_estimate=cost(1e6, 4 << 20),
        name="pack_quarter_b",
    )(place, attn, ffn)


def pack_own(attn, ffn, small):
    rows = attn.shape[0]
    step = rows // 2
    width_a = attn.shape[1] // 4 * 3 + LANES
    width_b = 2 * ffn.shape[2] + attn.shape[1] // 4
    return pl.pallas_call(
        pack_own_kernel,
        grid=(2,),
        in_specs=[
            pl.BlockSpec((step, attn.shape[1]), lambda i: (i, 0)),
            pl.BlockSpec((2, step, ffn.shape[2]), lambda i: (0, i, 0)),
            pl.BlockSpec((small.shape[0], step), lambda i: (0, i)),
        ],
        out_specs=[
            pl.BlockSpec((step, width_a), lambda i: (i, 0)),
            pl.BlockSpec((step, width_b), lambda i: (i, 0)),
        ],
        out_shape=[shape((rows, width_a), BF), shape((rows, width_b), BF)],
        compiler_params=params(16),
        cost_estimate=cost(1e6, 10 << 20),
        name="pack_own",
    )(attn, ffn, small)


def gathered_eighths(place, own_ref, near_ref, side_ref, far_near_ref, far_side_ref, into, sems):
    half = own_ref.shape[0]
    eighth = near_ref.shape[0]
    shard, core, low = place[0], place[1], place[2]
    other = (1 - shard) * half
    copies = []
    for number, (ref, start, count) in enumerate(
        (
            (own_ref, shard * half, half),
            (near_ref, other + (2 * core + low) * eighth, eighth),
            (side_ref, other + (2 * core + 1 - low) * eighth, eighth),
            (far_near_ref, other + (2 * (1 - core) + low) * eighth, eighth),
            (far_side_ref, other + (2 * (1 - core) + 1 - low) * eighth, eighth),
        )
    ):
        rows = pl.ds(pl.multiple_of(start, eighth), count)
        copies.append(pltpu.make_async_copy(ref, into.at[rows, :], sems.at[number]))
    return copies


def gathered_rows(place, own_ref, near_ref, far_ref, into, sems, cols=slice(None), first=0):
    half = own_ref.shape[0]
    quarter = near_ref.shape[0]
    shard = place[0]
    core = place[1]
    other = (1 - shard) * half
    copies = []
    for number, (ref, start, count) in enumerate(
        (
            (own_ref, shard * half, half),
            (near_ref, other + core * quarter, quarter),
            (far_ref, other + (1 - core) * quarter, quarter),
        )
    ):
        rows = pl.ds(pl.multiple_of(start, quarter), count)
        copies.append(
            pltpu.make_async_copy(ref.at[:, cols], into.at[rows, cols], sems.at[first + number])
        )
    return copies


def attend_kernel(
    place,
    tok_hbm,
    own_ref,
    near_ref,
    side_ref,
    far_near_ref,
    far_side_ref,
    seg_ref,
    picks_ref,
    q_ref,
    k_ref,
    v_ref,
    o_ref,
    lse_ref,
    rows_ref,
    tok_t_hbm,
    marks_ref,
    table_ref,
    tok_ref,
    tok_t_ref,
    w_scr,
    lse_scr,
    even,
    odd,
    sems,
    tok_sems,
    *,
    tile,
    slots,
    blocks,
):
    length = q_ref.shape[0]
    pair = pl.program_id(0)
    lane = lax.broadcasted_iota(jnp.int32, (1, LANES), 1)
    zero = jnp.zeros((), BF)

    eighth_refs = (own_ref, near_ref, side_ref, far_near_ref, far_side_ref)

    @pl.when(pair == 0)
    def _():
        copies = gathered_eighths(place, *eighth_refs, w_scr, sems)
        step = length // 4
        loads = [
            pltpu.make_async_copy(
                tok_hbm.at[n * step : (n + 1) * step, :],
                tok_ref.at[n * step : (n + 1) * step, :],
                tok_sems.at[n],
            )
            for n in range(4)
        ]
        for copy in copies + loads:
            copy.start()
        lse_scr[...] = jnp.zeros_like(lse_scr)
        marks_ref[...] = token_marks(seg_ref[...], blocks)
        for load in loads:
            load.wait()
        tok_t_ref[...] = piece_order(tok_ref, place[1])
        pltpu.make_async_copy(tok_t_ref, tok_t_hbm, tok_sems.at[4]).start()
        for copy in copies:
            copy.wait()
        small = w_scr[:, w_scr.shape[1] - LANES :].astype(F32)
        rows_ref[...] = jnp.transpose(small)[: rows_ref.shape[0], :]

    cols = pl.ds(pl.multiple_of(pair * 3 * LANES, LANES), 3 * LANES)
    here = pl.ds(pl.multiple_of(pair * LANES, LANES), LANES)
    bias = jnp.concatenate(
        [rows_ref[6:7, here], jnp.zeros((1, LANES), F32), rows_ref[7:8, here]], axis=1
    )
    qkv = (dotf(tok_ref[...], w_scr[:, cols]) + bias).astype(BF)
    q_ref[...] = qkv[:, :LANES]
    k_ref[...] = qkv[:, LANES : 2 * LANES]
    v_ref[...] = qkv[:, 2 * LANES :]
    keys, values = [], []
    for head in range(2):
        table_ref[head] = head_table(picks_ref[head], slots, blocks)
        key_marks = dotf(marks_ref[...], table_ref[head]).astype(BF)
        keys.append(jnp.concatenate([k_ref[...], key_marks], axis=1))
        values.append(jnp.where(lane // HD == head, v_ref[...], zero))
    steps = [(at, head) for at in range(0, length, tile) for head in range(2)]
    held = [even, odd]

    def score(index):
        at, head = steps[index]
        rows = pl.ds(at, tile)
        query = jnp.where(lane // HD == head, q_ref[rows, :] * jnp.asarray(HD**-0.5, BF), zero)
        return dotf(jnp.concatenate([query, marks_ref[rows, :]], axis=1), keys[head], NT)

    held[0][...] = score(0)
    first = None
    for index, (at, head) in enumerate(steps):
        rows = pl.ds(at, tile)
        if index + 1 < len(steps):
            held[(index + 1) % 2][...] = score(index + 1)
        now = held[index % 2]
        top = jnp.max(now[...], axis=1, keepdims=True)
        raised = jnp.exp(now[...] - top)
        total = jnp.sum(raised, axis=1, keepdims=True)
        mixed = dotf(raised.astype(BF), values[head]) * (1.0 / total)
        if head == 0:
            first = mixed
        else:
            o_ref[rows, :] = (first + mixed).astype(BF)
        lse_scr[rows, :] = jnp.where(
            lane == 2 * pair + head, top + jnp.log(total), lse_scr[rows, :]
        )

    @pl.when(pair == pl.num_programs(0) - 1)
    def _():
        lse_ref[...] = jnp.transpose(lse_scr[...])[: lse_ref.shape[0], :]
        pltpu.make_async_copy(tok_t_ref, tok_t_hbm, tok_sems.at[4]).wait()


def attend(place, tokens, rows_a, segments, random_blocks):
    length, model = tokens.shape
    blocks, heads, slots = random_blocks.shape[1:]
    picks = jnp.pad(
        random_blocks[0].transpose(1, 2, 0),
        ((0, 0), (0, 8 - slots), (0, LANES - blocks)),
        constant_values=-1,
    )
    width = rows_a[0].shape[1]
    pairs = (width - LANES) // (3 * LANES)
    tile = 256
    whole = lambda dims: pl.BlockSpec(dims, lambda i: (0,) * len(dims))
    anywhere = pl.BlockSpec(memory_space=pl.ANY)
    block = pl.BlockSpec((length, LANES), lambda i: (0, i))
    out_rows = 16
    return pl.pallas_call(
        functools.partial(attend_kernel, tile=tile, slots=slots, blocks=blocks),
        grid=(pairs,),
        in_specs=[
            SM,
            anywhere,
            anywhere,
            anywhere,
            anywhere,
            anywhere,
            anywhere,
            whole((1, length)),
            pl.BlockSpec((2, 8, LANES), lambda i: (i, 0, 0)),
        ],
        out_specs=[
            block,
            block,
            block,
            block,
            whole((out_rows, length)),
            whole((out_rows, model)),
            anywhere,
            whole((length, LANES)),
            pl.BlockSpec((2, LANES, LANES), lambda i: (i, 0, 0)),
        ],
        out_shape=[shape((length, pairs * LANES), BF)] * 4
        + [
            shape((out_rows, length), F32),
            shape((out_rows, model), F32),
            shape((model, length), BF),
            shape((length, LANES), BF),
            shape((heads, LANES, LANES), BF),
        ],
        scratch_shapes=[
            pltpu.VMEM((length, model), BF),
            pltpu.VMEM((model, length), BF),
            pltpu.VMEM((model, width), BF),
            pltpu.VMEM((length, LANES), F32),
            pltpu.VMEM((tile, length), F32),
            pltpu.VMEM((tile, length), F32),
            pltpu.SemaphoreType.DMA((5,)),
            pltpu.SemaphoreType.DMA((5,)),
        ],
        compiler_params=params(58),
        cost_estimate=cost(18e9, 12 << 20, 8 << 20),
        name="attend",
    )(place, tokens, *rows_a, segments, picks)


def attend_back_kernel(
    place,
    q_ref,
    k_ref,
    v_ref,
    do_ref,
    o_ref,
    marks_ref,
    table_ref,
    lse_ref,
    tok_t_hbm,
    mid_ref,
    keep_hbm,
    send_hbm,
    d_ref,
    keep_ref,
    send_ref,
    tok_t_ref,
    dq_sum,
    dv_sum,
    dk_sum,
    bias_scr,
    load_sem,
    out_sems,
    *,
    tile,
):
    length = q_ref.shape[0]
    pair = pl.program_id(0)
    load = pltpu.make_async_copy(tok_t_hbm, tok_t_ref, load_sem)

    @pl.when(pair == 0)
    def _():
        load.start()

    core = place[1]
    lane = lax.broadcasted_iota(jnp.int32, (1, LANES), 1)
    zero = jnp.zeros((), BF)
    scale = jnp.asarray(HD**-0.5, BF)
    prod = do_ref[...].astype(F32) * o_ref[...].astype(F32)
    high = prod.astype(BF)
    low = (prod - high.astype(F32)).astype(BF)
    pick = (
        lax.broadcasted_iota(jnp.int32, (8, LANES), 0)
        == lax.broadcasted_iota(jnp.int32, (8, LANES), 1) // HD
    ).astype(BF)
    inner = dotf(pick, high, NT) + dotf(pick, low, NT)
    keys_t = jnp.transpose(k_ref[...] * scale)
    for head in range(2):
        mine = lane // HD == head
        key_marks = dotf(marks_ref[...], table_ref[head]).astype(BF)
        keys = jnp.concatenate([k_ref[...], key_marks], axis=1)
        log_total = lse_ref[pl.ds(2 * pair + head, 1), :]
        for at in range(0, length, tile):
            here = pl.ds(at, tile)
            query = jnp.where(mine, q_ref[here, :] * scale, zero)
            upstream = jnp.where(mine, do_ref[here, :], zero)
            scores = dotf(keys, jnp.concatenate([query, marks_ref[here, :]], axis=1), NT)
            probs = jnp.exp(scores - log_total[:, at : at + tile])
            grad_probs = dotf(v_ref[...], upstream, NT)
            grad_scores = (probs * (grad_probs - inner[head : head + 1, at : at + tile])).astype(BF)
            grad_v = dotf(probs.astype(BF), upstream)
            grad_k = dotf(grad_scores, query)
            dq_sum[head * HD : (head + 1) * HD, here] = dotf(
                keys_t[head * HD : (head + 1) * HD], grad_scores
            )
            if head == 0 and at == 0:
                dv_sum[...] = grad_v
                dk_sum[...] = grad_k
            else:
                dv_sum[...] += grad_v
                dk_sum[...] += grad_k
    d_ref[:, :LANES] = jnp.transpose(dq_sum[...]).astype(BF)
    d_ref[:, LANES : 2 * LANES] = dk_sum[...].astype(BF)
    d_ref[:, 2 * LANES :] = dv_sum[...].astype(BF)
    outs = (keep_ref, send_ref)
    width = 3 * LANES

    @pl.when(pair == 0)
    def _():
        load.wait()

    def write_out(group, count):
        cols = pl.ds(pl.multiple_of(group * width, LANES), count)
        return [
            pltpu.make_async_copy(source.at[:, cols], into.at[:, cols], out_sems.at[number, group])
            for number, (source, into) in enumerate(((send_ref, send_hbm), (keep_ref, keep_hbm)))
        ]

    result = dotf(tok_t_ref[...], d_ref[...]).astype(BF)
    store_pieces(result, core, outs, pl.ds(pl.multiple_of(pair * width, LANES), width))
    for copy in write_out(pair, width):
        copy.start()
    here = pl.ds(pl.multiple_of(pair * LANES, LANES), LANES)
    bias_scr[0:1, here] = col_sum(d_ref[:, :LANES].astype(F32))
    bias_scr[1:2, here] = col_sum(d_ref[:, 2 * LANES :].astype(F32))

    @pl.when(pair == pl.num_programs(0) - 1)
    def _():
        model = mid_ref.shape[1]
        sums = jnp.concatenate(
            [
                mid_ref[0:6, :],
                bias_scr[0:2, :],
                mid_ref[8:16, :],
            ],
            axis=0,
        )
        sums = jnp.concatenate([sums, sums, jnp.zeros((LANES - 2 * PARAMS, model), F32)], axis=0)
        quarter = model // 4
        turned = jnp.transpose(sums)
        kept, sent = [], []
        for r0 in range(2):
            lower = turned[r0 * 2 * quarter : r0 * 2 * quarter + quarter]
            upper = turned[r0 * 2 * quarter + quarter : (r0 + 1) * 2 * quarter]
            kept.append(jnp.where(core == 0, lower, upper))
            sent.append(jnp.where(core == 0, upper, lower))
        total = keep_ref.shape[1]
        store_pieces(
            two_parts(jnp.concatenate(kept + sent, axis=0)), core, outs, slice(total - LANES, total)
        )
        groups = (total - LANES) // width
        last = write_out(groups, LANES)
        for copy in last:
            copy.start()
        for group in range(groups):
            for copy in write_out(group, width):
                copy.wait()
        for copy in last:
            copy.wait()


def attend_back(place, q, k, v, grad_mixed, mixed, marks, table, lse, tok_t, sums):
    length = q.shape[0]
    model = tok_t.shape[0]
    pairs = q.shape[1] // LANES
    width = 3 * LANES
    total = pairs * width + LANES
    whole = lambda dims: pl.BlockSpec(dims, lambda i: (0,) * len(dims))
    block = pl.BlockSpec((length, LANES), lambda i: (0, i))
    return pl.pallas_call(
        functools.partial(attend_back_kernel, tile=512),
        grid=(pairs,),
        in_specs=[SM]
        + [block] * 5
        + [whole(marks.shape), pl.BlockSpec((2, LANES, LANES), lambda i: (i, 0, 0))]
        + [whole(lse.shape), pl.BlockSpec(memory_space=pl.ANY), whole(sums.shape)],
        out_specs=[
            pl.BlockSpec(memory_space=pl.ANY),
            pl.BlockSpec(memory_space=pl.ANY),
            pl.BlockSpec((length, width), lambda i: (0, i)),
        ],
        out_shape=[
            shape((model // 2, total), BF),
            shape((model // 2, total), BF),
            shape((length, pairs * width), BF),
        ],
        scratch_shapes=[
            pltpu.VMEM((model // 2, total), BF),
            pltpu.VMEM((model // 2, total), BF),
            pltpu.VMEM((model, length), BF),
            pltpu.VMEM((LANES, length), F32),
            pltpu.VMEM((length, LANES), F32),
            pltpu.VMEM((length, LANES), F32),
            pltpu.VMEM((8, model), F32),
            pltpu.SemaphoreType.DMA,
            pltpu.SemaphoreType.DMA((2, pairs + 1)),
        ],
        compiler_params=params(54),
        cost_estimate=cost(30e9, 10 << 20, 8 << 20, 1.0),
        name="attend_back",
    )(place, q, k, v, grad_mixed, mixed, marks, table, lse, tok_t, sums)


def two_parts(values):
    lane = lax.broadcasted_iota(jnp.int32, (1, LANES), 1)
    rounded = values.astype(BF)
    return jnp.where(lane < PARAMS, rounded, (values - rounded.astype(F32)).astype(BF))


def both_lanes(values):
    lane = lax.broadcasted_iota(jnp.int32, (1, LANES), 1)
    later = pltpu.roll(values, LANES - PARAMS, 1)
    earlier = pltpu.roll(values, PARAMS, 1)
    return values + jnp.where(lane < PARAMS, later, jnp.where(lane < 2 * PARAMS, earlier, 0.0))


def summed(parts, small):
    total = parts[0].astype(F32)
    for part in parts[1:]:
        total = total + part.astype(F32)
    if not small:
        return total.astype(BF)
    at = total.shape[1] - LANES
    return jnp.concatenate([total[:, :at].astype(BF), two_parts(both_lanes(total[:, at:]))], axis=1)


def piece_order(lhs_ref, core):
    quarter = lhs_ref.shape[1] // 4
    cols = []
    for target in (core, 1 - core):
        for half in range(2):
            start = pl.multiple_of(half * 2 * quarter + target * quarter, quarter)
            cols.append(lhs_ref[:, pl.ds(start, quarter)])
    return jnp.transpose(jnp.concatenate(cols, axis=1))


def store_pieces(result, core, outs, cols):
    quarter = result.shape[0] // 4
    piece = quarter // 4
    for which, target in enumerate((core, 1 - core)):
        for r0 in range(2):
            for r2 in range(2):
                for r3 in range(2):
                    at = which * 2 * quarter + r0 * quarter + r2 * 2 * piece + r3 * piece
                    spot = jnp.where(target == 0, r0 * 4 + r2 * 2 + r3, r3 * 4 + r2 * 2 + r0)
                    rows = pl.ds(pl.multiple_of(spot * piece, piece), piece)
                    outs[which][rows, cols] = result[at : at + piece, :]


def weight_grad(lhs_t, rhs_ref, core, outs, first, tile=512):
    for at in range(0, rhs_ref.shape[1], tile):
        result = dotf(lhs_t, rhs_ref[:, at : at + tile]).astype(BF)
        store_pieces(result, core, outs, slice(first + at, first + at + tile))


def normed(hidden):
    center = hidden - jnp.mean(hidden, axis=-1, keepdims=True)
    spread = jnp.mean(center * center, axis=-1, keepdims=True)
    rate = lax.rsqrt(spread + norm_eps)
    return center * rate, rate


def norm_back(grad, unit, rate):
    return rate * (
        grad
        - jnp.mean(grad, axis=-1, keepdims=True)
        - unit * jnp.mean(grad * unit, axis=-1, keepdims=True)
    )


def col_sum(values):
    return jnp.sum(values, axis=0, keepdims=True)


def middle_kernel(
    place,
    rows_ref,
    tok_hbm,
    cot_hbm,
    mixed_hbm,
    own_hbm,
    near_hbm,
    far_hbm,
    out_hbm,
    dh_hbm,
    do_hbm,
    keep_hbm,
    send_hbm,
    sums_ref,
    tok_ref,
    cot_ref,
    mixed_ref,
    out_ref,
    dh_ref,
    do_ref,
    keep_ref,
    send_ref,
    w_scr,
    act_scr,
    du_scr,
    z_scr,
    df_scr,
    da_scr,
    sems,
    out_sems,
    *,
    tile,
):
    length, model = tok_ref.shape
    core = place[1]
    hidden_count = act_scr.shape[1]
    w_up = slice(0, hidden_count)
    w_down = slice(hidden_count, 2 * hidden_count)
    w_out = slice(2 * hidden_count, w_scr.shape[1])
    waits = {}
    number = 0
    for name, sources in (
        ("out", w_out),
        (0, ((mixed_hbm, mixed_ref), (tok_hbm, tok_ref))),
        ("up", w_up),
        ("down", w_down),
        ("cot", ((cot_hbm, cot_ref),)),
        *((at, ((mixed_hbm, mixed_ref), (tok_hbm, tok_ref))) for at in range(tile, length, tile)),
    ):
        if isinstance(sources, slice):
            copies = gathered_rows(
                place, own_hbm, near_hbm, far_hbm, w_scr, sems, sources, number
            )
        else:
            rows = slice(None) if name == "cot" else slice(name, name + tile)
            copies = [
                pltpu.make_async_copy(source.at[rows, :], into.at[rows, :], sems.at[number + n])
                for n, (source, into) in enumerate(sources)
            ]
        number += len(copies)
        for copy in copies:
            copy.start()
        waits[name] = copies

    def ready(name):
        for copy in waits.pop(name, ()):
            copy.wait()

    pending = []

    def write_out(source, into):
        copy = pltpu.make_async_copy(source, into, out_sems.at[len(pending)])
        copy.start()
        pending.append(copy)

    row = lambda number: rows_ref[number : number + 1, :]
    bias_up = jnp.concatenate([row(8), row(9), row(10), row(11)], axis=1)
    sums = [jnp.zeros((1, model), F32)] * 6
    sum_up = jnp.zeros((1, hidden_count), F32)
    for at in range(0, length, tile):
        here = pl.ds(at, tile)
        ready("out")
        ready(at)
        attn_out = dotf(mixed_ref[here, :], w_scr[:, w_out], NT) + row(4)
        unit_one, rate_one = normed(tok_ref[here, :].astype(F32) + attn_out)
        z_one = unit_one * row(0) + row(1)
        z_low = z_one.astype(BF)
        z_scr[here, :] = z_low
        ready("up")
        up = dotf(z_low, w_scr[:, w_up]) + bias_up
        below = 0.5 * (1.0 + lax.erf(up * (0.5**0.5)))
        slope = below + up * (jnp.exp(-0.5 * up * up) * (1.0 / (2.0 * 3.141592653589793) ** 0.5))
        active = (up * below).astype(BF)
        act_scr[here, :] = active
        ready("down")
        ffn_out = dotf(active, w_scr[:, w_down], NT) + row(5)
        unit_two, rate_two = normed(z_one + ffn_out)
        out_ref[here, :] = (unit_two * row(2) + row(3)).astype(BF)
        ready("cot")
        upstream = cot_ref[here, :].astype(F32)
        grad_two = norm_back(upstream * row(2), unit_two, rate_two)
        down_low = grad_two.astype(BF)
        df_scr[here, :] = down_low
        grad_up = (dotf(down_low, w_scr[:, w_down]) * slope).astype(BF)
        du_scr[here, :] = grad_up
        grad_z = grad_two + dotf(grad_up, w_scr[:, w_up], NT)
        grad_one = norm_back(grad_z * row(0), unit_one, rate_one)
        dh_ref[here, :] = grad_one
        attn_low = grad_one.astype(BF)
        da_scr[here, :] = attn_low
        do_ref[here, :] = dotf(attn_low, w_scr[:, w_out]).astype(BF)
        for source, into in ((out_ref, out_hbm), (dh_ref, dh_hbm), (do_ref, do_hbm)):
            write_out(source.at[here, :], into.at[here, :])
        parts = (
            grad_z * unit_one,
            grad_z,
            upstream * unit_two,
            upstream,
            attn_low.astype(F32),
            down_low.astype(F32),
        )
        sums = [a + col_sum(b) for a, b in zip(sums, parts)]
        sum_up = sum_up + col_sum(grad_up.astype(F32))
    for number in range(6):
        sums_ref[number : number + 1, :] = sums[number]
    sums_ref[6:8, :] = jnp.zeros((2, model), F32)
    for number in range(4):
        sums_ref[8 + number : 9 + number, :] = sum_up[:, number * model : (number + 1) * model]
    sums_ref[12:16, :] = jnp.zeros((4, model), F32)
    outs = (keep_ref, send_ref)
    for lhs, rhs, cols in (
        (z_scr, du_scr, w_up),
        (df_scr, act_scr, w_down),
        (da_scr, mixed_ref, w_out),
    ):
        weight_grad(piece_order(lhs, core), rhs, core, outs, cols.start)
        for source, into in ((send_ref, send_hbm), (keep_ref, keep_hbm)):
            write_out(source.at[:, cols], into.at[:, cols])
    for copy in pending:
        copy.wait()


def middle(place, tokens, cotangent, mixed, rows, own, near, far):
    length, model = tokens.shape
    width = own.shape[1]
    hidden_count = (width - mixed.shape[1]) // 2
    tile = 512
    anywhere = pl.BlockSpec(memory_space=pl.ANY)
    outs = [
        shape((length, model), BF),
        shape((length, model), F32),
        shape((length, mixed.shape[1]), BF),
        shape((model // 2, width), BF),
        shape((model // 2, width), BF),
    ]
    vmem = lambda x: pltpu.VMEM(x.shape, x.dtype)
    return pl.pallas_call(
        functools.partial(middle_kernel, tile=tile),
        in_specs=[SM, VM] + [anywhere] * 5 + [VM],
        out_specs=[anywhere] * 5 + [VM],
        out_shape=outs + [shape((16, model), F32)],
        scratch_shapes=[vmem(x) for x in (tokens, cotangent, mixed, *outs)]
        + [
            pltpu.VMEM((model, width), BF),
            pltpu.VMEM((length, hidden_count), BF),
            pltpu.VMEM((length, hidden_count), BF),
            pltpu.VMEM((length, model), BF),
            pltpu.VMEM((length, model), BF),
            pltpu.VMEM((length, model), BF),
            pltpu.SemaphoreType.DMA((10 + 2 * (length // tile),)),
            pltpu.SemaphoreType.DMA((3 * (length // tile) + 6,)),
        ],
        compiler_params=params(58),
        cost_estimate=cost(16e9, 16 << 20, 4 << 20, 1.0),
        name="middle",
    )(place, rows, tokens, cotangent, mixed, own, near, far)


def input_grad_kernel(
    place, dh_ref, d_ref, own_ref, near_ref, side_ref, far_near_ref, far_side_ref, out_ref, w_scr, sems
):
    eighth_refs = (own_ref, near_ref, side_ref, far_near_ref, far_side_ref)
    width = d_ref.shape[1]

    @pl.when(pl.program_id(0) == 0)
    def _():
        copies = gathered_eighths(place, *eighth_refs, w_scr, sems)
        for copy in copies:
            copy.start()
        for copy in copies:
            copy.wait()

    out_ref[...] = (dh_ref[...] + dotf(d_ref[...], w_scr[:, :width], NT)).astype(BF)


def input_gradient(place, dh, d, rows_a):
    length, model = dh.shape
    tile = 256
    anywhere = pl.BlockSpec(memory_space=pl.ANY)
    rows = lambda width: pl.BlockSpec((tile, width), lambda i: (i, 0))
    return pl.pallas_call(
        input_grad_kernel,
        grid=(length // tile,),
        in_specs=[SM, rows(model), rows(d.shape[1])] + [anywhere] * 5,
        out_specs=rows(model),
        out_shape=shape((length, model), BF),
        scratch_shapes=[pltpu.VMEM((model, rows_a[0].shape[1]), BF), pltpu.SemaphoreType.DMA((5,))],
        compiler_params=params(16),
        cost_estimate=cost(2 * length * model * d.shape[1], 8 << 20),
        name="input_gradient",
    )(place, dh, d, *rows_a)


def add_low(a, b):
    return (a.astype(F32) + b.astype(F32)).astype(BF)


def add_parts_kernel(place, *refs, small):
    refs[-1][...] = summed([ref[...] for ref in refs[:-1]], small)


def add_parts(place, parts, give, small):
    rows = min(part.shape[0] for part in parts)
    rows = rows // 2 if give else rows
    width = parts[0].shape[1]

    def pick(part):
        if part.shape[0] == rows:
            return pl.BlockSpec((rows, width), lambda i, place: (0, 0))
        return pl.BlockSpec((rows, width), lambda i, place: (1 - place[6] if give else place[6], 0))

    return pl.pallas_call(
        functools.partial(add_parts_kernel, small=small),
        grid_spec=pltpu.PrefetchScalarGridSpec(
            num_scalar_prefetch=1,
            grid=(1,),
            in_specs=[pick(part) for part in parts],
            out_specs=pl.BlockSpec((rows, width), lambda i, place: (0, 0)),
        ),
        out_shape=shape((rows, width), BF),
        compiler_params=params(8),
        cost_estimate=cost(len(parts) * rows * width, 2 * len(parts) * rows * width),
        name="add_parts",
    )(place, *parts)


def flip(count, bit):
    return [(i, i ^ (1 << bit)) for i in range(count)]


def mixed_flip(count, even, odd):
    return [(i, i ^ (1 << (odd if (i >> 1) & 1 else even))) for i in range(2 * count)]


STEPS = ((0, 2), (2, 3), (3, 0))


def mixed_mask(count, mask):
    pairs = []
    for i in range(2 * count):
        partner = i
        for bit, step in zip((2, 1), STEPS):
            if mask & bit:
                partner ^= 1 << step[(i >> 1) & 1]
        pairs.append((i, partner))
    return pairs


def split_kernel(place, keep_ref, got_ref, *outs, small):
    piece = outs[0].shape[0]
    mine = place[3] * 2 + place[4]
    for mask, out in enumerate(outs):
        rows = pl.ds(pl.multiple_of((mine ^ mask) * piece, piece), piece)
        out[...] = summed([keep_ref[rows, :], got_ref[rows, :]], small)


def swap_two(value, count, mask):
    return lax.ppermute(value, ("dp", "shard"), mixed_mask(count, mask))


def split(place, keep, got, small):
    rows, width = keep.shape
    steps = 1 if small else 4
    step = width // steps
    whole = pl.BlockSpec((rows, step), lambda i: (0, i))
    part = pl.BlockSpec((rows // 4, step), lambda i: (0, i))
    return pl.pallas_call(
        functools.partial(split_kernel, small=small),
        grid=(steps,),
        in_specs=[SM, whole, whole],
        out_specs=[part] * 4,
        out_shape=[shape((rows // 4, width), BF)] * 4,
        compiler_params=params(16),
        cost_estimate=cost(rows * width, 6 * rows * width),
        name="split",
    )(place, keep, got)


def swap_core(value, count):
    return lax.ppermute(value, "dp", flip(count, 0))


def swap_mixed(value, count, step):
    return lax.ppermute(value, ("dp", "shard"), mixed_flip(count, *step))


def swap_bit(value, count, bit):
    return lax.ppermute(value, "dp", flip(count, bit))


def after(value, *others):
    return lax.optimization_barrier((value,) + others)[0]


def adam_values(scalars, weight_ref, mean_ref, square_ref, grad, decay, outs):
    weight = weight_ref[...]
    mean_out = beta_one * mean_ref[...] + (1.0 - beta_one) * grad
    square_out = beta_two * square_ref[...] + (1.0 - beta_two) * grad * grad
    mean_hat = mean_out * scalars[2]
    square_hat = square_out * scalars[3]
    weight_out = weight - scalars[0] * (
        mean_hat / (jnp.sqrt(square_hat) + adam_eps) + decay * weight
    )
    outs[0][...] = weight_out
    outs[1][...] = mean_out
    outs[2][...] = square_out
    outs[3][...] = weight_out.astype(BF)


def piece_block(place, own, flips):
    bit2, bit3 = (place[4], place[5]) if own else (place[5], place[4])
    core = place[1] if own else 1 - place[1]
    return core * 4 + (bit2 ^ (flips >> 1)) * 2 + (bit3 ^ (flips & 1))


def chosen(index, values):
    result = values[-1]
    for number in range(len(values) - 2, -1, -1):
        result = jnp.where(index == number, values[number], result)
    return result


def adam_ffn_kernel(place, scalars, *refs, count):
    step = pl.program_id(0)
    stack, _, width = refs[count].shape
    for number in range(count):

        @pl.when(step == number)
        def _():
            grad = jnp.stack(
                [refs[number][:, w * width : (w + 1) * width].astype(F32) for w in range(stack)]
            )
            adam_values(scalars, *refs[count : count + 3], grad, scalars[1], refs[-4:])


def adam_ffn(place, scalars, pieces, state, before):
    count = len(pieces)
    stack, rows, width = state[0].shape
    step = rows // 8
    grads = [piece[0] for piece in pieces]
    take = pl.BlockSpec((step, stack * width), lambda p, place, sc: (0, 0))
    block = pl.BlockSpec(
        (stack, step, width),
        lambda p, place, sc: (0, chosen(p, [piece_block(place, *x[1:]) for x in pieces]), 0),
    )
    before = list(before or ())
    return pl.pallas_call(
        functools.partial(adam_ffn_kernel, count=count),
        grid_spec=pltpu.PrefetchScalarGridSpec(
            num_scalar_prefetch=2,
            grid=(count,),
            in_specs=[take] * count + [block] * 3 + [pl.BlockSpec(memory_space=pl.ANY)] * len(before),
            out_specs=[block] * 4,
        ),
        out_shape=[shape(state[0].shape, F32)] * 3 + [shape(state[0].shape, BF)],
        input_output_aliases={5 + count + n: n for n in range(len(before))},
        compiler_params=params(36),
        cost_estimate=cost(20 * count * step * width, 28 * count * step * width),
        name="adam_ffn",
    )(place, scalars, *grads, *state, *before)


def adam_attn_kernel(place, scalars, *refs, count, orders, small):
    grads, outer, state = refs[:count], refs[count : 2 * count], refs[2 * count : 2 * count + 3]
    rest = refs[2 * count + 3 :]
    step = pl.program_id(0)
    if small:
        little, (sw, sm, ss), rest = rest[:small], rest[small : small + 3], rest[small + 3 + 4 :]
        outs, small_outs, scr = rest[:4], rest[4:8], rest[8]

        @pl.when(step == 0)
        def _():
            for ref, order in zip(little, orders):
                rows = ref.shape[0]
                where = pl.ds(pl.multiple_of(piece_block(place, *order) * rows, rows), rows)
                scr[where, :] = ref[...].astype(F32)
            turned = jnp.transpose(both_lanes(scr[...]))[: sw.shape[0], :]
            adam_values(scalars, sw, sm, ss, turned, 0.0 * scalars[1], small_outs)
    else:
        outs = rest[-4:]
    for number in range(count):

        @pl.when(step == number)
        def _():
            grad = grads[number][...].astype(F32)
            pairs = grad.shape[1] // (3 * LANES)
            parts = [
                grad[:, p * 3 * LANES + kind * LANES : p * 3 * LANES + (kind + 1) * LANES]
                for kind in range(3)
                for p in range(pairs)
            ]
            parts.append(outer[number][...].astype(F32))
            adam_values(scalars, *state, jnp.concatenate(parts, axis=1), scalars[1], outs)


def adam_attn(place, scalars, pieces, pieces_b, state, before, every=None, small=None):
    count = len(pieces)
    rows, width = state[0].shape
    step = rows // 8
    out_width = width // 4
    grads = [piece[0] for piece in pieces]
    outer = [piece[0] for piece in pieces_b]
    last = outer[0].shape[1] // out_width - 1
    block = pl.BlockSpec(
        (step, width),
        lambda p, place, sc: (chosen(p, [piece_block(place, *x[1:]) for x in pieces]), 0),
    )
    anywhere = pl.BlockSpec(memory_space=pl.ANY)
    in_specs = [pl.BlockSpec(grads[0].shape, lambda p, place, sc: (0, 0))] * count
    in_specs += [pl.BlockSpec((step, out_width), lambda p, place, sc: (0, last))] * count
    in_specs += [block] * 3
    operands = [place, scalars, *grads, *outer, *state]
    out_specs = [block] * 4
    out_shape = [shape(state[0].shape, F32)] * 3 + [shape(state[0].shape, BF)]
    scratch = []
    if small:
        whole = pl.BlockSpec(small[0].shape, lambda p, place, sc: (0, 0))
        at = grads[0].shape[1] // LANES - 1
        in_specs += [pl.BlockSpec((step, LANES), lambda p, place, sc: (0, at))] * len(every)
        in_specs += [whole] * 3
        operands += [piece[0] for piece in every] + list(small)
        out_specs += [whole] * 4
        out_shape += [shape(small[0].shape, F32)] * 3 + [shape(small[0].shape, BF)]
        scratch = [pltpu.VMEM((rows, LANES), F32)]
    before = list(before or ())
    aliases = {len(operands) + n: n for n in range(len(before))}
    return pl.pallas_call(
        functools.partial(
            adam_attn_kernel,
            count=count,
            orders=[piece[1:] for piece in every or ()],
            small=len(every or ()),
        ),
        grid_spec=pltpu.PrefetchScalarGridSpec(
            num_scalar_prefetch=2,
            grid=(count,),
            in_specs=in_specs + [anywhere] * len(before),
            out_specs=out_specs,
            scratch_shapes=scratch,
        ),
        out_shape=out_shape,
        input_output_aliases=aliases,
        compiler_params=params(36),
        cost_estimate=cost(20 * count * step * width, 28 * count * step * width),
        name="adam_attn",
    )(*operands, *before)


def from_neighbour(value):
    return lax.ppermute(value, "shard", [(0, 1), (1, 0)])


def local(
    count,
    tokens,
    cotangent,
    segments,
    random_blocks,
    step_count,
    adam_rates,
    attn_master,
    attn_mean,
    attn_square,
    ffn_master,
    ffn_mean,
    ffn_square,
    small_master,
    small_mean,
    small_square,
):
    replica = lax.axis_index("dp")
    shard = lax.axis_index("shard")
    core, low, high = replica & 1, (replica >> 1) & 1, (replica >> 2) & 1
    even = core == 0
    place = jnp.stack(
        [
            shard,
            core,
            low,
            jnp.where(even, shard, low),
            jnp.where(even, low, high),
            jnp.where(even, high, low),
            jnp.where(even, high, shard),
        ]
    ).astype(jnp.int32)
    pairs = attn_master.shape[1] // 4 // LANES
    near_a = from_neighbour(pack_eighth_a(attn_master, small_master))
    quarter_b = pack_quarter_b(place, attn_master, ffn_master)
    near_a = after(near_a, quarter_b)
    near_b = from_neighbour(after(quarter_b, near_a))
    side_a = swap_bit(near_a, count, 1)
    own_a, own_b = pack_own(attn_master, ffn_master, small_master)
    side_a = after(side_a, own_a)
    rows_a = (own_a, near_a, side_a, swap_core(near_a, count), swap_core(side_a, count))
    q, k, v, mixed, lse, rows, tok_t, marks, table = attend(
        place, tokens, rows_a, segments, random_blocks
    )
    far_b = swap_core(after(near_b, lse), count)
    layer_out, dh, grad_mixed, keep_b, send_b, sums = middle(
        place, tokens, cotangent, mixed, rows, own_b, near_b, far_b
    )
    parts_b = list(split(place, keep_b, swap_core(send_b, count), False))
    parts_b = parts_b[:1] + [swap_two(parts_b[mask], count, mask) for mask in (1, 2, 3)]
    keep_a, send_a, d = attend_back(
        place, q, k, v, after(grad_mixed, parts_b[0]), mixed, marks, table, lse, tok_t, sums
    )
    got_a = swap_core(send_a, count)
    parts_b = parts_b[:1] + [after(part, d) for part in parts_b[1:]]
    got_b = swap_mixed(add_parts(place, parts_b, True, False), count, STEPS[2])

    step_value = step_count[0].astype(F32)
    scalars = jnp.stack(
        [
            adam_rates[0],
            adam_rates[1],
            1.0 / (1.0 - beta_one**step_value),
            1.0 / (1.0 - beta_two**step_value),
        ]
    )
    ffn_state = (ffn_master, ffn_mean, ffn_square)
    attn_state = (attn_master, attn_mean, attn_square)
    small_state = (small_master, small_mean, small_square)
    bits = [bit for bit in range(3, count.bit_length() - 1)]

    parts_a = list(split(place, keep_a, got_a, True))
    parts_a = parts_a[:1] + [swap_two(parts_a[mask], count, mask) for mask in (1, 2, 3)]
    total_b = add_parts(place, parts_b + [after(got_b, parts_a[0])], False, False)
    got_b = swap_bit(total_b, count, bits[0])
    input_grad = input_gradient(place, after(dh, total_b), d, rows_a)
    parts_a = parts_a[:1] + [after(part, input_grad) for part in parts_a[1:]]
    got_a = swap_mixed(add_parts(place, parts_a, True, True), count, STEPS[2])
    total_a = add_parts(place, parts_a + [got_a], False, True)
    got_a = swap_bit(total_a, count, bits[0])
    total_b = add_low(total_b, after(got_b, total_a))
    for bit in bits[1:]:
        total_b = add_low(total_b, swap_bit(total_b, count, bit))
    first, second = (3, 2), (2, 3)

    def wave(values, flips):
        return [(v, True, f) for v, f in zip(values, flips)] + [
            (swap_core(v, count), False, f) for v, f in zip(values, flips)
        ]

    b_one = wave([total_b], [0])
    got_b = [swap_mixed(total_b, count, first), swap_mixed(total_b, count, second)]
    ffn_new = adam_ffn(place, scalars, b_one, ffn_state, None)
    total_a = add_parts(place, [total_a, after(got_a, ffn_new[0])], False, True)
    for bit in bits[1:]:
        total_a = add_parts(place, [total_a, swap_bit(total_a, count, bit)], False, True)
    a_one = wave([total_a], [0])
    got_a = [swap_mixed(total_a, count, first), swap_mixed(total_a, count, second)]
    got_b = [after(piece, ffn_new[0], total_a) for piece in got_b]
    b_two = wave(got_b, [1, 2])
    got_b = swap_mixed(got_b[0], count, second)
    attn_new = adam_attn(place, scalars, a_one, b_one, attn_state, None)
    ffn_new = adam_ffn(place, scalars, b_two, ffn_state, ffn_new)
    got_a = [after(piece, attn_new[0]) for piece in got_a]
    a_two = wave(got_a, [1, 2])
    got_a = swap_mixed(got_a[0], count, second)
    b_three = wave([after(got_b, ffn_new[0])], [3])
    attn_new = adam_attn(place, scalars, a_two, b_two, attn_state, attn_new)
    a_three = wave([after(got_a, attn_new[0])], [3])
    ffn_new = adam_ffn(place, scalars, b_three, ffn_state, ffn_new)
    attn_new = adam_attn(
        place,
        scalars,
        a_three,
        b_three,
        attn_state,
        attn_new,
        a_one + a_two + a_three,
        small_state,
    )
    return (layer_out, input_grad) + tuple(attn_new[:4]) + tuple(ffn_new) + tuple(attn_new[4:])


def solution(mesh):
    tokens_in = P(("dp", "shard"), None)
    rows_in = P("shard", None)
    stack_in = P(None, "shard", None)
    cols_in = P(None, "shard")
    placed = (
        (tokens_in,) * 3
        + (P(("dp", "shard"), None, None, None), P(), P())
        + (rows_in,) * 3
        + (stack_in,) * 3
        + (cols_in,) * 3
    )
    return jax.shard_map(
        functools.partial(local, mesh.shape["dp"]),
        mesh=mesh,
        in_specs=placed,
        out_specs=(tokens_in,) * 2 + (rows_in,) * 4 + (stack_in,) * 4 + (cols_in,) * 4,
        check_vma=False,
    )
```
